256 devices in a mesh: ctx: 8 (over y_lo, x), tp: 32 (over y_hi, z, core).
Axes of the slice: x: 4, y: 4 (y_hi: 2, y_lo: 2; y = y_hi * 2 + y_lo), z: 8, core: 2. Of those that a mesh axis runs over, the one named last changes fastest.
Arguments:
- normed_rows: bfloat16 [6144, 4096], P(('ctx', 'tp')), may hold values from -6 to 6
- out_grad: bfloat16 [6144, 4096], P(('ctx', 'tp')), may hold values from -6 to 6
- inner_weight: bfloat16 [2, 4096, 8192], P(None, None, 'tp'), may hold values from -0.09375 to 0.09375
- state_weight: bfloat16 [4096, 256], replicated, may hold values from -0.09375 to 0.09375
- step_weight: bfloat16 [4096, 64], P(None, 'tp'), may hold values from -0.09375 to 0.09375
- conv_inner: float32 [4, 8192], P(None, 'tp'), may hold values from -3 to 3
- conv_state: float32 [4, 256], replicated, may hold values from -3 to 3
- step_bias: float32 [64], P('tp'), may hold values from -4 to -1
- decay_log: float32 [64], P('tp')
- norm_gain: float32 [8192], P('tp'), may hold values from 0.1 to 1.9
- out_weight: bfloat16 [8192, 4096], P('tp'), may hold values from -0.0625 to 0.0625
Outputs:
- input_grad: bfloat16 [6144, 4096], P(('ctx', 'tp'))
The draws below stay inside these ranges and needn't reach their ends.
All inputs are finite; a program needn't handle non-finite values.
Results may differ from the reference program's by a relative error of at most 0.0095.
Values may be sent and summed in bfloat16 or wider, within the bound.
A program may use at most 128 MiB of HBM per device.

```python
import math
import jax
import jax.numpy as jnp
from jax import lax

D = 4096
HEAD_DIM = 128
STATE = 128
CONV = 4
HEADS = 64
CHANNELS = 8192
SEQ = 6144


def draw_decay_log(key, part):
    pick_key, slow_key, fast_key = jax.random.split(key, 3)
    share = 0.5
    slow = jax.random.uniform(pick_key, (HEADS,), jnp.float32) < share
    slow_rate = jnp.exp(jax.random.uniform(slow_key, (HEADS,), jnp.float32, jnp.log(0.2), jnp.log(2.0))) / SEQ
    fast_rate = jnp.exp(jax.random.uniform(fast_key, (HEADS,), jnp.float32, jnp.log(0.05), -0.5))
    return jnp.log(jnp.where(slow, slow_rate, fast_rate)).astype(jnp.float32)


def shard_levels(stream_key, dims, cuts, low, largest):
    gain = 1.0
    for axis_at, parts in cuts:
        steps = jax.random.uniform(jax.random.fold_in(jax.random.fold_in(stream_key, 6), axis_at), (parts,), jnp.float32, low / len(cuts), largest / len(cuts))
        gain = gain * jnp.repeat(jnp.exp(steps), dims[axis_at] // parts).reshape((-1,) + (1,) * (len(dims) - 1 - axis_at))
    return gain


def centred(key, dims, scale, reach, pieces=(), held_as=jnp.bfloat16):
    array = jax.random.normal(key, dims, jnp.float32) * scale
    if len(pieces) > 0:
        array = shard_levels(key, dims, pieces, -0.22, 0.18) * array
    return jnp.clip(array, min=-reach, max=reach).astype(held_as)


def setup_inputs(seed: int = 0) -> dict:
    key_of = jax.random.split(jax.random.key(seed), 12)
    normed_rows = centred(key_of[0], (SEQ, D), 1.0, 6.0, ((0, 256),))
    out_grad = centred(key_of[1], (SEQ, D), 1.0, 6.0, ((0, 256),))
    inner_weight = centred(key_of[2], (2, D, CHANNELS), D ** -0.5, 0.09375, ((2, 32),))
    state_weight = centred(key_of[3], (D, 2 * STATE), D ** -0.5, 0.09375)
    step_weight = centred(key_of[4], (D, HEADS), D ** -0.5, 0.09375, ((1, 32),))
    conv_inner = centred(key_of[5], (CONV, CHANNELS), CONV ** -0.5, 3.0, ((1, 32),), jnp.float32)
    conv_state = centred(key_of[6], (CONV, 2 * STATE), CONV ** -0.5, 3.0, (), jnp.float32)
    step_bias = jnp.clip(-4.0 + 3.0 * jax.random.uniform(key_of[7], (HEADS,), jnp.float32) ** shard_levels(key_of[7], (HEADS,), ((0, 32),), -0.2, 0.2), -4.0, -1.0)
    decay_log = draw_decay_log(jax.random.fold_in(key_of[11], 71), 0)
    norm_gain = jnp.clip(1.0 + 0.18 * jax.random.normal(key_of[9], (CHANNELS,), jnp.float32), 0.1, 1.9)
    out_weight = centred(key_of[10], (CHANNELS, D), CHANNELS ** -0.5, 0.0625, ((0, 32),))
    return {"normed_rows": normed_rows, "out_grad": out_grad, "inner_weight": inner_weight, "state_weight": state_weight, "step_weight": step_weight, "conv_inner": conv_inner, "conv_state": conv_state, "step_bias": step_bias, "decay_log": decay_log, "norm_gain": norm_gain, "out_weight": out_weight}


EPSILON = 1e-05
EXACT = lax.Precision.HIGHEST

def decay_table(log_decay):
    running = jnp.cumsum(log_decay, axis=0)
    length = log_decay.shape[0]
    causal = (lax.broadcasted_iota(jnp.int32, (length, length), 0) >= lax.broadcasted_iota(jnp.int32, (length, length), 1)).astype(jnp.float32)
    spread_log = running.T[:, :, None] - running.T[:, None, :]
    return (running, jnp.exp(jnp.minimum(spread_log, 0.0)) * causal)

def within_shard(inner_act, step_size, log_decay, b_rows, c_rows, entering):
    running, decays = decay_table(log_decay)
    scores = jnp.dot(c_rows, b_rows.T, precision=EXACT)
    weights = decays * scores[None] * step_size.T[:, None, :]
    local_part = jnp.einsum('hts,shp->thp', weights, inner_act, precision=EXACT)
    carried = jnp.einsum('tn,hpn->thp', c_rows, entering, precision=EXACT) * jnp.exp(running)[:, :, None]
    return local_part + carried

def leaving_state(inner_act, step_size, log_decay, b_rows, entering):
    running = jnp.cumsum(log_decay, axis=0)
    weights = jnp.exp(running[-1][None, :] - running) * step_size
    own_state = jnp.einsum('th,thp,tn->hpn', weights, inner_act, b_rows, precision=EXACT)
    return jnp.exp(running[-1])[:, None, None] * entering + own_state

def scan_blocks(inner_act, step_size, log_decay, b_rows, c_rows):
    length = inner_act.shape[0]
    block_len = math.gcd(length, 128)
    block_count = length // block_len
    head_count = inner_act.shape[1]

    def advance(entering, blocks):
        act_part, size_part, decay_part, brow_part, crow_part = blocks
        output = within_shard(act_part, size_part, decay_part, brow_part, crow_part, entering)
        return (leaving_state(act_part, size_part, decay_part, brow_part, entering), output)
    initial = jnp.zeros((head_count, inner_act.shape[2], b_rows.shape[1]), jnp.float32)
    blocks = (inner_act.reshape(block_count, block_len, head_count, -1), step_size.reshape(block_count, block_len, head_count), log_decay.reshape(block_count, block_len, head_count), b_rows.reshape(block_count, block_len, -1), c_rows.reshape(block_count, block_len, -1))
    _, outputs = lax.scan(advance, initial, blocks)
    return outputs.reshape(length, head_count, -1)

def mixer_core(gate_value, conv_in, step_raw, conv_inner, conv_state, step_bias, decay_log, norm_gain):
    length = conv_in.shape[0]
    kernel = jnp.concatenate([conv_inner, conv_state], axis=1)
    padded = jnp.concatenate([jnp.zeros((CONV - 1, conv_in.shape[1]), jnp.float32), conv_in], axis=0)
    blended = jnp.zeros_like(conv_in)
    for offset in range(CONV):
        blended = blended + kernel[offset] * padded[offset:offset + length]
    active = jax.nn.silu(blended)
    inner_act = active[:, :CHANNELS].reshape(length, HEADS, HEAD_DIM)
    b_rows = active[:, CHANNELS:CHANNELS + STATE]
    c_rows = active[:, CHANNELS + STATE:]
    step_size = jax.nn.softplus(step_raw + step_bias)
    log_decay = -step_size * jnp.exp(decay_log)
    scan_out = scan_blocks(inner_act, step_size, log_decay, b_rows, c_rows).reshape(length, CHANNELS)
    gated_out = scan_out * jax.nn.silu(gate_value)
    mean_square = lax.optimization_barrier(jnp.mean(gated_out * gated_out, axis=1, keepdims=True))
    return gated_out * lax.rsqrt(mean_square + EPSILON) * norm_gain

def reference(normed_rows, out_grad, inner_weight, state_weight, step_weight, conv_inner, conv_state, step_bias, decay_log, norm_gain, out_weight):
    gate_raw = jnp.dot(normed_rows, inner_weight[0], preferred_element_type=jnp.float32).astype(jnp.bfloat16)
    inner_raw = jnp.dot(normed_rows, inner_weight[1], preferred_element_type=jnp.float32).astype(jnp.bfloat16)
    state_raw = jnp.dot(normed_rows, state_weight, preferred_element_type=jnp.float32).astype(jnp.bfloat16)
    step_raw = jnp.dot(normed_rows, step_weight, preferred_element_type=jnp.float32).astype(jnp.bfloat16)
    conv_in = jnp.concatenate([inner_raw, state_raw], axis=1).astype(jnp.float32)
    out_local = jnp.dot(out_grad, out_weight.T, preferred_element_type=jnp.float32)

    def forward(gate_value, conv_value, step_value):
        return mixer_core(gate_value, conv_value, step_value, conv_inner, conv_state, step_bias, decay_log, norm_gain)
    _, pull_back = jax.vjp(forward, gate_raw.astype(jnp.float32), conv_in, step_raw.astype(jnp.float32))
    d_gate, d_conv, d_step = pull_back(out_local)
    input_term = jnp.dot(d_gate.astype(jnp.bfloat16), inner_weight[0].T, preferred_element_type=jnp.float32)
    input_term = input_term + jnp.dot(d_conv[:, :CHANNELS].astype(jnp.bfloat16), inner_weight[1].T, preferred_element_type=jnp.float32)
    input_term = input_term + jnp.dot(d_step.astype(jnp.bfloat16), step_weight.T, preferred_element_type=jnp.float32)
    input_term = input_term + jnp.dot(d_conv[:, CHANNELS:], state_weight.astype(jnp.float32).T, precision=EXACT, preferred_element_type=jnp.float32)
    return input_term.astype(jnp.bfloat16)
```

```python
import functools

import jax
import jax.numpy as jnp
from jax import lax
from jax.experimental import pallas as pl
from jax.experimental.pallas import tpu as pltpu
from jax.sharding import PartitionSpec as P

HEAD_DIM = 128
STATE = 128
CONV = 4
EPSILON = 1e-05
EXACT = lax.Precision.HIGHEST
MESH = pl.DeviceIdType.MESH
F32 = jnp.float32
BF16 = jnp.bfloat16
VMEM_LIMIT = 60 * 1024 * 1024

Z = 8
RING = [(0, 0), (0, 1), (1, 0), (1, 1), (2, 0), (2, 1)]


def place():
    tp = lax.axis_index("tp")
    core = lax.rem(tp, 2)
    z = lax.rem(tp // 2, Z)
    yh = tp // (2 * Z)
    return yh, z, core


def tp_id(yh, z, core):
    return (yh * Z + z) * 2 + core


def greet(tp_partners, ctx_partners=()):
    barrier = pltpu.get_barrier_semaphore()
    for partner in tp_partners:
        pl.semaphore_signal(barrier, inc=1, device_id={"tp": partner}, device_id_type=MESH)
    for partner in ctx_partners:
        pl.semaphore_signal(barrier, inc=1, device_id={"ctx": partner}, device_id_type=MESH)
    pl.semaphore_wait(barrier, len(tp_partners) + len(ctx_partners))


class Gather:
    def __init__(self, own_ref, buf, swap, send_sem, recv_sem):
        self.own_ref, self.buf, self.swap = own_ref, buf, swap
        self.send_sem, self.recv_sem = send_sem, recv_sem
        self.yh, self.z, self.core = place()
        self.pair = 2 * own_ref.shape[0]
        self.half = own_ref.shape[1] // 2
        self.sibling = tp_id(self.yh, self.z, 1 - self.core)
        self.started = []

    def columns(self, core):
        return pl.ds(pl.multiple_of(core * self.half, self.half), self.half)

    def block(self, h, dz, core=None):
        yh = self.yh if h == 0 else 1 - self.yh
        chip = yh * Z + lax.rem(self.z + (dz + Z), Z)
        rows = pl.ds(pl.multiple_of(chip * self.pair, 16), self.pair)
        return self.buf.at[rows, self.columns(self.core if core is None else core)]

    def copy(self, slot, src, dst, partner):
        return pltpu.make_async_remote_copy(
            src_ref=src,
            dst_ref=dst,
            send_sem=self.send_sem.at[slot],
            recv_sem=self.recv_sem.at[slot],
            device_id={"tp": partner},
            device_id_type=MESH,
        )

    def send(self, slot, src, dst, partner):
        copy = self.copy(slot, src, dst, partner)
        copy.start()
        self.started.append(copy)

    def slot(self, way, s, h):
        return (1 if way > 0 else 8) + (2 * s + h if s < 3 else 6)

    def sibling_slot(self, h, dz):
        return 15 + (dz + 3) * 2 + h if dz > -4 else 15 + (14 if h == 0 else 15)

    def to_sibling(self, h, dz):
        here = self.block(h, dz)
        self.send(self.sibling_slot(h, dz), here, here, self.sibling)

    def along(self, way, s, h):
        here = self.block(h, -way * s)
        partner = tp_id(self.yh, lax.rem(self.z + way + Z, Z), self.core)
        self.send(self.slot(way, s, h), here, here, partner)

    def first_swap(self):
        self.send(31, self.own_ref.at[:, self.columns(1 - self.core)], self.swap, self.sibling)

    def begin(self):
        self.got(31, self.swap)
        mine = self.own_ref[:, self.columns(self.core)].astype(F32)
        other = self.swap[...].astype(F32)
        first = self.core == 0
        both = jnp.concatenate([jnp.where(first, mine, other), jnp.where(first, other, mine)], axis=0)
        here = self.block(0, 0)
        here[...] = both.astype(BF16)
        self.send(0, here, here, tp_id(1 - self.yh, self.z, self.core))
        self.along(1, 0, 0)
        self.along(-1, 0, 0)
        self.to_sibling(0, 0)

    def got(self, slot, block):
        self.copy(slot, block, block, self.sibling).wait_recv()

    def across(self):
        self.got(0, self.block(1, 0))
        self.along(1, 0, 1)
        self.along(-1, 0, 1)
        self.to_sibling(1, 0)

    def ring(self, s, h):
        for way in (1, -1):
            dz = -way * (s + 1)
            self.got(self.slot(way, s, h), self.block(h, dz))
            if s < 2 or (way > 0) == (h == 0):
                self.along(way, s + 1, h)
            self.to_sibling(h, dz)

    def last(self):
        for way, h in ((1, 0), (-1, 1)):
            self.got(self.slot(way, 3, h), self.block(h, -4))
            self.to_sibling(h, -4)

    def finish(self):
        for h in (0, 1):
            for dz in range(-4, 4):
                self.got(self.sibling_slot(h, dz), self.block(h, dz, 1 - self.core))

    def drain(self):
        for copy in self.started:
            copy.wait_send()

    def steps(self):
        return (
            [self.begin, self.across]
            + [functools.partial(self.ring, s, h) for s, h in RING]
            + [self.last]
        )


def gather_kernel(
    rows_ref,
    grads_ref,
    inner_hbm,
    state_hbm,
    step_ref,
    out_hbm,
    gate_ref,
    conv_ref,
    stepraw_ref,
    local_ref,
    rows_all,
    grads_all,
    swaps,
    inner_w,
    state_w,
    out_w,
    send_r,
    recv_r,
    send_g,
    recv_g,
    weight_sem,
):
    loads = [
        pltpu.make_async_copy(inner_hbm, inner_w, weight_sem.at[0]),
        pltpu.make_async_copy(state_hbm, state_w, weight_sem.at[1]),
        pltpu.make_async_copy(out_hbm, out_w, weight_sem.at[2]),
    ]
    for load in loads:
        load.start()
    yh, z, core = place()
    greet(
        [
            tp_id(1 - yh, z, core),
            tp_id(yh, lax.rem(z + 1, Z), core),
            tp_id(yh, lax.rem(z + Z - 1, Z), core),
            tp_id(yh, z, 1 - core),
        ]
    )
    first = Gather(rows_ref, rows_all, swaps.at[0], send_r, recv_r)
    second = Gather(grads_ref, grads_all, swaps.at[1], send_g, recv_g)
    first.first_swap()
    second.first_swap()
    for step in first.steps()[:-1]:
        step()
    second.begin()
    first.last()
    second.across()
    for load in loads:
        load.wait()
    first.finish()
    total = rows_all.shape[0]
    tile = 128

    def project(dst, column, weight):
        def turn(i, carry):
            at = pl.ds(pl.multiple_of(i * tile, tile), tile)
            value = jnp.dot(rows_all[at, :], weight[...], preferred_element_type=F32)
            dst[at, pl.ds(column, value.shape[1])] = value.astype(BF16).astype(dst.dtype)
            return carry

        lax.fori_loop(0, total // tile, turn, 0)

    width = inner_w.shape[2]
    work = [
        lambda: project(conv_ref, 0, inner_w.at[1]),
        lambda: project(conv_ref, width, state_w),
        lambda: project(stepraw_ref, 0, step_ref),
        lambda: project(gate_ref, 0, inner_w.at[0]),
    ]
    pending = [functools.partial(second.ring, s, h) for s, h in RING] + [second.last]
    for at, step in enumerate(pending):
        step()
        if at < len(work):
            work[at]()
    second.finish()

    def turn(i, carry):
        at = pl.ds(pl.multiple_of(i * tile, tile), tile)
        local_ref[at, :] = lax.dot_general(
            grads_all[at, :], out_w[...], (((1,), (1,)), ((), ())), preferred_element_type=F32
        )
        return carry

    lax.fori_loop(0, total // tile, turn, 0)
    first.drain()
    second.drain()


def gathered(rows, grads, inner_weight, state_weight, step_weight, out_weight):
    count, depth = rows.shape
    total = count * 4 * Z
    width, state_width = inner_weight.shape[2], state_weight.shape[1]
    vmem = pl.BlockSpec(memory_space=pltpu.VMEM)
    anywhere = pl.BlockSpec(memory_space=pl.ANY)
    return pl.pallas_call(
        gather_kernel,
        out_shape=(
            jax.ShapeDtypeStruct((total, width), BF16),
            jax.ShapeDtypeStruct((total, width + state_width), BF16),
            jax.ShapeDtypeStruct((total, 128), F32),
            jax.ShapeDtypeStruct((total, width), F32),
        ),
        in_specs=[vmem, vmem, anywhere, anywhere, vmem, anywhere],
        out_specs=(vmem, vmem, vmem, vmem),
        scratch_shapes=[
            pltpu.VMEM((total, depth), BF16),
            pltpu.VMEM((total, depth), BF16),
            pltpu.VMEM((2, count, depth // 2), BF16),
            pltpu.VMEM(inner_weight.shape, BF16),
            pltpu.VMEM(state_weight.shape, BF16),
            pltpu.VMEM(out_weight.shape, BF16),
            pltpu.SemaphoreType.DMA((32,)),
            pltpu.SemaphoreType.DMA((32,)),
            pltpu.SemaphoreType.DMA((32,)),
            pltpu.SemaphoreType.DMA((32,)),
            pltpu.SemaphoreType.DMA((3,)),
        ],
        compiler_params=pltpu.CompilerParams(
            collective_id=0, has_side_effects=True, vmem_limit_bytes=VMEM_LIMIT
        ),
        name="gather_project",
    )(rows, grads, inner_weight, state_weight, step_weight, out_weight)


def scatter_kernel(
    gate_ref,
    inner_ref,
    dstate_ref,
    dstep_ref,
    inner_hbm,
    state_hbm,
    step_ref,
    out_ref,
    inner_w,
    state_w,
    mine,
    sib_out,
    sib_in,
    plus_out,
    plus_in,
    minus_out,
    minus_in,
    y_out,
    y_in,
    last_out,
    last_in,
    send_sib,
    recv_sib,
    send_ring,
    recv_ring,
    y_sem,
    weight_sem,
):
    loads = [
        pltpu.make_async_copy(inner_hbm, inner_w, weight_sem.at[0]),
        pltpu.make_async_copy(state_hbm, state_w, weight_sem.at[1]),
    ]
    for load in loads:
        load.start()
    yh, z, core = place()
    sibling = tp_id(yh, z, 1 - core)
    right = tp_id(yh, lax.rem(z + 1, Z), core)
    left = tp_id(yh, lax.rem(z + Z - 1, Z), core)
    across = tp_id(1 - yh, z, core)
    greet([across, right, left, sibling])
    for load in loads:
        load.wait()
    rows, depth = out_ref.shape
    pair, half = 2 * rows, depth // 2
    tile = 512
    started = []

    def remote(src, dst, send_sem, recv_sem, partner):
        return pltpu.make_async_remote_copy(
            src_ref=src,
            dst_ref=dst,
            send_sem=send_sem,
            recv_sem=recv_sem,
            device_id={"tp": partner},
            device_id_type=MESH,
        )

    dims = (((1,), (1,)), ((), ()))

    def product(place_at, dz):
        zt = lax.rem(z + (dz + Z), Z)
        spots = []
        for h in (0, 1):
            yt = yh if h == 0 else 1 - yh
            spots.append(pl.ds(pl.multiple_of((yt * Z + zt) * pair, 16), pair))

        def side(which, keep):
            def turn(j, carry):
                at = pl.ds(pl.multiple_of(j * tile, tile), tile)
                cols = pl.ds(pl.multiple_of(which * half + j * tile, tile), tile)
                parts = []
                for ref in (gate_ref, inner_ref, dstate_ref, dstep_ref):
                    parts.append(jnp.concatenate([ref[spots[0], :], ref[spots[1], :]], axis=0))
                value = lax.dot_general(parts[0], inner_w[0, cols, :], dims, preferred_element_type=F32)
                value += lax.dot_general(parts[1], inner_w[1, cols, :], dims, preferred_element_type=F32)
                value += lax.dot_general(parts[2], state_w[cols, :], dims, preferred_element_type=F32)
                value += lax.dot_general(parts[3], step_ref[cols, :], dims, preferred_element_type=F32)
                for h in (0, 1):
                    keep[place_at, h, :, at] = value[h * pair : (h + 1) * pair].astype(keep.dtype)
                return carry

            lax.fori_loop(0, half // tile, turn, 0)

        side(1 - core, sib_out)
        copy = remote(
            sib_out.at[place_at], sib_in.at[place_at], send_sib.at[place_at], recv_sib.at[place_at], sibling
        )
        copy.start()
        started.append(copy)
        side(core, mine)

    order = [-4, 3, -3, 2, -2, 1, -1, 0]
    places = {dz: i for i, dz in enumerate(order)}

    def ring_slot(way, d, h):
        base = 0 if way > 0 else 7
        return base + (0 if d == 4 else 1 + (3 - d) * 2 + (1 - h))

    def message(way, d, h):
        dz = way * d if d < 4 else -4
        at = places[dz]
        outs, ins = (plus_out, plus_in) if way > 0 else (minus_out, minus_in)
        slot = ring_slot(way, d, h)
        local = slot % 7
        earlier = None
        if d < 3 or (d == 3 and (way > 0) == (h == 0)):
            earlier = ring_slot(way, d + 1, h)
            before = ins.at[earlier % 7]
            remote(before, before, send_ring.at[earlier], recv_ring.at[earlier], right).wait_recv()

        def turn(j, carry):
            cols = pl.ds(pl.multiple_of(j * tile, tile), tile)
            value = mine[at, h, :, cols] + sib_in[at, h, :, cols].astype(F32)
            if earlier is not None:
                value += ins[earlier % 7, :, cols].astype(F32)
            outs[local, :, cols] = value.astype(BF16)
            return carry

        lax.fori_loop(0, half // tile, turn, 0)
        copy = remote(
            outs.at[local], ins.at[local], send_ring.at[slot], recv_ring.at[slot], right if way > 0 else left
        )
        copy.start()
        started.append(copy)

    def sib_got(dz):
        at = places[dz]
        there = sib_in.at[at]
        remote(there, there, send_sib.at[at], recv_sib.at[at], sibling).wait_recv()

    product(places[-4], -4)
    product(places[3], 3)
    sib_got(-4)
    message(1, 4, 0)
    message(-1, 4, 1)
    product(places[-3], -3)
    for d in (3, 2, 1):
        sib_got(d)
        message(1, d, 1 if d == 3 else 1)
        if d > 1:
            product(places[d - 1], d - 1)
        else:
            product(places[0], 0)
        sib_got(-d)
        message(-1, d, 1 if d < 3 else 0)
        message(1, d, 0)
        message(-1, d, 0 if d < 3 else 1)
        if d > 1:
            product(places[-(d - 1)], -(d - 1))
    sib_got(0)
    at = places[0]

    def ring_got(way, h):
        ins = plus_in if way > 0 else minus_in
        slot = ring_slot(way, 1, h)
        there = ins.at[slot % 7]
        remote(there, there, send_ring.at[slot], recv_ring.at[slot], right).wait_recv()
        return ins, slot % 7

    plus_ref, plus_at = ring_got(1, 1)
    minus_ref, minus_at = ring_got(-1, 1)

    def other(j, carry):
        cols = pl.ds(pl.multiple_of(j * tile, tile), tile)
        value = mine[at, 1, :, cols] + sib_in[at, 1, :, cols].astype(F32)
        value += plus_ref[plus_at, :, cols].astype(F32) + minus_ref[minus_at, :, cols].astype(F32)
        y_out[:, cols] = value.astype(BF16)
        return carry

    lax.fori_loop(0, half // tile, other, 0)
    swap = remote(y_out, y_in, y_sem.at[0], y_sem.at[1], across)
    swap.start()
    plus_own, plus_own_at = ring_got(1, 0)
    minus_own, minus_own_at = ring_got(-1, 0)
    swap.wait()

    first = core == 0

    def final(j, carry):
        cols = pl.ds(pl.multiple_of(j * tile, tile), tile)
        value = mine[at, 0, :, cols] + sib_in[at, 0, :, cols].astype(F32)
        value += plus_own[plus_own_at, :, cols].astype(F32) + minus_own[minus_own_at, :, cols].astype(F32)
        value += y_in[:, cols].astype(F32)
        low, high = value[:rows], value[rows:]
        here = pl.ds(pl.multiple_of(core * half + j * tile, tile), tile)
        out_ref[:, here] = jnp.where(first, low, high).astype(BF16)
        last_out[:, cols] = jnp.where(first, high, low).astype(BF16)
        return carry

    lax.fori_loop(0, half // tile, final, 0)
    swap = remote(last_out, last_in, y_sem.at[2], y_sem.at[3], sibling)
    swap.start()
    swap.wait()
    out_ref[:, pl.ds(pl.multiple_of((1 - core) * half, half), half)] = last_in[...]
    for copy in started:
        copy.wait_send()


def scattered(d_gate, d_inner, d_state, d_step, inner_weight, state_weight, step_weight):
    total = d_gate.shape[0]
    rows, depth = total // (4 * Z), state_weight.shape[0]
    vmem = pl.BlockSpec(memory_space=pltpu.VMEM)
    anywhere = pl.BlockSpec(memory_space=pl.ANY)
    return pl.pallas_call(
        scatter_kernel,
        out_shape=jax.ShapeDtypeStruct((rows, depth), BF16),
        in_specs=[vmem, vmem, vmem, vmem, anywhere, anywhere, vmem],
        out_specs=vmem,
        scratch_shapes=[
            pltpu.VMEM(inner_weight.shape, BF16),
            pltpu.VMEM(state_weight.shape, BF16),
            pltpu.VMEM((Z, 2, 2 * rows, depth // 2), F32),
            pltpu.VMEM((Z, 2, 2 * rows, depth // 2), BF16),
            pltpu.VMEM((Z, 2, 2 * rows, depth // 2), BF16),
            pltpu.VMEM((7, 2 * rows, depth // 2), BF16),
            pltpu.VMEM((7, 2 * rows, depth // 2), BF16),
            pltpu.VMEM((7, 2 * rows, depth // 2), BF16),
            pltpu.VMEM((7, 2 * rows, depth // 2), BF16),
            pltpu.VMEM((2 * rows, depth // 2), BF16),
            pltpu.VMEM((2 * rows, depth // 2), BF16),
            pltpu.VMEM((rows, depth // 2), BF16),
            pltpu.VMEM((rows, depth // 2), BF16),
            pltpu.SemaphoreType.DMA((Z,)),
            pltpu.SemaphoreType.DMA((Z,)),
            pltpu.SemaphoreType.DMA((14,)),
            pltpu.SemaphoreType.DMA((14,)),
            pltpu.SemaphoreType.DMA((4,)),
            pltpu.SemaphoreType.DMA((2,)),
        ],
        compiler_params=pltpu.CompilerParams(
            collective_id=1, has_side_effects=True, vmem_limit_bytes=VMEM_LIMIT
        ),
        name="product_scatter",
    )(d_gate, d_inner, d_state, d_step, inner_weight, state_weight, step_weight)


def to(axis, partner, src, dst, send_sem, recv_sem):
    return pltpu.make_async_remote_copy(
        src_ref=src,
        dst_ref=dst,
        send_sem=send_sem,
        recv_sem=recv_sem,
        device_id={axis: partner},
        device_id_type=MESH,
    )


def dot(a, b, contract, precision=EXACT):
    return lax.dot_general(
        a, b, (contract, ((), ())), precision=precision, preferred_element_type=F32
    )


NN, NT, TN = ((1,), (0,)), ((1,), (1,)), ((0,), (0,))
CHUNK = 128
HALO = 8
SHARDS = 8


def mixer_kernel(
    step_bias_ref,
    decay_log_ref,
    gate_ref,
    conv_ref,
    stepraw_ref,
    local_ref,
    conv_inner_ref,
    conv_state_ref,
    gain_ref,
    d_gate_ref,
    d_inner_ref,
    d_state_ref,
    d_step_ref,
    ext,
    pre,
    act,
    xd,
    steps,
    cums,
    cb,
    decays,
    out,
    dy,
    states,
    d_states,
    entering,
    d_leaving,
    fwd_out,
    fwd_in,
    bwd_out,
    bwd_in,
    tot_out,
    tot_in,
    d_pre,
    d_b,
    u_loc,
    halo_sem,
    fwd_send,
    fwd_recv,
    bwd_send,
    bwd_recv,
    tot_send,
    tot_recv,
):
    tp, ctx = lax.axis_index("tp"), lax.axis_index("ctx")
    group = 4 * Z
    barrier = pltpu.get_barrier_semaphore()
    for j in range(1, group):
        pl.semaphore_signal(barrier, inc=1, device_id={"tp": lax.rem(tp + j, group)}, device_id_type=MESH)
    for j in range(1, SHARDS):
        pl.semaphore_signal(barrier, inc=1, device_id={"ctx": lax.rem(ctx + j, SHARDS)}, device_id_type=MESH)
    total = conv_ref.shape[0]
    width = gate_ref.shape[1]
    heads = width // HEAD_DIM
    chunks = total // CHUNK
    channels = width * group
    span = lambda k: slice(k * CHUNK, (k + 1) * CHUNK)
    ext[HALO:, :] = conv_ref[...].astype(F32)
    pl.semaphore_wait(barrier, group + SHARDS - 2)

    halo = to("ctx", lax.rem(ctx + 1, SHARDS), ext.at[total:, :], ext.at[:HALO, :], halo_sem.at[0], halo_sem.at[1])

    @pl.when(ctx < SHARDS - 1)
    def _():
        halo.start()

    lane = lax.broadcasted_iota(jnp.int32, (1, CHUNK), 1)
    rows_at = lax.broadcasted_iota(jnp.int32, (CHUNK, CHUNK), 0)
    cols_at = lax.broadcasted_iota(jnp.int32, (CHUNK, CHUNK), 1)
    causal = (rows_at >= cols_at).astype(F32)
    anti = (rows_at <= cols_at).astype(F32)

    def per_lane(values):
        row = jnp.zeros_like(values[0])
        for h, value in enumerate(values):
            row = jnp.where(lane == h, value, row)
        return row

    bias = per_lane([jnp.full((1, CHUNK), step_bias_ref[h], F32) for h in range(heads)])
    rate = per_lane([jnp.exp(jnp.full((1, CHUNK), decay_log_ref[h], F32)) for h in range(heads)])
    valid = lane < heads
    kernel = [
        jnp.concatenate([conv_inner_ref[k : k + 1, :], conv_state_ref[k : k + 1, :]], axis=1)
        for k in range(CONV)
    ]

    ends = []
    for k in range(chunks):
        raw = jnp.where(valid, stepraw_ref[span(k), :], 0.0) + bias
        step = jnp.maximum(raw, 0.0) + jnp.log1p(jnp.exp(-jnp.abs(raw)))
        step = jnp.where(valid, step, 0.0)
        steps[span(k), :] = step
        cum = dot(causal, -step * rate, NN)
        cums[span(k), :] = cum
        turned = cum.T
        ends.append([cum[CHUNK - 1 :, h : h + 1] for h in range(heads)])
        for h in range(heads):
            spread = cum[:, h : h + 1] - turned[h : h + 1, :]
            decays[k, h] = jnp.exp(jnp.minimum(spread, 0.0)) * causal

    @pl.when(ctx == 0)
    def _():
        ext[:HALO, :] = jnp.zeros((HALO, ext.shape[1]), F32)

    @pl.when(ctx > 0)
    def _():
        halo.wait_recv()

    for k in range(chunks):
        blended = jnp.zeros((CHUNK, ext.shape[1]), F32)
        for tap in range(CONV):
            start = k * CHUNK + HALO - (CONV - 1) + tap
            blended += kernel[tap] * ext[start : start + CHUNK, :]
        pre[span(k), :] = blended
        active = blended * jax.nn.sigmoid(blended)
        act[span(k), :] = active
        b_rows, c_rows = active[:, width : width + STATE], active[:, width + STATE :]
        cb[k] = dot(c_rows, b_rows, NT)
        for h in range(heads):
            lanes = slice(h * HEAD_DIM, (h + 1) * HEAD_DIM)
            fed = active[:, lanes] * steps[span(k), h : h + 1]
            xd[span(k), lanes] = fed
            left = jnp.exp(ends[k][h] - cums[span(k), h : h + 1])
            own = dot(fed * left, b_rows, TN)
            if k == 0:
                states[0, h] = jnp.zeros_like(own)
                states[1, h] = own
            else:
                states[k + 1, h] = jnp.exp(ends[k][h]) * states[k, h] + own

    befores = [[jnp.zeros((1, 1), F32) for _ in range(heads)]]
    for k in range(chunks):
        befores.append([befores[k][h] + ends[k][h] for h in range(heads)])
    whole = [jnp.exp(befores[chunks][h]) for h in range(heads)]
    row8 = lax.broadcasted_iota(jnp.int32, (8, CHUNK), 0)
    factors = jnp.zeros((8, CHUNK), F32)
    for h in range(heads):
        fwd_out[h * HEAD_DIM : (h + 1) * HEAD_DIM, :] = states[chunks, h]
        factors = jnp.where(row8 == h, whole[h], factors)
    fwd_out[heads * HEAD_DIM :, :] = factors
    bwd_out[heads * HEAD_DIM :, :] = factors

    forward = []
    for d in range(1, SHARDS):
        copy = to("ctx", lax.rem(ctx + d, SHARDS), fwd_out, fwd_in.at[d - 1], fwd_send.at[d - 1], fwd_recv.at[d - 1])
        forward.append(copy)

        @pl.when(ctx + d < SHARDS)
        def _(copy=copy):
            copy.start()

    def collect(gathered_in, copies, into, there):
        into[...] = jnp.zeros_like(into)
        for d in range(SHARDS - 1, 0, -1):

            @pl.when(there(d))
            def _(d=d):
                copies[d - 1].wait_recv()
                for h in range(heads):
                    at = heads * HEAD_DIM + h
                    factor = gathered_in[d - 1, at : at + 1, :]
                    into[h] = into[h] * factor + gathered_in[d - 1, h * HEAD_DIM : (h + 1) * HEAD_DIM, :]

    for k in range(chunks):
        c_rows = act[span(k), width + STATE :]
        for h in range(heads):
            lanes = slice(h * HEAD_DIM, (h + 1) * HEAD_DIM)
            value = dot(decays[k, h] * cb[k], xd[span(k), lanes], NN)
            if k > 0:
                value += jnp.exp(cums[span(k), h : h + 1]) * dot(c_rows, states[k, h], NT)
            out[span(k), lanes] = value

    collect(fwd_in, forward, entering, lambda d: ctx >= d)
    gain = gain_ref[...]
    ones = jnp.ones((8, width), F32)
    for k in range(chunks):
        c_rows = act[span(k), width + STATE :]
        for h in range(heads):
            lanes = slice(h * HEAD_DIM, (h + 1) * HEAD_DIM)
            grown = jnp.exp(cums[span(k), h : h + 1] + befores[k][h])
            out[span(k), lanes] = out[span(k), lanes] + grown * dot(c_rows, entering[h], NT)
            states[k, h] = states[k, h] + jnp.exp(befores[k][h]) * entering[h]
        gate = gate_ref[span(k), :].astype(F32)
        gated = out[span(k), :] * (gate * jax.nn.sigmoid(gate))
        squares = dot(ones, gated * gated, NT)
        crosses = dot(ones, gain * local_ref[span(k), :] * gated, NT)
        tot_out[0:1, span(k)] = squares[0:1, :]
        tot_out[1:2, span(k)] = crosses[0:1, :]
    for h in range(heads):
        states[chunks, h] = states[chunks, h] + whole[h] * entering[h]

    totals = []
    for j in range(1, group):
        copy = to("tp", lax.rem(tp + j, group), tot_out, tot_in.at[j - 1], tot_send.at[j - 1], tot_recv.at[j - 1])
        copy.start()
        totals.append(copy)
    sums = tot_out[...]
    for j, copy in enumerate(totals):
        copy.wait_recv()
        sums = sums + tot_in[j]

    for k in range(chunks):
        held = jnp.concatenate([sums[:, span(k)], jnp.zeros((CHUNK - 2, CHUNK), F32)], axis=0).T
        inverse = lax.rsqrt(held[:, 0:1] / channels + EPSILON)
        pull = inverse * inverse * inverse * (held[:, 1:2] / channels)
        gate = gate_ref[span(k), :].astype(F32)
        sigmoid = jax.nn.sigmoid(gate)
        opened = gate * sigmoid
        value = out[span(k), :]
        d_gated = inverse * (gain * local_ref[span(k), :]) - value * opened * pull
        d_gate_ref[span(k), :] = (d_gated * value * sigmoid * (1.0 + gate * (1.0 - sigmoid))).astype(BF16)
        dy[span(k), :] = d_gated * opened

    for k in range(chunks - 1, -1, -1):
        c_rows = act[span(k), width + STATE :]
        for h in range(heads):
            lanes = slice(h * HEAD_DIM, (h + 1) * HEAD_DIM)
            own = dot(dy[span(k), lanes] * jnp.exp(cums[span(k), h : h + 1]), c_rows, TN)
            if k < chunks - 1:
                own += jnp.exp(ends[k][h]) * d_states[k + 1, h]
            d_states[k, h] = own
    for h in range(heads):
        bwd_out[h * HEAD_DIM : (h + 1) * HEAD_DIM, :] = d_states[0, h]
    backward = []
    for d in range(1, SHARDS):
        copy = to("ctx", lax.rem(ctx + SHARDS - d, SHARDS), bwd_out, bwd_in.at[d - 1], bwd_send.at[d - 1], bwd_recv.at[d - 1])
        backward.append(copy)

        @pl.when(ctx >= d)
        def _(copy=copy):
            copy.start()

    d_c = cb
    for k in range(chunks):
        b_rows, c_rows = act[span(k), width : width + STATE], act[span(k), width + STATE :]
        d_cb = jnp.zeros((CHUNK, CHUNK), F32)
        d_crows = jnp.zeros((CHUNK, STATE), F32)
        for h in range(heads):
            lanes = slice(h * HEAD_DIM, (h + 1) * HEAD_DIM)
            grad = dy[span(k), lanes]
            d_cb += decays[k, h] * dot(grad, xd[span(k), lanes], NT)
            u_loc[span(k), lanes] = dot(decays[k, h] * cb[k], grad, TN)
            d_crows += jnp.exp(cums[span(k), h : h + 1]) * dot(grad, states[k, h], NN)
        d_b[span(k), :] = dot(d_cb, c_rows, TN)
        d_c[k] = d_crows + dot(d_cb, b_rows, NN)

    collect(bwd_in, backward, d_leaving, lambda d: ctx + d < SHARDS)
    after = [jnp.zeros((1, 1), F32) for _ in range(heads)]
    d_states[chunks] = d_leaving[...]
    for k in range(chunks - 1, 0, -1):
        after = [after[h] + ends[k][h] for h in range(heads)]
        for h in range(heads):
            d_states[k, h] = d_states[k, h] + jnp.exp(after[h]) * d_leaving[h]

    halo2 = to("ctx", lax.rem(ctx + SHARDS - 1, SHARDS), d_pre.at[:HALO, :], d_pre.at[total:, :], halo_sem.at[2], halo_sem.at[3])
    for k in range(chunks):
        b_rows = act[span(k), width : width + STATE]
        d_brows = d_b[span(k), :]
        d_acts = []
        pulls = jnp.zeros((CHUNK, CHUNK), F32)
        feeds = jnp.zeros((CHUNK, CHUNK), F32)
        edge = jnp.zeros((1, CHUNK), F32)
        for h in range(heads):
            lanes = slice(h * HEAD_DIM, (h + 1) * HEAD_DIM)
            step = steps[span(k), h : h + 1]
            left = jnp.exp(ends[k][h] - cums[span(k), h : h + 1])
            d_next = d_states[k + 1, h]
            grad = u_loc[span(k), lanes] + left * dot(b_rows, d_next, NT)
            d_brows += dot(xd[span(k), lanes] * left, d_next, NN)
            d_acts.append(grad * step)
            fed = jnp.sum(grad * act[span(k), lanes], axis=1, keepdims=True)
            met = jnp.sum(dy[span(k), lanes] * out[span(k), lanes], axis=1, keepdims=True)
            pulls = jnp.where(lane == h, met - step * fed, pulls)
            feeds = jnp.where(lane == h, fed, feeds)
            edge = jnp.where(lane == h, jnp.sum(d_next * states[k + 1, h]), edge)
        d_decay = dot(anti, pulls, NN) + edge
        raw = jnp.where(valid, stepraw_ref[span(k), :], 0.0) + bias
        d_raw = (feeds - rate * d_decay) * jax.nn.sigmoid(raw)
        d_step_ref[span(k), :] = d_raw[:, :heads].astype(BF16)
        d_act = jnp.concatenate(d_acts + [d_brows, d_c[k]], axis=1)
        value = pre[span(k), :]
        sigmoid = jax.nn.sigmoid(value)
        d_pre[span(k), :] = d_act * sigmoid * (1.0 + value * (1.0 - sigmoid))
        if k == 0:

            @pl.when(ctx > 0)
            def _():
                halo2.start()

    @pl.when(ctx == SHARDS - 1)
    def _():
        d_pre[total:, :] = jnp.zeros((HALO, d_pre.shape[1]), F32)

    @pl.when(ctx < SHARDS - 1)
    def _():
        halo2.wait_recv()

    for k in range(chunks):
        blended = jnp.zeros((CHUNK, ext.shape[1]), F32)
        for tap in range(CONV):
            start = k * CHUNK + CONV - 1 - tap
            blended += kernel[tap] * d_pre[start : start + CHUNK, :]
        d_inner_ref[span(k), :] = blended[:, :width].astype(BF16)
        d_state_ref[span(k), :] = blended[:, width:].astype(BF16)

    @pl.when(ctx < SHARDS - 1)
    def _():
        halo.wait_send()

    @pl.when(ctx > 0)
    def _():
        halo2.wait_send()

    for d in range(1, SHARDS):

        @pl.when(ctx + d < SHARDS)
        def _(d=d):
            forward[d - 1].wait_send()

        @pl.when(ctx >= d)
        def _(d=d):
            backward[d - 1].wait_send()

    for copy in totals:
        copy.wait_send()


def mixed(gate, conv, stepraw, local, conv_inner, conv_state, step_bias, decay_log, norm_gain):
    total, width = gate.shape
    heads = width // HEAD_DIM
    both = conv.shape[1]
    chunks = total // CHUNK
    group = 4 * Z
    vmem = pl.BlockSpec(memory_space=pltpu.VMEM)
    smem = pl.BlockSpec(memory_space=pltpu.SMEM)
    message = heads * HEAD_DIM + 8
    return pl.pallas_call(
        mixer_kernel,
        out_shape=(
            jax.ShapeDtypeStruct((total, width), BF16),
            jax.ShapeDtypeStruct((total, width), BF16),
            jax.ShapeDtypeStruct((total, both - width), BF16),
            jax.ShapeDtypeStruct((total, heads), BF16),
        ),
        in_specs=[smem, smem] + [vmem] * 7,
        out_specs=(vmem,) * 4,
        scratch_shapes=[
            pltpu.VMEM((HALO + total, both), F32),
            pltpu.VMEM((total, both), F32),
            pltpu.VMEM((total, both), F32),
            pltpu.VMEM((total, width), F32),
            pltpu.VMEM((total, CHUNK), F32),
            pltpu.VMEM((total, CHUNK), F32),
            pltpu.VMEM((chunks, CHUNK, CHUNK), F32),
            pltpu.VMEM((chunks, heads, CHUNK, CHUNK), F32),
            pltpu.VMEM((total, width), F32),
            pltpu.VMEM((total, width), F32),
            pltpu.VMEM((chunks + 1, heads, HEAD_DIM, STATE), F32),
            pltpu.VMEM((chunks + 1, heads, HEAD_DIM, STATE), F32),
            pltpu.VMEM((heads, HEAD_DIM, STATE), F32),
            pltpu.VMEM((heads, HEAD_DIM, STATE), F32),
            pltpu.VMEM((message, STATE), F32),
            pltpu.VMEM((SHARDS - 1, message, STATE), F32),
            pltpu.VMEM((message, STATE), F32),
            pltpu.VMEM((SHARDS - 1, message, STATE), F32),
            pltpu.VMEM((2, total), F32),
            pltpu.VMEM((group - 1, 2, total), F32),
            pltpu.VMEM((total + HALO, both), F32),
            pltpu.VMEM((total, STATE), F32),
            pltpu.VMEM((total, width), F32),
            pltpu.SemaphoreType.DMA((4,)),
            pltpu.SemaphoreType.DMA((SHARDS - 1,)),
            pltpu.SemaphoreType.DMA((SHARDS - 1,)),
            pltpu.SemaphoreType.DMA((SHARDS - 1,)),
            pltpu.SemaphoreType.DMA((SHARDS - 1,)),
            pltpu.SemaphoreType.DMA((group - 1,)),
            pltpu.SemaphoreType.DMA((group - 1,)),
        ],
        compiler_params=pltpu.CompilerParams(
            collective_id=2, has_side_effects=True, vmem_limit_bytes=VMEM_LIMIT
        ),
        name="mixer",
    )(step_bias, decay_log, gate, conv, stepraw, local, conv_inner, conv_state, norm_gain.reshape(1, -1))


def body(
    normed_rows,
    out_grad,
    inner_weight,
    state_weight,
    step_weight,
    conv_inner,
    conv_state,
    step_bias,
    decay_log,
    norm_gain,
    out_weight,
):
    gate, conv, stepraw, local = gathered(
        normed_rows, out_grad, inner_weight, state_weight, step_weight, out_weight
    )
    d_gate, d_inner, d_state, d_step = mixed(
        gate, conv, stepraw, local, conv_inner, conv_state, step_bias, decay_log, norm_gain
    )
    return scattered(d_gate, d_inner, d_state, d_step, inner_weight, state_weight, step_weight)


def solution(mesh):
    placed = (
        P(("ctx", "tp"), None),
        P(("ctx", "tp"), None),
        P(None, None, "tp"),
        P(),
        P(None, "tp"),
        P(None, "tp"),
        P(),
        P("tp"),
        P("tp"),
        P("tp"),
        P("tp", None),
    )
    return jax.shard_map(
        body, mesh=mesh, in_specs=placed, out_specs=P(("ctx", "tp"), None), check_vma=False
    )
```

```python
import functools
from types import SimpleNamespace

import jax
import jax.numpy as jnp
from jax import lax
from jax.experimental import pallas as pl
from jax.experimental.pallas import tpu as pltpu
from jax.sharding import PartitionSpec as P

HEAD_DIM = 128
STATE = 128
CONV = 4
EPSILON = 1e-05
EXACT = lax.Precision.HIGHEST
MESH = pl.DeviceIdType.MESH
F32 = jnp.float32
BF16 = jnp.bfloat16
VMEM_LIMIT = 62 * 1024 * 1024

Z = 8
GROUP = 4 * Z
ROW = 4
SHARDS = 2 * ROW
CHUNK = 128
HALO = 8
NN, NT, TN = ((1,), (0,)), ((1,), (1,)), ((0,), (0,))


def place():
    tp = lax.axis_index("tp")
    return tp // (2 * Z), lax.rem(tp // 2, Z), lax.rem(tp, 2)


def tp_id(yh, z, core):
    return (yh * Z + lax.rem(z + Z, Z)) * 2 + core


def remote(axis, partner, src, dst, send_sem, recv_sem):
    return pltpu.make_async_remote_copy(
        src_ref=src,
        dst_ref=dst,
        send_sem=send_sem,
        recv_sem=recv_sem,
        device_id={axis: partner},
        device_id_type=MESH,
    )


def dot(a, b, contract, precision=EXACT):
    return lax.dot_general(a, b, (contract, ((), ())), precision=precision, preferred_element_type=F32)


def dot16(a, b, contract):
    return lax.dot_general(a, b, (contract, ((), ())), preferred_element_type=F32)


class Gather:
    def __init__(self, own_ref, buf, swap, send_sem, recv_sem):
        self.own_ref, self.buf, self.swap = own_ref, buf, swap
        self.send_sem, self.recv_sem = send_sem, recv_sem
        self.yh, self.z, self.core = place()
        self.pair = 2 * own_ref.shape[0]
        self.half = own_ref.shape[1] // 2
        self.sibling = tp_id(self.yh, self.z, 1 - self.core)
        self.started = []

    def block(self, h, dz, sub, core=None):
        yh = self.yh if h == 0 else 1 - self.yh
        chip = yh * Z + lax.rem(self.z + (dz + Z), Z)
        rows = pl.ds(pl.multiple_of(chip * self.pair, 16), self.pair)
        quarter = self.half // 2
        at = (self.core if core is None else core) * self.half + sub * quarter
        return self.buf.at[rows, pl.ds(pl.multiple_of(at, quarter), quarter)]

    def copy(self, slot, src, dst, partner):
        return remote("tp", partner, src, dst, self.send_sem.at[slot], self.recv_sem.at[slot])

    def send(self, slot, src, dst, partner):
        copy = self.copy(slot, src, dst, partner)
        copy.start()
        self.started.append(copy)

    def got(self, slot, block):
        self.copy(slot, block, block, self.sibling).wait_recv()

    def across(self, sub, d):
        here = self.block(0, (1 - 2 * sub) * d, sub)
        self.send(sub * 31 + d, here, here, tp_id(1 - self.yh, self.z, self.core))

    def along(self, kind, sub, d):
        way = 1 - 2 * sub
        if kind == "long":
            here = self.block(0, way * (d - 1), sub)
            self.send(sub * 31 + 4 + d, here, here, tp_id(self.yh, self.z - way, self.core))
        elif kind == "short":
            here = self.block(0, -way * (d - 1), sub)
            self.send(sub * 31 + 9 + d, here, here, tp_id(self.yh, self.z + way, self.core))
        else:
            here = self.block(1, -way * (d - 1), sub)
            self.send(sub * 31 + 11 + d, here, here, tp_id(self.yh, self.z + way, self.core))

    def sibling_slot(self, h, dz, sub):
        return sub * 31 + 15 + h * 8 + dz % 8

    def to_sibling(self, h, dz, sub):
        here = self.block(h, dz, sub)
        self.send(self.sibling_slot(h, dz, sub), here, here, self.sibling)

    def first_swap(self):
        columns = pl.ds(pl.multiple_of((1 - self.core) * self.half, self.half), self.half)
        self.send(62, self.own_ref.at[:, columns], self.swap, self.sibling)

    def begin(self):
        self.got(62, self.swap)
        columns = pl.ds(pl.multiple_of(self.core * self.half, self.half), self.half)
        mine = self.own_ref[:, columns].astype(F32)
        other = self.swap[...].astype(F32)
        first = self.core == 0
        both = jnp.concatenate([jnp.where(first, mine, other), jnp.where(first, other, mine)], axis=0)
        quarter = self.half // 2
        for sub in (0, 1):
            self.block(0, 0, sub)[...] = both[:, sub * quarter : (sub + 1) * quarter].astype(BF16)
        for sub in (0, 1):
            self.along("long", sub, 1)
            self.across(sub, 0)
            self.along("short", sub, 1)
            self.to_sibling(0, 0, sub)

    def long(self, d):
        for sub in (0, 1):
            dz = (1 - 2 * sub) * d
            self.got(sub * 31 + 4 + d, self.block(0, dz, sub))
            if d < 5:
                self.along("long", sub, d + 1)
                self.across(sub, d)
            self.to_sibling(0, dz, sub)

    def short(self, d):
        for sub in (0, 1):
            dz = -(1 - 2 * sub) * d
            self.got(sub * 31 + 9 + d, self.block(0, dz, sub))
            if d < 2:
                self.along("short", sub, d + 1)
            self.to_sibling(0, dz, sub)

    def met(self, d):
        for sub in (0, 1):
            dz = (1 - 2 * sub) * d
            self.got(sub * 31 + d, self.block(1, dz, sub))
            if d == 0:
                self.along("other", sub, 1)
            self.to_sibling(1, dz, sub)

    def other(self, d):
        for sub in (0, 1):
            dz = -(1 - 2 * sub) * d
            self.got(sub * 31 + 11 + d, self.block(1, dz, sub))
            if d < 3:
                self.along("other", sub, d + 1)
            self.to_sibling(1, dz, sub)

    def steps(self):
        order = [
            (self.long, 1), (self.short, 1), (self.met, 0), (self.long, 2), (self.short, 2), (self.met, 1),
            (self.other, 1), (self.long, 3), (self.met, 2), (self.other, 2), (self.long, 4), (self.met, 3),
            (self.other, 3), (self.long, 5), (self.met, 4),
        ]
        return [functools.partial(step, d) for step, d in order]

    def finish(self):
        for sub in (0, 1):
            for h in (0, 1):
                for dz in range(8):
                    self.got(self.sibling_slot(h, dz, sub), self.block(h, dz, sub, 1 - self.core))

    def drain(self):
        for copy in self.started:
            copy.wait_send()


class Scatter:
    order = (-3, 3, -4, 2, -2, 1, -1, 0)

    def __init__(self, r, rows, depth):
        self.r = r
        self.yh, self.z, self.core = place()
        self.sibling = tp_id(self.yh, self.z, 1 - self.core)
        self.rows, self.pair, self.half = rows, 2 * rows, depth // 2
        self.quarter = self.half // 2
        self.tile = 512
        self.started = []

    def at(self, dz):
        return self.order.index(dz if dz < 4 and dz > -4 else -4 if abs(dz) == 4 else dz - 8 if dz > 0 else dz + 8)

    def start(self, copy):
        copy.start()
        self.started.append(copy)

    def product(self, dz):
        r, at, half, tile = self.r, self.at(dz), self.half, self.tile
        zt = lax.rem(self.z + (dz + Z), Z)
        spots = []
        for h in (0, 1):
            yt = self.yh if h == 0 else 1 - self.yh
            spots.append(pl.ds(pl.multiple_of((yt * Z + zt) * self.pair, 16), self.pair))

        def side(which, keep):
            def turn(j, carry):
                here = pl.ds(pl.multiple_of(j * tile, tile), tile)
                cols = pl.ds(pl.multiple_of(which * half + j * tile, tile), tile)
                parts = []
                for ref in (r.d_gate, r.d_inner, r.d_state, r.d_step):
                    parts.append(jnp.concatenate([ref[spots[0], :], ref[spots[1], :]], axis=0))
                value = dot16(parts[0], r.inner_w[0, cols, :], NT)
                value += dot16(parts[1], r.inner_w[1, cols, :], NT)
                value += dot16(parts[2], r.state_w[cols, :], NT)
                value += dot16(parts[3], r.step_w[:, cols], NN)
                for h in (0, 1):
                    keep[at, h, :, here] = value[h * self.pair : (h + 1) * self.pair].astype(keep.dtype)
                return carry

            lax.fori_loop(0, half // tile, turn, 0)

        side(1 - self.core, r.sib_out)
        self.start(
            remote("tp", self.sibling, r.sib_out.at[at], r.sib_in.at[at], r.sib_send.at[at], r.sib_recv.at[at])
        )
        side(self.core, r.mine)

    def sib_got(self, dz):
        at, r = self.at(dz), self.r
        there = r.sib_in.at[at]
        remote("tp", self.sibling, there, there, r.sib_send.at[at], r.sib_recv.at[at]).wait_recv()

    def got(self, slot):
        there = self.r.ring_in.at[slot]
        remote("tp", self.sibling, there, there, self.r.ring_send.at[slot], self.r.ring_recv.at[slot]).wait_recv()

    def slot(self, kind, sub, d):
        return sub * 15 + {"y": 0, "long": 4, "short": 9, "other": 11}[kind] + d

    def value(self, h, dz, sub, slots, columns):
        at, r = self.at(dz), self.r
        here = pl.ds(pl.multiple_of(sub * self.quarter + columns, self.tile), self.tile)
        there = pl.ds(pl.multiple_of(columns, self.tile), self.tile)
        total = r.mine[at, h, :, here] + r.sib_in[at, h, :, here].astype(F32)
        for slot in slots:
            total += r.ring_in[slot, :, there].astype(F32)
        return total

    def message(self, kind, sub, d):
        way = 1 - 2 * sub
        earlier = []
        if kind == "y":
            h, dz, partner = 1, way * d, tp_id(1 - self.yh, self.z, self.core)
            if d == 0:
                earlier.append(self.slot("other", sub, 1))
        elif kind == "long":
            h, dz, partner = 0, way * d, tp_id(self.yh, self.z + way, self.core)
            if d < 5:
                earlier += [self.slot("long", sub, d + 1), self.slot("y", sub, d)]
        elif kind == "short":
            h, dz, partner = 0, -way * d, tp_id(self.yh, self.z - way, self.core)
            if d < 2:
                earlier.append(self.slot("short", sub, d + 1))
        else:
            h, dz, partner = 1, -way * d, tp_id(self.yh, self.z - way, self.core)
            if d < 3:
                earlier.append(self.slot("other", sub, d + 1))
        for slot in earlier:
            self.got(slot)
        slot, r = self.slot(kind, sub, d), self.r

        def turn(j, carry):
            columns = j * self.tile
            there = pl.ds(pl.multiple_of(columns, self.tile), self.tile)
            r.ring_out[slot, :, there] = self.value(h, dz, sub, earlier, columns).astype(BF16)
            return carry

        lax.fori_loop(0, self.quarter // self.tile, turn, 0)
        self.start(
            remote("tp", partner, r.ring_out.at[slot], r.ring_in.at[slot], r.ring_send.at[slot], r.ring_recv.at[slot])
        )

    def run(self, out_ref):
        r, core, half = self.r, self.core, self.half

        def both(kind, d):
            for sub in (0, 1):
                self.message(kind, sub, d)

        self.product(-3)
        self.product(3)
        self.sib_got(-3)
        self.message("long", 0, 5)
        self.message("other", 0, 3)
        self.message("y", 1, 3)
        self.product(-4)
        self.sib_got(3)
        self.message("long", 1, 5)
        self.message("other", 1, 3)
        self.message("y", 0, 3)
        self.product(2)
        self.sib_got(-4)
        both("y", 4)
        self.product(-2)
        both("long", 4)
        self.sib_got(2)
        self.message("short", 1, 2)
        self.message("y", 0, 2)
        self.sib_got(-2)
        self.message("short", 0, 2)
        self.message("y", 1, 2)
        self.product(1)
        both("other", 2)
        both("long", 3)
        self.product(-1)
        self.sib_got(1)
        self.sib_got(-1)
        both("y", 1)
        both("other", 1)
        both("short", 1)
        self.product(0)
        both("long", 2)
        self.sib_got(0)
        both("y", 0)
        both("long", 1)
        first = core == 0
        for sub in (0, 1):
            earlier = [self.slot(*key) for key in (("short", sub, 1), ("y", sub, 0), ("long", sub, 1))]
            for slot in earlier:
                self.got(slot)

            def final(j, carry, sub=sub, earlier=earlier):
                columns = j * self.tile
                value = self.value(0, 0, sub, earlier, columns)
                low, high = value[: self.rows], value[self.rows :]
                at = sub * self.quarter + columns
                here = pl.ds(pl.multiple_of(core * half + at, self.tile), self.tile)
                out_ref[:, here] = jnp.where(first, low, high).astype(BF16)
                there = pl.ds(pl.multiple_of(columns, self.tile), self.tile)
                r.last_out[sub, :, there] = jnp.where(first, high, low).astype(BF16)
                return carry

            lax.fori_loop(0, self.quarter // self.tile, final, 0)
            self.start(
                remote(
                    "tp", self.sibling, r.last_out.at[sub], r.last_in.at[sub], r.last_send.at[sub], r.last_recv.at[sub]
                )
            )
        for sub in (0, 1):
            there = r.last_in.at[sub]
            remote("tp", self.sibling, there, there, r.last_send.at[sub], r.last_recv.at[sub]).wait_recv()
            at = (1 - core) * half + sub * self.quarter
            out_ref[:, pl.ds(pl.multiple_of(at, self.quarter), self.quarter)] = r.last_in[sub]
        for copy in self.started:
            copy.wait_send()


class Exchange:
    def __init__(self, out, into, cross_out, cross_in, send_sem, recv_sem, factors_in, heads, forward):
        self.ctx = lax.axis_index("ctx")
        self.x, self.y = lax.rem(self.ctx, ROW), self.ctx // ROW
        self.out, self.into, self.heads, self.forward = out, into, heads, forward
        self.factors_in, self.cross_out, self.cross_in = factors_in, cross_out, cross_in
        self.gives = self.y == (0 if forward else 1)
        self.copies = [
            remote("ctx", self.peer(j), out, into.at[j - 1], send_sem.at[j - 1], recv_sem.at[j - 1])
            for j in range(1, ROW)
        ]
        self.cross = remote(
            "ctx", lax.rem(self.ctx + ROW, SHARDS), cross_out, cross_in, send_sem.at[ROW - 1], recv_sem.at[ROW - 1]
        )

    def peer(self, j):
        return self.y * ROW + lax.rem(self.x + j, ROW)

    def start(self):
        for copy in self.copies:
            copy.start()

    def step(self, value, slot):
        parts = []
        for h in range(self.heads):
            state = self.into[slot, h * HEAD_DIM : (h + 1) * HEAD_DIM, :].astype(F32)
            parts.append(value[h] * self.factors_in[slot, h : h + 1, :] + state)
        return parts

    def chain(self, total):
        for j in range(ROW - 1, 0, -1):
            there = self.x >= j if self.forward else self.x + j < ROW
            slot = j - 1 if self.forward else ROW - 1 - j

            @pl.when(there)
            def _(slot=slot):
                for h, part in enumerate(self.step([total[h] for h in range(self.heads)], slot)):
                    total[h] = part

    def give(self, total, own, factors):
        for copy in self.copies:
            copy.wait_recv()

        @pl.when(self.gives)
        def _():
            total[...] = jnp.zeros_like(total)
            self.chain(total)
            for h in range(self.heads):
                self.cross_sum[h] = total[h] * factors[h : h + 1, :] + own[h]
            for j in range(1, ROW):
                there = self.x + j < ROW if self.forward else self.x >= j
                slot = ROW - 1 - j if self.forward else j - 1

                @pl.when(there)
                def _(slot=slot):
                    for h, part in enumerate(self.step([self.cross_sum[h] for h in range(self.heads)], slot)):
                        self.cross_sum[h] = part

            for h in range(self.heads):
                self.cross_out[h * HEAD_DIM : (h + 1) * HEAD_DIM, :] = self.cross_sum[h]
            self.cross.start()

    def take(self, total):
        @pl.when(jnp.logical_not(self.gives))
        def _():
            self.cross.wait_recv()
            for h in range(self.heads):
                total[h] = self.cross_in[h * HEAD_DIM : (h + 1) * HEAD_DIM, :].astype(F32)
            self.chain(total)

    def drain(self):
        for copy in self.copies:
            copy.wait_send()

        @pl.when(self.gives)
        def _():
            self.cross.wait_send()


def mixer_forward(r, tick):
    ctx = lax.axis_index("ctx")
    total, both = r.conv.shape
    width = both - 2 * STATE
    heads = width // HEAD_DIM
    chunks = total // CHUNK
    span = lambda k: slice(k * CHUNK, (k + 1) * CHUNK)
    r.ext[HALO:, :] = r.conv[...].astype(F32)
    halo = remote("ctx", lax.rem(ctx + 1, SHARDS), r.ext.at[total:, :], r.ext.at[:HALO, :], r.halo_sem.at[0], r.halo_sem.at[1])

    @pl.when(ctx < SHARDS - 1)
    def _():
        halo.start()

    lane = lax.broadcasted_iota(jnp.int32, (1, CHUNK), 1)
    rows_at = lax.broadcasted_iota(jnp.int32, (CHUNK, CHUNK), 0)
    cols_at = lax.broadcasted_iota(jnp.int32, (CHUNK, CHUNK), 1)
    causal = (rows_at >= cols_at).astype(F32)

    def per_lane(values):
        row = jnp.zeros_like(values[0])
        for h, value in enumerate(values):
            row = jnp.where(lane == h, value, row)
        return row

    bias = per_lane([jnp.full((1, CHUNK), r.step_bias[h], F32) for h in range(heads)])
    rate = per_lane([jnp.exp(jnp.full((1, CHUNK), r.decay_log[h], F32)) for h in range(heads)])
    valid = lane < heads
    kernel = [
        jnp.concatenate([r.conv_inner[k : k + 1, :], r.conv_state[k : k + 1, :]], axis=1) for k in range(CONV)
    ]
    ends = []
    for k in range(chunks):
        raw = jnp.where(valid, r.stepraw[span(k), :], 0.0) + bias
        step = jnp.maximum(raw, 0.0) + jnp.log1p(jnp.exp(-jnp.abs(raw)))
        step = jnp.where(valid, step, 0.0)
        r.steps[span(k), :] = step
        cum = dot(causal, -step * rate, NN)
        r.cums[span(k), :] = cum
        turned = cum.T
        ends.append([cum[CHUNK - 1 :, h : h + 1] for h in range(heads)])
        for h in range(heads):
            spread = cum[:, h : h + 1] - turned[h : h + 1, :]
            r.decays[k, h] = jnp.exp(jnp.minimum(spread, 0.0)) * causal
    tick()

    @pl.when(ctx == 0)
    def _():
        r.ext[:HALO, :] = jnp.zeros((HALO, both), F32)

    @pl.when(ctx > 0)
    def _():
        halo.wait_recv()

    for k in range(chunks):
        blended = jnp.zeros((CHUNK, both), F32)
        for tap in range(CONV):
            start = k * CHUNK + HALO - (CONV - 1) + tap
            blended += kernel[tap] * r.ext[start : start + CHUNK, :]
        r.pre[span(k), :] = blended
        active = blended * jax.nn.sigmoid(blended)
        r.act[span(k), :] = active
        b_rows, c_rows = active[:, width : width + STATE], active[:, width + STATE :]
        r.cb[k] = dot(c_rows, b_rows, NT)
        for h in range(heads):
            lanes = slice(h * HEAD_DIM, (h + 1) * HEAD_DIM)
            fed = active[:, lanes] * r.steps[span(k), h : h + 1]
            r.xd[span(k), lanes] = fed
            left = jnp.exp(ends[k][h] - r.cums[span(k), h : h + 1])
            own = dot(fed * left, b_rows, TN)
            if k == 0:
                r.states[0, h] = jnp.zeros_like(own)
                r.states[1, h] = own
            else:
                r.states[k + 1, h] = jnp.exp(ends[k][h]) * r.states[k, h] + own
        if k % 3 == 2:
            tick()

    befores = [[jnp.zeros((1, 1), F32) for _ in range(heads)]]
    for k in range(chunks):
        befores.append([befores[k][h] + ends[k][h] for h in range(heads)])
    whole = [jnp.exp(befores[chunks][h]) for h in range(heads)]
    row8 = lax.broadcasted_iota(jnp.int32, (8, CHUNK), 0)
    factors = jnp.zeros((8, CHUNK), F32)
    for h in range(heads):
        r.fwd_out[h * HEAD_DIM : (h + 1) * HEAD_DIM, :] = r.states[chunks, h]
        factors = jnp.where(row8 == h, whole[h], factors)
    r.factors_out[...] = factors
    forward = Exchange(
        r.fwd_out, r.fwd_in, r.cross_out.at[0], r.cross_in.at[0], r.fwd_send, r.fwd_recv, r.factors_in, heads, True
    )
    forward.cross_sum = r.cross_sum
    factor_copies = [
        remote(
            "ctx", forward.peer(j), r.factors_out, r.factors_in.at[j - 1], r.factor_send.at[j - 1], r.factor_recv.at[j - 1]
        )
        for j in range(1, ROW)
    ]
    for copy in factor_copies:
        copy.start()
    forward.start()
    tick()

    for k in range(chunks):
        c_rows = r.act[span(k), width + STATE :]
        for h in range(heads):
            lanes = slice(h * HEAD_DIM, (h + 1) * HEAD_DIM)
            value = dot(r.decays[k, h] * r.cb[k], r.xd[span(k), lanes], NN)
            if k > 0:
                value += jnp.exp(r.cums[span(k), h : h + 1]) * dot(c_rows, r.states[k, h], NT)
            r.out[span(k), lanes] = value
        if k % 3 == 2:
            tick()

    for copy in factor_copies:
        copy.wait_recv()
    forward.give(r.entering, r.states.at[chunks], factors)
    tick()
    forward.take(r.entering)
    tick()
    for k in range(chunks):
        c_rows = r.act[span(k), width + STATE :]
        for h in range(heads):
            lanes = slice(h * HEAD_DIM, (h + 1) * HEAD_DIM)
            grown = jnp.exp(r.cums[span(k), h : h + 1] + befores[k][h])
            r.out[span(k), lanes] = r.out[span(k), lanes] + grown * dot(c_rows, r.entering[h], NT)
            r.states[k, h] = r.states[k, h] + jnp.exp(befores[k][h]) * r.entering[h]
        if k % 2 == 1:
            tick()
    for h in range(heads):
        r.states[chunks, h] = r.states[chunks, h] + whole[h] * r.entering[h]

    def drain():
        @pl.when(ctx < SHARDS - 1)
        def _():
            halo.wait_send()

        for copy in factor_copies:
            copy.wait_send()
        forward.drain()

    return SimpleNamespace(
        total=total, both=both, width=width, heads=heads, chunks=chunks, span=span, lane=lane, bias=bias, rate=rate,
        valid=valid, kernel=kernel, ends=ends, factors=factors, drain=drain, rows_at=rows_at, cols_at=cols_at,
    )


def token_sums(r, f):
    gain = r.gain[...]
    ones = jnp.ones((8, f.width), F32)
    for k in range(f.chunks):
        gate = r.gate[f.span(k), :].astype(F32)
        gated = r.out[f.span(k), :] * (gate * jax.nn.sigmoid(gate))
        squares = dot(ones, gated * gated, NT)
        crosses = dot(ones, gain * r.local[f.span(k), :] * gated, NT)
        r.tot_out[0, 0:1, f.span(k)] = squares[0:1, :]
        r.tot_out[0, 1:2, f.span(k)] = crosses[0:1, :]
    yh, z, core = place()
    copies = []

    def swap(phase, partners, base):
        mine = []
        for j, partner in enumerate(partners):
            slot = base + j
            copy = remote(
                "tp", partner, r.tot_out.at[phase], r.tot_in.at[slot], r.tot_send.at[slot], r.tot_recv.at[slot]
            )
            copy.start()
            mine.append(copy)
        sums = r.tot_out[phase]
        for j, copy in enumerate(mine):
            copy.wait_recv()
            sums = sums + r.tot_in[base + j]
        copies.extend(mine)
        return sums

    near = [tp_id(yh, z, 1 - core), tp_id(1 - yh, z, core), tp_id(1 - yh, z, 1 - core)]
    r.tot_out[1] = swap(0, near, 0)
    sums = swap(1, [tp_id(yh, z + j, core) for j in range(1, Z)], len(near))
    return sums, copies


def mixer_backward(r, f, sums):
    ctx = lax.axis_index("ctx")
    span, chunks, heads, width, total = f.span, f.chunks, f.heads, f.width, f.total
    channels = width * GROUP
    gain = r.gain[...]
    anti = (f.rows_at <= f.cols_at).astype(F32)
    ends = f.ends
    for k in range(chunks):
        held = jnp.concatenate([sums[:, span(k)], jnp.zeros((CHUNK - 2, CHUNK), F32)], axis=0).T
        inverse = lax.rsqrt(held[:, 0:1] / channels + EPSILON)
        pull = inverse * inverse * inverse * (held[:, 1:2] / channels)
        gate = r.gate[span(k), :].astype(F32)
        sigmoid = jax.nn.sigmoid(gate)
        opened = gate * sigmoid
        value = r.out[span(k), :]
        d_gated = inverse * (gain * r.local[span(k), :]) - value * opened * pull
        r.d_gate[span(k), :] = (d_gated * value * sigmoid * (1.0 + gate * (1.0 - sigmoid))).astype(BF16)
        r.dy[span(k), :] = d_gated * opened

    for k in range(chunks - 1, -1, -1):
        c_rows = r.act[span(k), width + STATE :]
        for h in range(heads):
            lanes = slice(h * HEAD_DIM, (h + 1) * HEAD_DIM)
            own = dot(r.dy[span(k), lanes] * jnp.exp(r.cums[span(k), h : h + 1]), c_rows, TN)
            if k < chunks - 1:
                own += jnp.exp(ends[k][h]) * r.d_states[k + 1, h]
            r.d_states[k, h] = own
    for h in range(heads):
        r.bwd_out[h * HEAD_DIM : (h + 1) * HEAD_DIM, :] = r.d_states[0, h]
    backward = Exchange(
        r.bwd_out, r.bwd_in, r.cross_out.at[1], r.cross_in.at[1], r.bwd_send, r.bwd_recv, r.factors_in, heads, False
    )
    backward.cross_sum = r.cross_sum
    backward.start()

    def local(k):
        b_rows, c_rows = r.act[span(k), width : width + STATE], r.act[span(k), width + STATE :]
        d_cb = jnp.zeros((CHUNK, CHUNK), F32)
        d_crows = jnp.zeros((CHUNK, STATE), F32)
        for h in range(heads):
            lanes = slice(h * HEAD_DIM, (h + 1) * HEAD_DIM)
            grad = r.dy[span(k), lanes]
            d_cb += r.decays[k, h] * dot(grad, r.xd[span(k), lanes], NT)
            r.u_loc[span(k), lanes] = dot(r.decays[k, h] * r.cb[k], grad, TN)
            d_crows += jnp.exp(r.cums[span(k), h : h + 1]) * dot(grad, r.states[k, h], NN)
        r.d_b[span(k), :] = dot(d_cb, c_rows, TN)
        r.d_c[span(k), :] = d_crows + dot(d_cb, b_rows, NN)

    for k in range(chunks // 2):
        local(k)
    backward.give(r.d_leaving, r.d_states.at[0], f.factors)
    for k in range(chunks // 2, chunks):
        local(k)
    backward.take(r.d_leaving)
    after = [jnp.zeros((1, 1), F32) for _ in range(heads)]
    for h in range(heads):
        r.d_states[chunks, h] = r.d_leaving[h]
    for k in range(chunks - 1, 0, -1):
        after = [after[h] + ends[k][h] for h in range(heads)]
        for h in range(heads):
            r.d_states[k, h] = r.d_states[k, h] + jnp.exp(after[h]) * r.d_leaving[h]

    halo = remote("ctx", lax.rem(ctx + SHARDS - 1, SHARDS), r.d_pre.at[:HALO, :], r.d_pre.at[total:, :], r.halo_sem.at[2], r.halo_sem.at[3])
    for k in range(chunks):
        b_rows = r.act[span(k), width : width + STATE]
        d_brows = r.d_b[span(k), :]
        d_acts = []
        pulls = jnp.zeros((CHUNK, CHUNK), F32)
        feeds = jnp.zeros((CHUNK, CHUNK), F32)
        edge = jnp.zeros((1, CHUNK), F32)
        for h in range(heads):
            lanes = slice(h * HEAD_DIM, (h + 1) * HEAD_DIM)
            step = r.steps[span(k), h : h + 1]
            left = jnp.exp(ends[k][h] - r.cums[span(k), h : h + 1])
            d_next = r.d_states[k + 1, h]
            grad = r.u_loc[span(k), lanes] + left * dot(b_rows, d_next, NT)
            d_brows += dot(r.xd[span(k), lanes] * left, d_next, NN)
            d_acts.append(grad * step)
            fed = jnp.sum(grad * r.act[span(k), lanes], axis=1, keepdims=True)
            met = jnp.sum(r.dy[span(k), lanes] * r.out[span(k), lanes], axis=1, keepdims=True)
            pulls = jnp.where(f.lane == h, met - step * fed, pulls)
            feeds = jnp.where(f.lane == h, fed, feeds)
            edge = jnp.where(f.lane == h, jnp.sum(d_next * r.states[k + 1, h]), edge)
        d_decay = dot(anti, pulls, NN) + edge
        raw = jnp.where(f.valid, r.stepraw[span(k), :], 0.0) + f.bias
        d_raw = (feeds - f.rate * d_decay) * jax.nn.sigmoid(raw)
        r.d_step[span(k), :] = d_raw[:, :heads].astype(BF16)
        d_act = jnp.concatenate(d_acts + [d_brows, r.d_c[span(k), :]], axis=1)
        value = r.pre[span(k), :]
        sigmoid = jax.nn.sigmoid(value)
        r.d_pre[span(k), :] = d_act * sigmoid * (1.0 + value * (1.0 - sigmoid))
        if k == 0:

            @pl.when(ctx > 0)
            def _():
                halo.start()

    @pl.when(ctx == SHARDS - 1)
    def _():
        r.d_pre[total:, :] = jnp.zeros((HALO, f.both), F32)

    @pl.when(ctx < SHARDS - 1)
    def _():
        halo.wait_recv()

    for k in range(chunks):
        blended = jnp.zeros((CHUNK, f.both), F32)
        for tap in range(CONV):
            start = k * CHUNK + CONV - 1 - tap
            blended += f.kernel[tap] * r.d_pre[start : start + CHUNK, :]
        r.d_inner[span(k), :] = blended[:, :width].astype(BF16)
        r.d_state[span(k), :] = blended[:, width:].astype(BF16)

    def drain():
        @pl.when(ctx > 0)
        def _():
            halo.wait_send()

        backward.drain()

    return drain


def whole_kernel(names, *refs):
    r = SimpleNamespace(**dict(zip(names, refs, strict=True)))
    loads = [
        pltpu.make_async_copy(src, dst, r.weight_sem.at[i])
        for i, (src, dst) in enumerate(
            ((r.inner_hbm, r.inner_w), (r.state_hbm, r.state_w), (r.out_hbm, r.out_w), (r.step_hbm, r.step_w))
        )
    ]
    for load in loads:
        load.start()
    yh, z, core = place()
    ctx = lax.axis_index("ctx")
    barrier = pltpu.get_barrier_semaphore()
    tp_partners = [tp_id(yh, z, 1 - core), tp_id(1 - yh, z, core), tp_id(1 - yh, z, 1 - core)]
    tp_partners += [tp_id(yh, z + j, core) for j in range(1, Z)]
    row = ctx // ROW * ROW
    ctx_partners = [row + lax.rem(ctx - row + j, ROW) for j in range(1, ROW)]
    ctx_partners += [lax.rem(ctx + j, SHARDS) for j in (ROW, 1, SHARDS - 1)]
    for axis, partners in (("tp", tp_partners), ("ctx", ctx_partners)):
        for partner in partners:
            pl.semaphore_signal(barrier, inc=1, device_id={axis: partner}, device_id_type=MESH)
    pl.semaphore_wait(barrier, len(tp_partners) + len(ctx_partners))

    first = Gather(r.rows, r.rows_all, r.swaps.at[0], r.send_r, r.recv_r)
    second = Gather(r.grads, r.grads_all, r.swaps.at[1], r.send_g, r.recv_g)
    first.first_swap()
    second.first_swap()
    first.begin()
    early, late = first.steps()[:-3], first.steps()[-3:]
    for step in early:
        step()
    second.begin()
    pending = second.steps()
    for step in late:
        step()
        pending.pop(0)()
    for load in loads:
        load.wait()
    first.finish()

    def tick():
        if pending:
            pending.pop(0)()

    total, tile = r.rows_all.shape[0], 128

    def project(dst, column, weight, source, contract):
        def tiles(low, high):
            def turn(i, carry):
                at = pl.ds(pl.multiple_of(i * tile, tile), tile)
                value = dot16(source[at, :], weight[...], contract)
                if dst.dtype == F32 and source is r.rows_all:
                    value = value.astype(BF16)
                dst[at, pl.ds(column, value.shape[1])] = value.astype(dst.dtype)
                return carry

            lax.fori_loop(low, high, turn, 0)

        tiles(0, total // tile // 2)
        tick()
        tiles(total // tile // 2, total // tile)
        tick()

    width = r.inner_w.shape[2]
    project(r.conv, 0, r.inner_w.at[1], r.rows_all, NN)
    project(r.conv, width, r.state_w, r.rows_all, NN)
    project(r.stepraw, 0, r.step_w, r.rows_all, NT)
    project(r.gate, 0, r.inner_w.at[0], r.rows_all, NN)
    f = mixer_forward(r, tick)
    while pending:
        tick()
    second.finish()
    project(r.local, 0, r.out_w, r.grads_all, NT)
    sums, total_copies = token_sums(r, f)
    drain = mixer_backward(r, f, sums)
    rows, depth = r.result.shape
    Scatter(r, rows, depth).run(r.result)
    f.drain()
    drain()
    for copy in total_copies:
        copy.wait_send()
    first.drain()
    second.drain()


def body(
    normed_rows,
    out_grad,
    inner_weight,
    state_weight,
    step_weight,
    conv_inner,
    conv_state,
    step_bias,
    decay_log,
    norm_gain,
    out_weight,
):
    count, depth = normed_rows.shape
    total = count * GROUP
    width, state_width = inner_weight.shape[2], state_weight.shape[1]
    both = width + state_width
    heads = width // HEAD_DIM
    chunks = total // CHUNK
    pair, half = 2 * count, depth // 2
    quarter = half // 2
    vmem = pl.BlockSpec(memory_space=pltpu.VMEM)
    smem = pl.BlockSpec(memory_space=pltpu.SMEM)
    anywhere = pl.BlockSpec(memory_space=pl.ANY)
    inputs = {
        "step_bias": (step_bias, smem),
        "decay_log": (decay_log, smem),
        "rows": (normed_rows, vmem),
        "grads": (out_grad, vmem),
        "conv_inner": (conv_inner, vmem),
        "conv_state": (conv_state, vmem),
        "gain": (norm_gain.reshape(1, -1), vmem),
        "inner_hbm": (inner_weight, anywhere),
        "state_hbm": (state_weight, anywhere),
        "out_hbm": (out_weight, anywhere),
        "step_hbm": (step_weight.T, anywhere),
    }
    state = (heads, HEAD_DIM, STATE)
    message = (heads * HEAD_DIM, STATE)
    scratch = {
        "rows_all": ((total, depth), BF16),
        "grads_all": ((total, depth), BF16),
        "swaps": ((2, count, half), BF16),
        "inner_w": (inner_weight.shape, BF16),
        "state_w": (state_weight.shape, BF16),
        "out_w": (out_weight.shape, BF16),
        "step_w": (step_weight.shape[::-1], BF16),
        "gate": ((total, width), BF16),
        "conv": ((total, both), BF16),
        "stepraw": ((total, CHUNK), F32),
        "local": ((total, width), F32),
        "ext": ((HALO + total, both), F32),
        "pre": ((total, both), F32),
        "act": ((total, both), F32),
        "xd": ((total, width), F32),
        "steps": ((total, CHUNK), F32),
        "cums": ((total, CHUNK), F32),
        "cb": ((chunks, CHUNK, CHUNK), F32),
        "decays": ((chunks, heads, CHUNK, CHUNK), F32),
        "out": ((total, width), F32),
        "dy": ((total, width), F32),
        "states": ((chunks + 1,) + state, F32),
        "d_states": ((chunks + 1,) + state, F32),
        "entering": (state, F32),
        "d_leaving": (state, F32),
        "fwd_out": (message, F32),
        "fwd_in": ((ROW - 1,) + message, F32),
        "bwd_out": (message, F32),
        "bwd_in": ((ROW - 1,) + message, F32),
        "cross_out": ((2,) + message, F32),
        "cross_in": ((2,) + message, F32),
        "cross_sum": (state, F32),
        "factors_out": ((8, CHUNK), F32),
        "factors_in": ((ROW - 1, 8, CHUNK), F32),
        "tot_out": ((2, 2, total), F32),
        "tot_in": ((3 + Z - 1, 2, total), F32),
        "d_pre": ((total + HALO, both), F32),
        "d_b": ((total, STATE), F32),
        "d_c": ((total, STATE), F32),
        "u_loc": ((total, width), F32),
        "d_gate": ((total, width), BF16),
        "d_inner": ((total, width), BF16),
        "d_state": ((total, state_width), BF16),
        "d_step": ((total, heads), BF16),
        "mine": ((Z, 2, pair, half), F32),
        "sib_out": ((Z, 2, pair, half), BF16),
        "sib_in": ((Z, 2, pair, half), BF16),
        "ring_out": ((30, pair, quarter), BF16),
        "ring_in": ((30, pair, quarter), BF16),
        "last_out": ((2, count, quarter), BF16),
        "last_in": ((2, count, quarter), BF16),
    }
    semaphores = {
        "weight_sem": 4,
        "send_r": 63,
        "recv_r": 63,
        "send_g": 63,
        "recv_g": 63,
        "halo_sem": 4,
        "factor_send": ROW - 1,
        "factor_recv": ROW - 1,
        "fwd_send": ROW,
        "fwd_recv": ROW,
        "bwd_send": ROW,
        "bwd_recv": ROW,
        "tot_send": 3 + Z - 1,
        "tot_recv": 3 + Z - 1,
        "sib_send": Z,
        "sib_recv": Z,
        "ring_send": 30,
        "ring_recv": 30,
        "last_send": 2,
        "last_recv": 2,
    }
    names = list(inputs) + ["result"] + list(scratch) + list(semaphores)
    return pl.pallas_call(
        functools.partial(whole_kernel, names),
        out_shape=jax.ShapeDtypeStruct((count, depth), BF16),
        in_specs=[spec for _, spec in inputs.values()],
        out_specs=vmem,
        scratch_shapes=[pltpu.VMEM(shape, dtype) for shape, dtype in scratch.values()]
        + [pltpu.SemaphoreType.DMA((n,)) for n in semaphores.values()],
        compiler_params=pltpu.CompilerParams(collective_id=0, has_side_effects=True, vmem_limit_bytes=VMEM_LIMIT),
        name="mixer_grad",
    )(*[value for value, _ in inputs.values()])


def solution(mesh):
    placed = (
        P(("ctx", "tp"), None),
        P(("ctx", "tp"), None),
        P(None, None, "tp"),
        P(),
        P(None, "tp"),
        P(None, "tp"),
        P(),
        P("tp"),
        P("tp"),
        P("tp"),
        P("tp", None),
    )
    return jax.shard_map(
        body, mesh=mesh, in_specs=placed, out_specs=P(("ctx", "tp"), None), check_vma=False
    )
```

```python
import functools
from types import SimpleNamespace

import jax
import jax.numpy as jnp
from jax import lax
from jax.experimental import pallas as pl
from jax.experimental.pallas import tpu as pltpu
from jax.sharding import PartitionSpec as P

HEAD_DIM = 128
STATE = 128
CONV = 4
EPSILON = 1e-05
EXACT = lax.Precision.HIGHEST
NEAR = lax.Precision.HIGH
MESH = pl.DeviceIdType.MESH
F32 = jnp.float32
BF16 = jnp.bfloat16
VMEM_LIMIT = 62 * 1024 * 1024

Z = 8
GROUP = 4 * Z
ROW = 4
SHARDS = 2 * ROW
CHUNK = 128
HALO = 8
NN, NT, TN = ((1,), (0,)), ((1,), (1,)), ((0,), (0,))


def place():
    tp = lax.axis_index("tp")
    return tp // (2 * Z), lax.rem(tp // 2, Z), lax.rem(tp, 2)


def tp_id(yh, z, core):
    return (yh * Z + lax.rem(z + Z, Z)) * 2 + core


def remote(axis, partner, src, dst, send_sem, recv_sem):
    return pltpu.make_async_remote_copy(
        src_ref=src,
        dst_ref=dst,
        send_sem=send_sem,
        recv_sem=recv_sem,
        device_id={axis: partner},
        device_id_type=MESH,
    )


def dot(a, b, contract, precision=NEAR):
    return lax.dot_general(a, b, (contract, ((), ())), precision=precision, preferred_element_type=F32)


def dot16(a, b, contract):
    return lax.dot_general(a, b, (contract, ((), ())), preferred_element_type=F32)


class Gather:
    def __init__(self, own_ref, buf, swap, send_sem, recv_sem):
        self.own_ref, self.buf, self.swap = own_ref, buf, swap
        self.send_sem, self.recv_sem = send_sem, recv_sem
        self.yh, self.z, self.core = place()
        self.pair = 2 * own_ref.shape[0]
        self.half = own_ref.shape[1] // 2
        self.sibling = tp_id(self.yh, self.z, 1 - self.core)
        self.started = []

    def block(self, h, dz, sub, core=None):
        yh = self.yh if h == 0 else 1 - self.yh
        chip = yh * Z + lax.rem(self.z + (dz + Z), Z)
        rows = pl.ds(pl.multiple_of(chip * self.pair, 16), self.pair)
        quarter = self.half // 2
        at = (self.core if core is None else core) * self.half + sub * quarter
        return self.buf.at[rows, pl.ds(pl.multiple_of(at, quarter), quarter)]

    def copy(self, slot, src, dst, partner):
        return remote("tp", partner, src, dst, self.send_sem.at[slot], self.recv_sem.at[slot])

    def send(self, slot, src, dst, partner):
        copy = self.copy(slot, src, dst, partner)
        copy.start()
        self.started.append(copy)

    def got(self, slot, block):
        self.copy(slot, block, block, self.sibling).wait_recv()

    def across(self, sub, d):
        here = self.block(0, (1 - 2 * sub) * d, sub)
        self.send(sub * 31 + d, here, here, tp_id(1 - self.yh, self.z, self.core))

    def along(self, kind, sub, d):
        way = 1 - 2 * sub
        if kind == "long":
            here = self.block(0, way * (d - 1), sub)
            self.send(sub * 31 + 4 + d, here, here, tp_id(self.yh, self.z - way, self.core))
        elif kind == "short":
            here = self.block(0, -way * (d - 1), sub)
            self.send(sub * 31 + 9 + d, here, here, tp_id(self.yh, self.z + way, self.core))
        else:
            here = self.block(1, -way * (d - 1), sub)
            self.send(sub * 31 + 11 + d, here, here, tp_id(self.yh, self.z + way, self.core))

    def sibling_slot(self, h, dz, sub):
        return sub * 31 + 15 + h * 8 + dz % 8

    def to_sibling(self, h, dz, sub):
        here = self.block(h, dz, sub)
        self.send(self.sibling_slot(h, dz, sub), here, here, self.sibling)

    def first_swap(self):
        columns = pl.ds(pl.multiple_of((1 - self.core) * self.half, self.half), self.half)
        self.send(62, self.own_ref.at[:, columns], self.swap, self.sibling)

    def begin(self):
        self.got(62, self.swap)
        columns = pl.ds(pl.multiple_of(self.core * self.half, self.half), self.half)
        mine = self.own_ref[:, columns].astype(F32)
        other = self.swap[...].astype(F32)
        first = self.core == 0
        both = jnp.concatenate([jnp.where(first, mine, other), jnp.where(first, other, mine)], axis=0)
        quarter = self.half // 2
        for sub in (0, 1):
            self.block(0, 0, sub)[...] = both[:, sub * quarter : (sub + 1) * quarter].astype(BF16)
        for sub in (0, 1):
            self.along("long", sub, 1)
            self.across(sub, 0)
            self.along("short", sub, 1)
            self.to_sibling(0, 0, sub)

    def long(self, d):
        for sub in (0, 1):
            dz = (1 - 2 * sub) * d
            self.got(sub * 31 + 4 + d, self.block(0, dz, sub))
            if d < 5:
                self.along("long", sub, d + 1)
                self.across(sub, d)
            self.to_sibling(0, dz, sub)

    def short(self, d):
        for sub in (0, 1):
            dz = -(1 - 2 * sub) * d
            self.got(sub * 31 + 9 + d, self.block(0, dz, sub))
            if d < 2:
                self.along("short", sub, d + 1)
            self.to_sibling(0, dz, sub)

    def met(self, d):
        for sub in (0, 1):
            dz = (1 - 2 * sub) * d
            self.got(sub * 31 + d, self.block(1, dz, sub))
            if d == 0:
                self.along("other", sub, 1)
            self.to_sibling(1, dz, sub)

    def other(self, d):
        for sub in (0, 1):
            dz = -(1 - 2 * sub) * d
            self.got(sub * 31 + 11 + d, self.block(1, dz, sub))
            if d < 3:
                self.along("other", sub, d + 1)
            self.to_sibling(1, dz, sub)

    def steps(self):
        order = [
            (self.long, 1), (self.short, 1), (self.met, 0), (self.long, 2), (self.short, 2), (self.met, 1),
            (self.other, 1), (self.long, 3), (self.met, 2), (self.other, 2), (self.long, 4), (self.met, 3),
            (self.other, 3), (self.long, 5), (self.met, 4),
        ]
        return [functools.partial(step, d) for step, d in order]

    def finish(self):
        for sub in (0, 1):
            for h in (0, 1):
                for dz in range(8):
                    self.got(self.sibling_slot(h, dz, sub), self.block(h, dz, sub, 1 - self.core))

    def drain(self):
        for copy in self.started:
            copy.wait_send()


class Scatter:
    order = (-3, 3, -4, 2, -2, 1, -1, 0)

    def __init__(self, r, rows, depth):
        self.r = r
        self.yh, self.z, self.core = place()
        self.sibling = tp_id(self.yh, self.z, 1 - self.core)
        self.rows, self.pair, self.half = rows, 2 * rows, depth // 2
        self.quarter = self.half // 2
        self.tile = 512
        self.started = []

    def at(self, dz):
        return self.order.index(dz if dz < 4 and dz > -4 else -4 if abs(dz) == 4 else dz - 8 if dz > 0 else dz + 8)

    def start(self, copy):
        copy.start()
        self.started.append(copy)

    def product(self, dz):
        r, at, half, tile = self.r, self.at(dz), self.half, self.tile
        zt = lax.rem(self.z + (dz + Z), Z)
        spots = []
        for h in (0, 1):
            yt = self.yh if h == 0 else 1 - self.yh
            spots.append(pl.ds(pl.multiple_of((yt * Z + zt) * self.pair, 16), self.pair))

        parts = []
        for ref in (r.d_gate, r.d_inner, r.d_state, r.d_step):
            parts.append(jnp.concatenate([ref[spots[0], :], ref[spots[1], :]], axis=0))

        def side(which, keep):
            def turn(j, carry):
                here = pl.ds(pl.multiple_of(j * tile, tile), tile)
                cols = pl.ds(pl.multiple_of(which * half + j * tile, tile), tile)
                value = dot16(parts[3], r.step_w[:, cols], NN)
                for i in range(3):
                    width = parts[i].shape[1]
                    value += dot16(parts[i], r.rows_all[i * width : (i + 1) * width, cols], NN)
                for h in (0, 1):
                    keep[at, h, :, here] = value[h * self.pair : (h + 1) * self.pair].astype(keep.dtype)
                return carry

            lax.fori_loop(0, half // tile, turn, 0)

        side(1 - self.core, r.sib_out)
        self.start(
            remote("tp", self.sibling, r.sib_out.at[at], r.sib_in.at[at], r.sib_send.at[at], r.sib_recv.at[at])
        )
        side(self.core, r.mine)

    def sib_got(self, dz):
        at, r = self.at(dz), self.r
        there = r.sib_in.at[at]
        remote("tp", self.sibling, there, there, r.sib_send.at[at], r.sib_recv.at[at]).wait_recv()

    def got(self, slot):
        there = self.r.ring_in.at[slot]
        remote("tp", self.sibling, there, there, self.r.ring_send.at[slot], self.r.ring_recv.at[slot]).wait_recv()

    def slot(self, kind, sub, d):
        return sub * 15 + {"y": 0, "long": 4, "short": 9, "other": 11}[kind] + d

    def value(self, h, dz, sub, slots, columns):
        at, r = self.at(dz), self.r
        here = pl.ds(pl.multiple_of(sub * self.quarter + columns, self.tile), self.tile)
        there = pl.ds(pl.multiple_of(columns, self.tile), self.tile)
        total = r.mine[at, h, :, here] + r.sib_in[at, h, :, here].astype(F32)
        for slot in slots:
            total += r.ring_in[slot, :, there].astype(F32)
        return total

    def message(self, kind, sub, d):
        way = 1 - 2 * sub
        earlier = []
        if kind == "y":
            h, dz, partner = 1, way * d, tp_id(1 - self.yh, self.z, self.core)
            if d == 0:
                earlier.append(self.slot("other", sub, 1))
        elif kind == "long":
            h, dz, partner = 0, way * d, tp_id(self.yh, self.z + way, self.core)
            if d < 5:
                earlier += [self.slot("long", sub, d + 1), self.slot("y", sub, d)]
        elif kind == "short":
            h, dz, partner = 0, -way * d, tp_id(self.yh, self.z - way, self.core)
            if d < 2:
                earlier.append(self.slot("short", sub, d + 1))
        else:
            h, dz, partner = 1, -way * d, tp_id(self.yh, self.z - way, self.core)
            if d < 3:
                earlier.append(self.slot("other", sub, d + 1))
        for slot in earlier:
            self.got(slot)
        slot, r = self.slot(kind, sub, d), self.r

        def turn(j, carry):
            columns = j * self.tile
            there = pl.ds(pl.multiple_of(columns, self.tile), self.tile)
            r.ring_out[slot, :, there] = self.value(h, dz, sub, earlier, columns).astype(BF16)
            return carry

        lax.fori_loop(0, self.quarter // self.tile, turn, 0)
        self.start(
            remote("tp", partner, r.ring_out.at[slot], r.ring_in.at[slot], r.ring_send.at[slot], r.ring_recv.at[slot])
        )

    def run(self, out_ref):
        r, core, half = self.r, self.core, self.half

        def both(kind, d):
            for sub in (0, 1):
                self.message(kind, sub, d)

        self.product(-3)
        self.product(3)
        self.sib_got(-3)
        self.message("long", 0, 5)
        self.message("other", 0, 3)
        self.message("y", 1, 3)
        self.product(-4)
        self.sib_got(3)
        self.message("long", 1, 5)
        self.message("other", 1, 3)
        self.message("y", 0, 3)
        self.product(2)
        self.sib_got(-4)
        both("y", 4)
        self.product(-2)
        both("long", 4)
        self.sib_got(2)
        self.message("short", 1, 2)
        self.message("y", 0, 2)
        self.sib_got(-2)
        self.message("short", 0, 2)
        self.message("y", 1, 2)
        self.product(1)
        both("other", 2)
        both("long", 3)
        self.product(-1)
        self.sib_got(1)
        self.sib_got(-1)
        both("y", 1)
        both("other", 1)
        both("short", 1)
        self.product(0)
        both("long", 2)
        self.sib_got(0)
        both("y", 0)
        both("long", 1)
        first = core == 0
        for sub in (0, 1):
            earlier = [self.slot(*key) for key in (("short", sub, 1), ("y", sub, 0), ("long", sub, 1))]
            for slot in earlier:
                self.got(slot)

            def final(j, carry, sub=sub, earlier=earlier):
                columns = j * self.tile
                value = self.value(0, 0, sub, earlier, columns)
                low, high = value[: self.rows], value[self.rows :]
                at = sub * self.quarter + columns
                here = pl.ds(pl.multiple_of(core * half + at, self.tile), self.tile)
                out_ref[:, here] = jnp.where(first, low, high).astype(BF16)
                there = pl.ds(pl.multiple_of(columns, self.tile), self.tile)
                r.last_out[sub, :, there] = jnp.where(first, high, low).astype(BF16)
                return carry

            lax.fori_loop(0, self.quarter // self.tile, final, 0)
            self.start(
                remote(
                    "tp", self.sibling, r.last_out.at[sub], r.last_in.at[sub], r.last_send.at[sub], r.last_recv.at[sub]
                )
            )
        for sub in (0, 1):
            there = r.last_in.at[sub]
            remote("tp", self.sibling, there, there, r.last_send.at[sub], r.last_recv.at[sub]).wait_recv()
            at = (1 - core) * half + sub * self.quarter
            out_ref[:, pl.ds(pl.multiple_of(at, self.quarter), self.quarter)] = r.last_in[sub]
        for copy in self.started:
            copy.wait_send()


class Turned:
    def __init__(self, r):
        self.r = r
        self.size = r.stage.shape[1]
        self.blocks = r.step_w.shape[1] // self.size
        self.todo = [functools.partial(self.out_block, j) for j in range(self.blocks)]
        self.copies = []
        for i, ref in enumerate((r.inner_w.at[0], r.inner_w.at[1], r.state_w)):
            self.todo += [functools.partial(self.block, i, ref, j) for j in range(self.blocks)]

    def span(self, j):
        return slice(j * self.size, (j + 1) * self.size)

    def out_load(self, j):
        r = self.r
        return pltpu.make_async_copy(r.out_hbm.at[:, self.span(j)], r.stage.at[j % 2], r.stage_sem.at[j % 2])

    def begin(self):
        for j in (0, 1):
            self.out_load(j).start()

    def out_block(self, j):
        self.out_load(j).wait()
        self.r.out_t[self.span(j), :] = self.r.stage[j % 2].T
        if j + 2 < self.blocks:
            self.out_load(j + 2).start()

    def block(self, i, ref, j):
        slot = len(self.copies) % 4
        if len(self.copies) >= 4:
            self.copies[-4].wait()
        self.r.stage[2 + slot] = ref[self.span(j), :].T
        copy = pltpu.make_async_copy(
            self.r.stage.at[2 + slot], self.r.turned_hbm.at[i, :, self.span(j)], self.r.stage_sem.at[2 + slot]
        )
        copy.start()
        self.copies.append(copy)

    def some(self, count):
        for _ in range(count):
            if self.todo:
                self.todo.pop(0)()

    def finish(self):
        self.some(len(self.todo))
        for copy in self.copies[-4:]:
            copy.wait()

    def back(self):
        width = self.r.inner_w.shape[2]
        loads = [
            pltpu.make_async_copy(
                self.r.turned_hbm.at[i], self.r.rows_all.at[i * width : (i + 1) * width, :], self.r.back_sem.at[i]
            )
            for i in range(3)
        ]
        for load in loads:
            load.start()
        return loads


class Exchange:
    def __init__(self, out, into, cross_out, cross_in, send_sem, recv_sem, factors_in, heads, forward):
        self.ctx = lax.axis_index("ctx")
        self.x, self.y = lax.rem(self.ctx, ROW), self.ctx // ROW
        self.out, self.into, self.heads, self.forward = out, into, heads, forward
        self.factors_in, self.cross_out, self.cross_in = factors_in, cross_out, cross_in
        self.gives = self.y == (0 if forward else 1)
        self.copies = [
            remote("ctx", self.peer(j), out, into.at[j - 1], send_sem.at[j - 1], recv_sem.at[j - 1])
            for j in range(1, ROW)
        ]
        self.cross = remote(
            "ctx", lax.rem(self.ctx + ROW, SHARDS), cross_out, cross_in, send_sem.at[ROW - 1], recv_sem.at[ROW - 1]
        )

    def peer(self, j):
        return self.y * ROW + lax.rem(self.x + j, ROW)

    def start(self):
        for copy in self.copies:
            copy.start()

    def step(self, value, slot):
        parts = []
        for h in range(self.heads):
            state = self.into[slot, h * HEAD_DIM : (h + 1) * HEAD_DIM, :].astype(F32)
            parts.append(value[h] * self.factors_in[slot, h : h + 1, :] + state)
        return parts

    def chain(self, total):
        for j in range(ROW - 1, 0, -1):
            there = self.x >= j if self.forward else self.x + j < ROW
            slot = j - 1 if self.forward else ROW - 1 - j

            @pl.when(there)
            def _(slot=slot):
                for h, part in enumerate(self.step([total[h] for h in range(self.heads)], slot)):
                    total[h] = part

    def give(self, total, own, factors):
        for copy in self.copies:
            copy.wait_recv()

        @pl.when(self.gives)
        def _():
            total[...] = jnp.zeros_like(total)
            self.chain(total)
            for h in range(self.heads):
                self.cross_sum[h] = total[h] * factors[h : h + 1, :] + own[h]
            for j in range(1, ROW):
                there = self.x + j < ROW if self.forward else self.x >= j
                slot = ROW - 1 - j if self.forward else j - 1

                @pl.when(there)
                def _(slot=slot):
                    for h, part in enumerate(self.step([self.cross_sum[h] for h in range(self.heads)], slot)):
                        self.cross_sum[h] = part

            for h in range(self.heads):
                self.cross_out[h * HEAD_DIM : (h + 1) * HEAD_DIM, :] = self.cross_sum[h]
            self.cross.start()

    def take(self, total):
        @pl.when(jnp.logical_not(self.gives))
        def _():
            self.cross.wait_recv()
            for h in range(self.heads):
                total[h] = self.cross_in[h * HEAD_DIM : (h + 1) * HEAD_DIM, :].astype(F32)
            self.chain(total)

    def drain(self):
        for copy in self.copies:
            copy.wait_send()

        @pl.when(self.gives)
        def _():
            self.cross.wait_send()


def mixer_forward(r, tick):
    ctx = lax.axis_index("ctx")
    total, both = r.conv.shape
    width = both - 2 * STATE
    heads = width // HEAD_DIM
    chunks = total // CHUNK
    span = lambda k: slice(k * CHUNK, (k + 1) * CHUNK)
    r.ext[HALO:, :] = r.conv[...].astype(F32)
    halo = remote("ctx", lax.rem(ctx + 1, SHARDS), r.ext.at[total:, :], r.ext.at[:HALO, :], r.halo_sem.at[0], r.halo_sem.at[1])

    @pl.when(ctx < SHARDS - 1)
    def _():
        halo.start()

    lane = lax.broadcasted_iota(jnp.int32, (1, CHUNK), 1)
    rows_at = lax.broadcasted_iota(jnp.int32, (CHUNK, CHUNK), 0)
    cols_at = lax.broadcasted_iota(jnp.int32, (CHUNK, CHUNK), 1)
    causal = (rows_at >= cols_at).astype(F32)

    def per_lane(values):
        row = jnp.zeros_like(values[0])
        for h, value in enumerate(values):
            row = jnp.where(lane == h, value, row)
        return row

    bias = per_lane([jnp.full((1, CHUNK), r.step_bias[h], F32) for h in range(heads)])
    rate = per_lane([jnp.exp(jnp.full((1, CHUNK), r.decay_log[h], F32)) for h in range(heads)])
    valid = lane < heads
    kernel = [
        jnp.concatenate([r.conv_inner[k : k + 1, :], r.conv_state[k : k + 1, :]], axis=1) for k in range(CONV)
    ]
    ends = []
    for k in range(chunks):
        raw = jnp.where(valid, r.stepraw[span(k), :], 0.0) + bias
        step = jnp.maximum(raw, 0.0) + jnp.log1p(jnp.exp(-jnp.abs(raw)))
        step = jnp.where(valid, step, 0.0)
        r.steps[span(k), :] = step
        cum = dot(causal, -step * rate, NN, EXACT)
        r.cums[span(k), :] = cum
        turned = cum.T
        ends.append([cum[CHUNK - 1 :, h : h + 1] for h in range(heads)])
        for h in range(heads):
            spread = cum[:, h : h + 1] - turned[h : h + 1, :]
            r.decays[k, h] = jnp.exp(jnp.minimum(spread, 0.0)) * causal
    tick()

    @pl.when(ctx == 0)
    def _():
        r.ext[:HALO, :] = jnp.zeros((HALO, both), F32)

    @pl.when(ctx > 0)
    def _():
        halo.wait_recv()

    for k in range(chunks):
        blended = jnp.zeros((CHUNK, both), F32)
        for tap in range(CONV):
            start = k * CHUNK + HALO - (CONV - 1) + tap
            blended += kernel[tap] * r.ext[start : start + CHUNK, :]
        r.pre[span(k), :] = blended
        active = blended * jax.nn.sigmoid(blended)
        r.act[span(k), :] = active
        b_rows, c_rows = active[:, width : width + STATE], active[:, width + STATE :]
        r.cb[k] = dot(c_rows, b_rows, NT)
        for h in range(heads):
            lanes = slice(h * HEAD_DIM, (h + 1) * HEAD_DIM)
            fed = active[:, lanes] * r.steps[span(k), h : h + 1]
            r.xd[span(k), lanes] = fed
            left = jnp.exp(ends[k][h] - r.cums[span(k), h : h + 1])
            own = dot(fed * left, b_rows, TN)
            if k == 0:
                r.states[0, h] = jnp.zeros_like(own)
                r.states[1, h] = own
            else:
                r.states[k + 1, h] = jnp.exp(ends[k][h]) * r.states[k, h] + own
        if k % 3 == 2:
            tick()

    befores = [[jnp.zeros((1, 1), F32) for _ in range(heads)]]
    for k in range(chunks):
        befores.append([befores[k][h] + ends[k][h] for h in range(heads)])
    whole = [jnp.exp(befores[chunks][h]) for h in range(heads)]
    row8 = lax.broadcasted_iota(jnp.int32, (8, CHUNK), 0)
    factors = jnp.zeros((8, CHUNK), F32)
    for h in range(heads):
        r.fwd_out[h * HEAD_DIM : (h + 1) * HEAD_DIM, :] = r.states[chunks, h]
        factors = jnp.where(row8 == h, whole[h], factors)
    r.factors_out[...] = factors
    forward = Exchange(
        r.fwd_out, r.fwd_in, r.cross_out.at[0], r.cross_in.at[0], r.fwd_send, r.fwd_recv, r.factors_in, heads, True
    )
    forward.cross_sum = r.cross_sum
    factor_copies = [
        remote(
            "ctx", forward.peer(j), r.factors_out, r.factors_in.at[j - 1], r.factor_send.at[j - 1], r.factor_recv.at[j - 1]
        )
        for j in range(1, ROW)
    ]
    for copy in factor_copies:
        copy.start()
    forward.start()
    tick()

    for k in range(chunks):
        c_rows = r.act[span(k), width + STATE :]
        for h in range(heads):
            lanes = slice(h * HEAD_DIM, (h + 1) * HEAD_DIM)
            value = dot(r.decays[k, h] * r.cb[k], r.xd[span(k), lanes], NN)
            if k > 0:
                value += jnp.exp(r.cums[span(k), h : h + 1]) * dot(c_rows, r.states[k, h], NT)
            r.out[span(k), lanes] = value
        if k % 3 == 2:
            tick()

    for copy in factor_copies:
        copy.wait_recv()
    forward.give(r.entering, r.states.at[chunks], factors)
    tick()
    forward.take(r.entering)
    tick()
    for k in range(chunks):
        c_rows = r.act[span(k), width + STATE :]
        for h in range(heads):
            lanes = slice(h * HEAD_DIM, (h + 1) * HEAD_DIM)
            grown = jnp.exp(r.cums[span(k), h : h + 1] + befores[k][h])
            r.out[span(k), lanes] = r.out[span(k), lanes] + grown * dot(c_rows, r.entering[h], NT)
            r.states[k, h] = r.states[k, h] + jnp.exp(befores[k][h]) * r.entering[h]
        if k % 2 == 1:
            tick()
    for h in range(heads):
        r.states[chunks, h] = r.states[chunks, h] + whole[h] * r.entering[h]

    def drain():
        @pl.when(ctx < SHARDS - 1)
        def _():
            halo.wait_send()

        for copy in factor_copies:
            copy.wait_send()
        forward.drain()

    return SimpleNamespace(
        total=total, both=both, width=width, heads=heads, chunks=chunks, span=span, lane=lane, bias=bias, rate=rate,
        valid=valid, kernel=kernel, ends=ends, factors=factors, drain=drain, rows_at=rows_at, cols_at=cols_at,
    )


def token_sums(r, f):
    gain = r.gain[...]
    ones = jnp.ones((8, f.width), F32)
    for k in range(f.chunks):
        gate = r.gate[f.span(k), :].astype(F32)
        gated = r.out[f.span(k), :] * (gate * jax.nn.sigmoid(gate))
        squares = dot(ones, gated * gated, NT)
        crosses = dot(ones, gain * r.local[f.span(k), :] * gated, NT)
        r.tot_out[0, 0:1, f.span(k)] = squares[0:1, :]
        r.tot_out[0, 1:2, f.span(k)] = crosses[0:1, :]
    yh, z, core = place()
    copies = []

    def swap(phase, partners, base):
        mine = []
        for j, partner in enumerate(partners):
            slot = base + j
            copy = remote(
                "tp", partner, r.tot_out.at[phase], r.tot_in.at[slot], r.tot_send.at[slot], r.tot_recv.at[slot]
            )
            copy.start()
            mine.append(copy)
        sums = r.tot_out[phase]
        for j, copy in enumerate(mine):
            copy.wait_recv()
            sums = sums + r.tot_in[base + j]
        copies.extend(mine)
        return sums

    near = [tp_id(yh, z, 1 - core), tp_id(1 - yh, z, core), tp_id(1 - yh, z, 1 - core)]
    r.tot_out[1] = swap(0, near, 0)
    sums = swap(1, [tp_id(yh, z + j, core) for j in range(1, Z)], len(near))
    return sums, copies


def mixer_backward(r, f, sums):
    ctx = lax.axis_index("ctx")
    span, chunks, heads, width, total = f.span, f.chunks, f.heads, f.width, f.total
    channels = width * GROUP
    gain = r.gain[...]
    anti = (f.rows_at <= f.cols_at).astype(F32)
    ends = f.ends
    for k in range(chunks):
        held = jnp.concatenate([sums[:, span(k)], jnp.zeros((CHUNK - 2, CHUNK), F32)], axis=0).T
        inverse = lax.rsqrt(held[:, 0:1] / channels + EPSILON)
        pull = inverse * inverse * inverse * (held[:, 1:2] / channels)
        gate = r.gate[span(k), :].astype(F32)
        sigmoid = jax.nn.sigmoid(gate)
        opened = gate * sigmoid
        value = r.out[span(k), :]
        d_gated = inverse * (gain * r.local[span(k), :]) - value * opened * pull
        r.d_gate[span(k), :] = (d_gated * value * sigmoid * (1.0 + gate * (1.0 - sigmoid))).astype(BF16)
        r.dy[span(k), :] = d_gated * opened

    for k in range(chunks - 1, -1, -1):
        c_rows = r.act[span(k), width + STATE :]
        for h in range(heads):
            lanes = slice(h * HEAD_DIM, (h + 1) * HEAD_DIM)
            own = dot(r.dy[span(k), lanes] * jnp.exp(r.cums[span(k), h : h + 1]), c_rows, TN)
            if k < chunks - 1:
                own += jnp.exp(ends[k][h]) * r.d_states[k + 1, h]
            r.d_states[k, h] = own
    for h in range(heads):
        r.bwd_out[h * HEAD_DIM : (h + 1) * HEAD_DIM, :] = r.d_states[0, h]
    backward = Exchange(
        r.bwd_out, r.bwd_in, r.cross_out.at[1], r.cross_in.at[1], r.bwd_send, r.bwd_recv, r.factors_in, heads, False
    )
    backward.cross_sum = r.cross_sum
    backward.start()

    def local(k):
        b_rows, c_rows = r.act[span(k), width : width + STATE], r.act[span(k), width + STATE :]
        d_cb = jnp.zeros((CHUNK, CHUNK), F32)
        d_crows = jnp.zeros((CHUNK, STATE), F32)
        for h in range(heads):
            lanes = slice(h * HEAD_DIM, (h + 1) * HEAD_DIM)
            grad = r.dy[span(k), lanes]
            d_cb += r.decays[k, h] * dot(grad, r.xd[span(k), lanes], NT)
            r.u_loc[span(k), lanes] = dot(r.decays[k, h] * r.cb[k], grad, TN)
            d_crows += jnp.exp(r.cums[span(k), h : h + 1]) * dot(grad, r.states[k, h], NN)
        r.d_b[span(k), :] = dot(d_cb, c_rows, TN)
        r.d_c[span(k), :] = d_crows + dot(d_cb, b_rows, NN)

    for k in range(chunks // 2):
        local(k)
    backward.give(r.d_leaving, r.d_states.at[0], f.factors)
    for k in range(chunks // 2, chunks):
        local(k)
    backward.take(r.d_leaving)
    after = [jnp.zeros((1, 1), F32) for _ in range(heads)]
    for h in range(heads):
        r.d_states[chunks, h] = r.d_leaving[h]
    for k in range(chunks - 1, 0, -1):
        after = [after[h] + ends[k][h] for h in range(heads)]
        for h in range(heads):
            r.d_states[k, h] = r.d_states[k, h] + jnp.exp(after[h]) * r.d_leaving[h]

    halo = remote("ctx", lax.rem(ctx + SHARDS - 1, SHARDS), r.d_pre.at[:HALO, :], r.d_pre.at[total:, :], r.halo_sem.at[2], r.halo_sem.at[3])
    for k in range(chunks):
        b_rows = r.act[span(k), width : width + STATE]
        d_brows = r.d_b[span(k), :]
        d_acts = []
        pulls = jnp.zeros((CHUNK, CHUNK), F32)
        feeds = jnp.zeros((CHUNK, CHUNK), F32)
        edge = jnp.zeros((1, CHUNK), F32)
        for h in range(heads):
            lanes = slice(h * HEAD_DIM, (h + 1) * HEAD_DIM)
            step = r.steps[span(k), h : h + 1]
            left = jnp.exp(ends[k][h] - r.cums[span(k), h : h + 1])
            d_next = r.d_states[k + 1, h]
            grad = r.u_loc[span(k), lanes] + left * dot(b_rows, d_next, NT)
            d_brows += dot(r.xd[span(k), lanes] * left, d_next, NN)
            d_acts.append(grad * step)
            fed = jnp.sum(grad * r.act[span(k), lanes], axis=1, keepdims=True)
            met = jnp.sum(r.dy[span(k), lanes] * r.out[span(k), lanes], axis=1, keepdims=True)
            pulls = jnp.where(f.lane == h, met - step * fed, pulls)
            feeds = jnp.where(f.lane == h, fed, feeds)
            edge = jnp.where(f.lane == h, jnp.sum(d_next * r.states[k + 1, h]), edge)
        d_decay = dot(anti, pulls, NN, EXACT) + edge
        raw = jnp.where(f.valid, r.stepraw[span(k), :], 0.0) + f.bias
        d_raw = (feeds - f.rate * d_decay) * jax.nn.sigmoid(raw)
        r.d_step[span(k), :] = d_raw[:, :heads].astype(BF16)
        d_act = jnp.concatenate(d_acts + [d_brows, r.d_c[span(k), :]], axis=1)
        value = r.pre[span(k), :]
        sigmoid = jax.nn.sigmoid(value)
        r.d_pre[span(k), :] = d_act * sigmoid * (1.0 + value * (1.0 - sigmoid))
        if k == 0:

            @pl.when(ctx > 0)
            def _():
                halo.start()

    @pl.when(ctx == SHARDS - 1)
    def _():
        r.d_pre[total:, :] = jnp.zeros((HALO, f.both), F32)

    @pl.when(ctx < SHARDS - 1)
    def _():
        halo.wait_recv()

    for k in range(chunks):
        blended = jnp.zeros((CHUNK, f.both), F32)
        for tap in range(CONV):
            start = k * CHUNK + CONV - 1 - tap
            blended += f.kernel[tap] * r.d_pre[start : start + CHUNK, :]
        r.d_inner[span(k), :] = blended[:, :width].astype(BF16)
        r.d_state[span(k), :] = blended[:, width:].astype(BF16)

    def drain():
        @pl.when(ctx > 0)
        def _():
            halo.wait_send()

        backward.drain()

    return drain


def whole_kernel(names, *refs):
    r = SimpleNamespace(**dict(zip(names, refs, strict=True)))
    loads = [
        pltpu.make_async_copy(src, dst, r.weight_sem.at[i])
        for i, (src, dst) in enumerate(
            ((r.inner_hbm, r.inner_w), (r.state_hbm, r.state_w), (r.step_hbm, r.step_w))
        )
    ]
    for load in loads:
        load.start()
    turned = Turned(r)
    turned.begin()
    yh, z, core = place()
    ctx = lax.axis_index("ctx")
    barrier = pltpu.get_barrier_semaphore()
    tp_partners = [tp_id(yh, z, 1 - core), tp_id(1 - yh, z, core), tp_id(1 - yh, z, 1 - core)]
    tp_partners += [tp_id(yh, z + j, core) for j in range(1, Z)]
    row = ctx // ROW * ROW
    ctx_partners = [row + lax.rem(ctx - row + j, ROW) for j in range(1, ROW)]
    ctx_partners += [lax.rem(ctx + j, SHARDS) for j in (ROW, 1, SHARDS - 1)]
    for axis, partners in (("tp", tp_partners), ("ctx", ctx_partners)):
        for partner in partners:
            pl.semaphore_signal(barrier, inc=1, device_id={axis: partner}, device_id_type=MESH)
    pl.semaphore_wait(barrier, len(tp_partners) + len(ctx_partners))

    first = Gather(r.rows, r.rows_all, r.swaps.at[0], r.send_r, r.recv_r)
    second = Gather(r.grads, r.grads_all, r.swaps.at[1], r.send_g, r.recv_g)
    first.first_swap()
    second.first_swap()
    first.begin()
    early, late = first.steps()[:-3], first.steps()[-3:]
    turned.some(6)
    for load in loads:
        load.wait()
    for step in early:
        step()
        turned.some(4)
    second.begin()
    pending = second.steps()
    for step in late:
        step()
        pending.pop(0)()
    turned.finish()
    first.finish()

    def tick():
        if pending:
            pending.pop(0)()

    total, tile = r.rows_all.shape[0], 128

    def project(dst, column, weight, source, contract):
        def tiles(low, high):
            def turn(i, carry):
                at = pl.ds(pl.multiple_of(i * tile, tile), tile)
                value = dot16(source[at, :], weight[...], contract)
                if dst.dtype == F32 and source is r.rows_all:
                    value = value.astype(BF16)
                dst[at, pl.ds(column, value.shape[1])] = value.astype(dst.dtype)
                return carry

            lax.fori_loop(low, high, turn, 0)

        tiles(0, total // tile // 2)
        tick()
        tiles(total // tile // 2, total // tile)
        tick()

    width = r.inner_w.shape[2]
    project(r.conv, 0, r.inner_w.at[1], r.rows_all, NN)
    project(r.conv, width, r.state_w, r.rows_all, NN)
    project(r.stepraw, 0, r.step_w, r.rows_all, NT)
    project(r.gate, 0, r.inner_w.at[0], r.rows_all, NN)
    first.drain()
    weights = turned.back()
    f = mixer_forward(r, tick)
    while pending:
        tick()
    second.finish()
    project(r.local, 0, r.out_t, r.grads_all, NN)
    sums, total_copies = token_sums(r, f)
    drain = mixer_backward(r, f, sums)
    for load in weights:
        load.wait()
    rows, depth = r.result.shape
    Scatter(r, rows, depth).run(r.result)
    f.drain()
    drain()
    for copy in total_copies:
        copy.wait_send()
    second.drain()


def body(
    normed_rows,
    out_grad,
    inner_weight,
    state_weight,
    step_weight,
    conv_inner,
    conv_state,
    step_bias,
    decay_log,
    norm_gain,
    out_weight,
):
    count, depth = normed_rows.shape
    total = count * GROUP
    width, state_width = inner_weight.shape[2], state_weight.shape[1]
    both = width + state_width
    heads = width // HEAD_DIM
    chunks = total // CHUNK
    pair, half = 2 * count, depth // 2
    quarter = half // 2
    vmem = pl.BlockSpec(memory_space=pltpu.VMEM)
    smem = pl.BlockSpec(memory_space=pltpu.SMEM)
    anywhere = pl.BlockSpec(memory_space=pl.ANY)
    inputs = {
        "step_bias": (step_bias, smem),
        "decay_log": (decay_log, smem),
        "rows": (normed_rows, vmem),
        "grads": (out_grad, vmem),
        "conv_inner": (conv_inner, vmem),
        "conv_state": (conv_state, vmem),
        "gain": (norm_gain.reshape(1, -1), vmem),
        "inner_hbm": (inner_weight, anywhere),
        "state_hbm": (state_weight, anywhere),
        "out_hbm": (out_weight, anywhere),
        "step_hbm": (step_weight.T, anywhere),
    }
    state = (heads, HEAD_DIM, STATE)
    message = (heads * HEAD_DIM, STATE)
    scratch = {
        "rows_all": ((total, depth), BF16),
        "grads_all": ((total, depth), BF16),
        "swaps": ((2, count, half), BF16),
        "inner_w": (inner_weight.shape, BF16),
        "state_w": (state_weight.shape, BF16),
        "out_t": (out_weight.shape[::-1], BF16),
        "stage": ((6, width, width), BF16),
        "step_w": (step_weight.shape[::-1], BF16),
        "gate": ((total, width), BF16),
        "conv": ((total, both), BF16),
        "stepraw": ((total, CHUNK), F32),
        "local": ((total, width), F32),
        "ext": ((HALO + total, both), F32),
        "pre": ((total, both), F32),
        "act": ((total, both), F32),
        "xd": ((total, width), F32),
        "steps": ((total, CHUNK), F32),
        "cums": ((total, CHUNK), F32),
        "cb": ((chunks, CHUNK, CHUNK), F32),
        "decays": ((chunks, heads, CHUNK, CHUNK), F32),
        "out": ((total, width), F32),
        "dy": ((total, width), F32),
        "states": ((chunks + 1,) + state, F32),
        "d_states": ((chunks + 1,) + state, F32),
        "entering": (state, F32),
        "d_leaving": (state, F32),
        "fwd_out": (message, F32),
        "fwd_in": ((ROW - 1,) + message, F32),
        "bwd_out": (message, F32),
        "bwd_in": ((ROW - 1,) + message, F32),
        "cross_out": ((2,) + message, F32),
        "cross_in": ((2,) + message, F32),
        "cross_sum": (state, F32),
        "factors_out": ((8, CHUNK), F32),
        "factors_in": ((ROW - 1, 8, CHUNK), F32),
        "tot_out": ((2, 2, total), F32),
        "tot_in": ((3 + Z - 1, 2, total), F32),
        "d_pre": ((total + HALO, both), F32),
        "d_b": ((total, STATE), F32),
        "d_c": ((total, STATE), F32),
        "u_loc": ((total, width), F32),
        "d_gate": ((total, width), BF16),
        "d_inner": ((total, width), BF16),
        "d_state": ((total, state_width), BF16),
        "d_step": ((total, heads), BF16),
        "mine": ((Z, 2, pair, half), F32),
        "sib_out": ((Z, 2, pair, half), BF16),
        "sib_in": ((Z, 2, pair, half), BF16),
        "ring_out": ((30, pair, quarter), BF16),
        "ring_in": ((30, pair, quarter), BF16),
        "last_out": ((2, count, quarter), BF16),
        "last_in": ((2, count, quarter), BF16),
    }
    semaphores = {
        "weight_sem": 3,
        "stage_sem": 6,
        "back_sem": 3,
        "send_r": 63,
        "recv_r": 63,
        "send_g": 63,
        "recv_g": 63,
        "halo_sem": 4,
        "factor_send": ROW - 1,
        "factor_recv": ROW - 1,
        "fwd_send": ROW,
        "fwd_recv": ROW,
        "bwd_send": ROW,
        "bwd_recv": ROW,
        "tot_send": 3 + Z - 1,
        "tot_recv": 3 + Z - 1,
        "sib_send": Z,
        "sib_recv": Z,
        "ring_send": 30,
        "ring_recv": 30,
        "last_send": 2,
        "last_recv": 2,
    }
    names = list(inputs) + ["result", "turned_hbm"] + list(scratch) + list(semaphores)
    return pl.pallas_call(
        functools.partial(whole_kernel, names),
        out_shape=(
            jax.ShapeDtypeStruct((count, depth), BF16),
            jax.ShapeDtypeStruct((3, width, depth), BF16),
        ),
        in_specs=[spec for _, spec in inputs.values()],
        out_specs=(vmem, anywhere),
        scratch_shapes=[pltpu.VMEM(shape, dtype) for shape, dtype in scratch.values()]
        + [pltpu.SemaphoreType.DMA((n,)) for n in semaphores.values()],
        compiler_params=pltpu.CompilerParams(collective_id=0, has_side_effects=True, vmem_limit_bytes=VMEM_LIMIT),
        name="mixer_grad",
    )(*[value for value, _ in inputs.values()])[0]


def solution(mesh):
    placed = (
        P(("ctx", "tp"), None),
        P(("ctx", "tp"), None),
        P(None, None, "tp"),
        P(),
        P(None, "tp"),
        P(None, "tp"),
        P(),
        P("tp"),
        P("tp"),
        P("tp"),
        P("tp", None),
    )
    return jax.shard_map(
        body, mesh=mesh, in_specs=placed, out_specs=P(("ctx", "tp"), None), check_vma=False
    )
```

```python
import functools
from types import SimpleNamespace

import jax
import jax.numpy as jnp
from jax import lax
from jax.experimental import pallas as pl
from jax.experimental.pallas import tpu as pltpu
from jax.sharding import PartitionSpec as P

HEAD_DIM = 128
STATE = 128
CONV = 4
EPSILON = 1e-05
EXACT = lax.Precision.HIGHEST
NEAR = lax.Precision.HIGH
MESH = pl.DeviceIdType.MESH
F32 = jnp.float32
BF16 = jnp.bfloat16
VMEM_LIMIT = 62 * 1024 * 1024

Z = 8
GROUP = 4 * Z
ROW = 4
SHARDS = 2 * ROW
CHUNK = 128
HALO = 8
NN, NT, TN = ((1,), (0,)), ((1,), (1,)), ((0,), (0,))


def place():
    tp = lax.axis_index("tp")
    return tp // (2 * Z), lax.rem(tp // 2, Z), lax.rem(tp, 2)


def tp_id(yh, z, core):
    return (yh * Z + lax.rem(z + Z, Z)) * 2 + core


def remote(axis, partner, src, dst, send_sem, recv_sem):
    return pltpu.make_async_remote_copy(
        src_ref=src,
        dst_ref=dst,
        send_sem=send_sem,
        recv_sem=recv_sem,
        device_id={axis: partner},
        device_id_type=MESH,
    )


def dot(a, b, contract, precision=NEAR):
    return lax.dot_general(a, b, (contract, ((), ())), precision=precision, preferred_element_type=F32)


def dot16(a, b, contract):
    return lax.dot_general(a, b, (contract, ((), ())), preferred_element_type=F32)


class Gather:
    def __init__(self, own_ref, buf, swap, send_sem, recv_sem):
        self.own_ref, self.buf, self.swap = own_ref, buf, swap
        self.send_sem, self.recv_sem = send_sem, recv_sem
        self.yh, self.z, self.core = place()
        self.pair = 2 * own_ref.shape[0]
        self.half = own_ref.shape[1] // 2
        self.sibling = tp_id(self.yh, self.z, 1 - self.core)
        self.started = []

    def block(self, h, dz, sub, core=None):
        yh = self.yh if h == 0 else 1 - self.yh
        chip = yh * Z + lax.rem(self.z + (dz + Z), Z)
        rows = pl.ds(pl.multiple_of(chip * self.pair, 16), self.pair)
        quarter = self.half // 2
        at = (self.core if core is None else core) * self.half + sub * quarter
        return self.buf.at[rows, pl.ds(pl.multiple_of(at, quarter), quarter)]

    def copy(self, slot, src, dst, partner):
        return remote("tp", partner, src, dst, self.send_sem.at[slot], self.recv_sem.at[slot])

    def send(self, slot, src, dst, partner):
        copy = self.copy(slot, src, dst, partner)
        copy.start()
        self.started.append(copy)

    def got(self, slot, block):
        self.copy(slot, block, block, self.sibling).wait_recv()

    def across(self, sub, d):
        here = self.block(0, (1 - 2 * sub) * d, sub)
        self.send(sub * 31 + d, here, here, tp_id(1 - self.yh, self.z, self.core))

    def along(self, kind, sub, d):
        way = 1 - 2 * sub
        if kind == "long":
            here = self.block(0, way * (d - 1), sub)
            self.send(sub * 31 + 4 + d, here, here, tp_id(self.yh, self.z - way, self.core))
        elif kind == "short":
            here = self.block(0, -way * (d - 1), sub)
            self.send(sub * 31 + 9 + d, here, here, tp_id(self.yh, self.z + way, self.core))
        else:
            here = self.block(1, -way * (d - 1), sub)
            self.send(sub * 31 + 11 + d, here, here, tp_id(self.yh, self.z + way, self.core))

    def sibling_slot(self, h, dz, sub):
        return sub * 31 + 15 + h * 8 + dz % 8

    def to_sibling(self, h, dz, sub):
        here = self.block(h, dz, sub)
        self.send(self.sibling_slot(h, dz, sub), here, here, self.sibling)

    def first_swap(self):
        columns = pl.ds(pl.multiple_of((1 - self.core) * self.half, self.half), self.half)
        self.send(62, self.own_ref.at[:, columns], self.swap, self.sibling)

    def begin(self):
        self.got(62, self.swap)
        columns = pl.ds(pl.multiple_of(self.core * self.half, self.half), self.half)
        mine = self.own_ref[:, columns].astype(F32)
        other = self.swap[...].astype(F32)
        first = self.core == 0
        both = jnp.concatenate([jnp.where(first, mine, other), jnp.where(first, other, mine)], axis=0)
        quarter = self.half // 2
        for sub in (0, 1):
            self.block(0, 0, sub)[...] = both[:, sub * quarter : (sub + 1) * quarter].astype(BF16)
        for sub in (0, 1):
            self.along("long", sub, 1)
            self.across(sub, 0)
            self.along("short", sub, 1)
            self.to_sibling(0, 0, sub)

    def long(self, d):
        for sub in (0, 1):
            dz = (1 - 2 * sub) * d
            self.got(sub * 31 + 4 + d, self.block(0, dz, sub))
            if d < 5:
                self.along("long", sub, d + 1)
                self.across(sub, d)
            self.to_sibling(0, dz, sub)

    def short(self, d):
        for sub in (0, 1):
            dz = -(1 - 2 * sub) * d
            self.got(sub * 31 + 9 + d, self.block(0, dz, sub))
            if d < 2:
                self.along("short", sub, d + 1)
            self.to_sibling(0, dz, sub)

    def met(self, d):
        for sub in (0, 1):
            dz = (1 - 2 * sub) * d
            self.got(sub * 31 + d, self.block(1, dz, sub))
            if d == 0:
                self.along("other", sub, 1)
            self.to_sibling(1, dz, sub)

    def other(self, d):
        for sub in (0, 1):
            dz = -(1 - 2 * sub) * d
            self.got(sub * 31 + 11 + d, self.block(1, dz, sub))
            if d < 3:
                self.along("other", sub, d + 1)
            self.to_sibling(1, dz, sub)

    def steps(self):
        order = [
            (self.long, 1), (self.short, 1), (self.met, 0), (self.long, 2), (self.short, 2), (self.met, 1),
            (self.other, 1), (self.long, 3), (self.met, 2), (self.other, 2), (self.long, 4), (self.met, 3),
            (self.other, 3), (self.long, 5), (self.met, 4),
        ]
        return [functools.partial(step, d) for step, d in order]

    def finish(self):
        for sub in (0, 1):
            for h in (0, 1):
                for dz in range(8):
                    self.got(self.sibling_slot(h, dz, sub), self.block(h, dz, sub, 1 - self.core))

    def drain(self):
        for copy in self.started:
            copy.wait_send()


class Scatter:
    order = (-3, 3, -4, 2, -2, 1, -1, 0)

    def __init__(self, r, rows, depth):
        self.r = r
        self.yh, self.z, self.core = place()
        self.sibling = tp_id(self.yh, self.z, 1 - self.core)
        self.rows, self.pair, self.half = rows, 2 * rows, depth // 2
        self.quarter = self.half // 2
        self.tile = 512
        self.started = []

    def at(self, dz):
        return self.order.index(dz if dz < 4 and dz > -4 else -4 if abs(dz) == 4 else dz - 8 if dz > 0 else dz + 8)

    def start(self, copy):
        copy.start()
        self.started.append(copy)

    def product(self, dz):
        r, at, half, tile = self.r, self.at(dz), self.half, self.tile
        zt = lax.rem(self.z + (dz + Z), Z)
        spots = []
        for h in (0, 1):
            yt = self.yh if h == 0 else 1 - self.yh
            spots.append(pl.ds(pl.multiple_of((yt * Z + zt) * self.pair, 16), self.pair))

        parts = []
        for ref in (r.d_gate, r.d_inner, r.d_state, r.d_step):
            parts.append(jnp.concatenate([ref[spots[0], :], ref[spots[1], :]], axis=0))

        def side(which, keep):
            def turn(j, carry):
                here = pl.ds(pl.multiple_of(j * tile, tile), tile)
                cols = pl.ds(pl.multiple_of(which * half + j * tile, tile), tile)
                value = dot16(parts[3], r.step_w[:, cols], NN)
                for i in range(3):
                    width = parts[i].shape[1]
                    value += dot16(parts[i], r.rows_all[i * width : (i + 1) * width, cols], NN)
                for h in (0, 1):
                    keep[at, h, :, here] = value[h * self.pair : (h + 1) * self.pair].astype(keep.dtype)
                return carry

            lax.fori_loop(0, half // tile, turn, 0)

        side(1 - self.core, r.sib_out)
        self.start(
            remote("tp", self.sibling, r.sib_out.at[at], r.sib_in.at[at], r.sib_send.at[at], r.sib_recv.at[at])
        )
        side(self.core, r.mine)

    def sib_got(self, dz):
        at, r = self.at(dz), self.r
        there = r.sib_in.at[at]
        remote("tp", self.sibling, there, there, r.sib_send.at[at], r.sib_recv.at[at]).wait_recv()

    def got(self, slot):
        there = self.r.ring_in.at[slot]
        remote("tp", self.sibling, there, there, self.r.ring_send.at[slot], self.r.ring_recv.at[slot]).wait_recv()

    def slot(self, kind, sub, d):
        return sub * 15 + {"y": 0, "long": 4, "short": 9, "other": 11}[kind] + d

    def value(self, h, dz, sub, slots, columns):
        at, r = self.at(dz), self.r
        here = pl.ds(pl.multiple_of(sub * self.quarter + columns, self.tile), self.tile)
        there = pl.ds(pl.multiple_of(columns, self.tile), self.tile)
        total = r.mine[at, h, :, here] + r.sib_in[at, h, :, here].astype(F32)
        for slot in slots:
            total += r.ring_in[slot, :, there].astype(F32)
        return total

    def message(self, kind, sub, d):
        way = 1 - 2 * sub
        earlier = []
        if kind == "y":
            h, dz, partner = 1, way * d, tp_id(1 - self.yh, self.z, self.core)
            if d == 0:
                earlier.append(self.slot("other", sub, 1))
        elif kind == "long":
            h, dz, partner = 0, way * d, tp_id(self.yh, self.z + way, self.core)
            if d < 5:
                earlier += [self.slot("long", sub, d + 1), self.slot("y", sub, d)]
        elif kind == "short":
            h, dz, partner = 0, -way * d, tp_id(self.yh, self.z - way, self.core)
            if d < 2:
                earlier.append(self.slot("short", sub, d + 1))
        else:
            h, dz, partner = 1, -way * d, tp_id(self.yh, self.z - way, self.core)
            if d < 3:
                earlier.append(self.slot("other", sub, d + 1))
        for slot in earlier:
            self.got(slot)
        slot, r = self.slot(kind, sub, d), self.r

        def turn(j, carry):
            columns = j * self.tile
            there = pl.ds(pl.multiple_of(columns, self.tile), self.tile)
            r.ring_out[slot, :, there] = self.value(h, dz, sub, earlier, columns).astype(BF16)
            return carry

        lax.fori_loop(0, self.quarter // self.tile, turn, 0)
        self.start(
            remote("tp", partner, r.ring_out.at[slot], r.ring_in.at[slot], r.ring_send.at[slot], r.ring_recv.at[slot])
        )

    def run(self, out_ref):
        r, core, half = self.r, self.core, self.half

        def both(kind, d):
            for sub in (0, 1):
                self.message(kind, sub, d)

        self.product(-4)
        self.product(-3)
        self.sib_got(-4)
        both("y", 4)
        self.sib_got(-3)
        self.message("long", 0, 5)
        self.message("other", 0, 3)
        self.product(3)
        self.sib_got(3)
        self.message("long", 1, 5)
        self.message("other", 1, 3)
        both("y", 3)
        self.product(2)
        both("long", 4)
        self.product(-2)
        self.sib_got(2)
        self.message("short", 1, 2)
        self.message("y", 0, 2)
        self.sib_got(-2)
        self.message("short", 0, 2)
        self.message("y", 1, 2)
        both("other", 2)
        self.product(1)
        both("long", 3)
        self.product(-1)
        self.sib_got(1)
        self.sib_got(-1)
        both("y", 1)
        both("other", 1)
        self.product(0)
        both("long", 2)
        self.sib_got(0)
        both("y", 0)
        both("short", 1)
        both("long", 1)
        first = core == 0
        for sub in (0, 1):
            earlier = [self.slot(*key) for key in (("short", sub, 1), ("y", sub, 0), ("long", sub, 1))]
            for slot in earlier:
                self.got(slot)

            def final(j, carry, sub=sub, earlier=earlier):
                columns = j * self.tile
                value = self.value(0, 0, sub, earlier, columns)
                low, high = value[: self.rows], value[self.rows :]
                at = sub * self.quarter + columns
                here = pl.ds(pl.multiple_of(core * half + at, self.tile), self.tile)
                out_ref[:, here] = jnp.where(first, low, high).astype(BF16)
                there = pl.ds(pl.multiple_of(columns, self.tile), self.tile)
                r.last_out[sub, :, there] = jnp.where(first, high, low).astype(BF16)
                return carry

            lax.fori_loop(0, self.quarter // self.tile, final, 0)
            self.start(
                remote(
                    "tp", self.sibling, r.last_out.at[sub], r.last_in.at[sub], r.last_send.at[sub], r.last_recv.at[sub]
                )
            )
        for sub in (0, 1):
            there = r.last_in.at[sub]
            remote("tp", self.sibling, there, there, r.last_send.at[sub], r.last_recv.at[sub]).wait_recv()
            at = (1 - core) * half + sub * self.quarter
            out_ref[:, pl.ds(pl.multiple_of(at, self.quarter), self.quarter)] = r.last_in[sub]
        for copy in self.started:
            copy.wait_send()


class Turned:
    def __init__(self, r):
        self.r = r
        self.size = r.stage.shape[1]
        self.blocks = r.step_w.shape[1] // self.size
        self.todo = [functools.partial(self.out_block, j) for j in range(self.blocks)]
        self.copies = []
        for i, ref in enumerate((r.inner_w.at[0], r.inner_w.at[1], r.state_w)):
            self.todo += [functools.partial(self.block, i, ref, j) for j in range(self.blocks)]

    def span(self, j):
        return slice(j * self.size, (j + 1) * self.size)

    def out_load(self, j):
        r = self.r
        return pltpu.make_async_copy(r.out_hbm.at[:, self.span(j)], r.stage.at[j % 2], r.stage_sem.at[j % 2])

    def begin(self):
        for j in (0, 1):
            self.out_load(j).start()

    def out_block(self, j):
        self.out_load(j).wait()
        self.r.out_t[self.span(j), :] = self.r.stage[j % 2].T
        if j + 2 < self.blocks:
            self.out_load(j + 2).start()

    def block(self, i, ref, j):
        slot = len(self.copies) % 4
        if len(self.copies) >= 4:
            self.copies[-4].wait()
        self.r.stage[2 + slot] = ref[self.span(j), :].T
        copy = pltpu.make_async_copy(
            self.r.stage.at[2 + slot], self.r.turned_hbm.at[i, :, self.span(j)], self.r.stage_sem.at[2 + slot]
        )
        copy.start()
        self.copies.append(copy)

    def some(self, count):
        for _ in range(count):
            if self.todo:
                self.todo.pop(0)()

    def finish(self):
        self.some(len(self.todo))
        for copy in self.copies[-4:]:
            copy.wait()

    def back(self):
        width = self.r.inner_w.shape[2]
        loads = [
            pltpu.make_async_copy(
                self.r.turned_hbm.at[i], self.r.rows_all.at[i * width : (i + 1) * width, :], self.r.back_sem.at[i]
            )
            for i in range(3)
        ]
        for load in loads:
            load.start()
        return loads


class Exchange:
    def __init__(self, out, into, cross_out, cross_in, send_sem, recv_sem, factors_in, heads, forward):
        self.ctx = lax.axis_index("ctx")
        self.x, self.y = lax.rem(self.ctx, ROW), self.ctx // ROW
        self.out, self.into, self.heads, self.forward = out, into, heads, forward
        self.factors_in, self.cross_out, self.cross_in = factors_in, cross_out, cross_in
        self.gives = self.y == (0 if forward else 1)
        self.copies = [
            remote("ctx", self.peer(j), out, into.at[j - 1], send_sem.at[j - 1], recv_sem.at[j - 1])
            for j in range(1, ROW)
        ]
        self.cross = remote(
            "ctx", lax.rem(self.ctx + ROW, SHARDS), cross_out, cross_in, send_sem.at[ROW - 1], recv_sem.at[ROW - 1]
        )

    def peer(self, j):
        return self.y * ROW + lax.rem(self.x + j, ROW)

    def start(self):
        for copy in self.copies:
            copy.start()

    def step(self, value, slot):
        parts = []
        for h in range(self.heads):
            state = self.into[slot, h * HEAD_DIM : (h + 1) * HEAD_DIM, :].astype(F32)
            parts.append(value[h] * self.factors_in[slot, h : h + 1, :] + state)
        return parts

    def chain(self, total):
        for j in range(ROW - 1, 0, -1):
            there = self.x >= j if self.forward else self.x + j < ROW
            slot = j - 1 if self.forward else ROW - 1 - j

            @pl.when(there)
            def _(slot=slot):
                for h, part in enumerate(self.step([total[h] for h in range(self.heads)], slot)):
                    total[h] = part

    def give(self, total, own, factors):
        for copy in self.copies:
            copy.wait_recv()

        @pl.when(self.gives)
        def _():
            total[...] = jnp.zeros_like(total)
            self.chain(total)
            for h in range(self.heads):
                self.cross_sum[h] = total[h] * factors[h : h + 1, :] + own[h]
            for j in range(1, ROW):
                there = self.x + j < ROW if self.forward else self.x >= j
                slot = ROW - 1 - j if self.forward else j - 1

                @pl.when(there)
                def _(slot=slot):
                    for h, part in enumerate(self.step([self.cross_sum[h] for h in range(self.heads)], slot)):
                        self.cross_sum[h] = part

            for h in range(self.heads):
                self.cross_out[h * HEAD_DIM : (h + 1) * HEAD_DIM, :] = self.cross_sum[h]
            self.cross.start()

    def take(self, total):
        @pl.when(jnp.logical_not(self.gives))
        def _():
            self.cross.wait_recv()
            for h in range(self.heads):
                total[h] = self.cross_in[h * HEAD_DIM : (h + 1) * HEAD_DIM, :].astype(F32)
            self.chain(total)

    def drain(self):
        for copy in self.copies:
            copy.wait_send()

        @pl.when(self.gives)
        def _():
            self.cross.wait_send()


def mixer_forward(r, tick, while_sent, while_crossing):
    ctx = lax.axis_index("ctx")
    total, both = r.conv.shape
    width = both - 2 * STATE
    heads = width // HEAD_DIM
    chunks = total // CHUNK
    span = lambda k: slice(k * CHUNK, (k + 1) * CHUNK)
    r.ext[HALO:, :] = r.conv[...].astype(F32)
    halo = remote("ctx", lax.rem(ctx + 1, SHARDS), r.ext.at[total:, :], r.ext.at[:HALO, :], r.halo_sem.at[0], r.halo_sem.at[1])

    @pl.when(ctx < SHARDS - 1)
    def _():
        halo.start()

    lane = lax.broadcasted_iota(jnp.int32, (1, CHUNK), 1)
    rows_at = lax.broadcasted_iota(jnp.int32, (CHUNK, CHUNK), 0)
    cols_at = lax.broadcasted_iota(jnp.int32, (CHUNK, CHUNK), 1)
    causal = (rows_at >= cols_at).astype(F32)

    def per_lane(values):
        row = jnp.zeros_like(values[0])
        for h, value in enumerate(values):
            row = jnp.where(lane == h, value, row)
        return row

    bias = per_lane([jnp.full((1, CHUNK), r.step_bias[h], F32) for h in range(heads)])
    rate = per_lane([jnp.exp(jnp.full((1, CHUNK), r.decay_log[h], F32)) for h in range(heads)])
    valid = lane < heads
    kernel = [
        jnp.concatenate([r.conv_inner[k : k + 1, :], r.conv_state[k : k + 1, :]], axis=1) for k in range(CONV)
    ]
    ends = []
    for k in range(chunks):
        raw = jnp.where(valid, r.stepraw[span(k), :], 0.0) + bias
        step = jnp.maximum(raw, 0.0) + jnp.log1p(jnp.exp(-jnp.abs(raw)))
        step = jnp.where(valid, step, 0.0)
        r.steps[span(k), :] = step
        cum = dot(causal, -step * rate, NN, EXACT)
        r.cums[span(k), :] = cum
        turned = cum.T
        ends.append([cum[CHUNK - 1 :, h : h + 1] for h in range(heads)])
        for h in range(heads):
            spread = cum[:, h : h + 1] - turned[h : h + 1, :]
            r.decays[k, h] = jnp.exp(jnp.minimum(spread, 0.0)) * causal
    tick()

    @pl.when(ctx == 0)
    def _():
        r.ext[:HALO, :] = jnp.zeros((HALO, both), F32)

    @pl.when(ctx > 0)
    def _():
        halo.wait_recv()

    for k in range(chunks):
        blended = jnp.zeros((CHUNK, both), F32)
        for tap in range(CONV):
            start = k * CHUNK + HALO - (CONV - 1) + tap
            blended += kernel[tap] * r.ext[start : start + CHUNK, :]
        r.pre[span(k), :] = blended
        active = blended * jax.nn.sigmoid(blended)
        r.act[span(k), :] = active
        b_rows, c_rows = active[:, width : width + STATE], active[:, width + STATE :]
        r.cb[k] = dot(c_rows, b_rows, NT)
        for h in range(heads):
            lanes = slice(h * HEAD_DIM, (h + 1) * HEAD_DIM)
            fed = active[:, lanes] * r.steps[span(k), h : h + 1]
            r.xd[span(k), lanes] = fed
            left = jnp.exp(ends[k][h] - r.cums[span(k), h : h + 1])
            own = dot(fed * left, b_rows, TN)
            if k == 0:
                r.states[0, h] = jnp.zeros_like(own)
                r.states[1, h] = own
            else:
                r.states[k + 1, h] = jnp.exp(ends[k][h]) * r.states[k, h] + own
        if k % 3 == 2:
            tick()

    befores = [[jnp.zeros((1, 1), F32) for _ in range(heads)]]
    for k in range(chunks):
        befores.append([befores[k][h] + ends[k][h] for h in range(heads)])
    whole = [jnp.exp(befores[chunks][h]) for h in range(heads)]
    row8 = lax.broadcasted_iota(jnp.int32, (8, CHUNK), 0)
    factors = jnp.zeros((8, CHUNK), F32)
    for h in range(heads):
        r.fwd_out[h * HEAD_DIM : (h + 1) * HEAD_DIM, :] = r.states[chunks, h]
        factors = jnp.where(row8 == h, whole[h], factors)
    r.factors_out[...] = factors
    forward = Exchange(
        r.fwd_out, r.fwd_in, r.cross_out.at[0], r.cross_in.at[0], r.fwd_send, r.fwd_recv, r.factors_in, heads, True
    )
    forward.cross_sum = r.cross_sum
    factor_copies = [
        remote(
            "ctx", forward.peer(j), r.factors_out, r.factors_in.at[j - 1], r.factor_send.at[j - 1], r.factor_recv.at[j - 1]
        )
        for j in range(1, ROW)
    ]
    for copy in factor_copies:
        copy.start()
    forward.start()
    tick()

    for k in range(chunks):
        c_rows = r.act[span(k), width + STATE :]
        for h in range(heads):
            lanes = slice(h * HEAD_DIM, (h + 1) * HEAD_DIM)
            value = dot(r.decays[k, h] * r.cb[k], r.xd[span(k), lanes], NN)
            if k > 0:
                value += jnp.exp(r.cums[span(k), h : h + 1]) * dot(c_rows, r.states[k, h], NT)
            r.out[span(k), lanes] = value
        if k % 3 == 2:
            tick()

    while_sent()
    for copy in factor_copies:
        copy.wait_recv()
    forward.give(r.entering, r.states.at[chunks], factors)
    while_crossing()
    forward.take(r.entering)
    for k in range(chunks):
        c_rows = r.act[span(k), width + STATE :]
        for h in range(heads):
            lanes = slice(h * HEAD_DIM, (h + 1) * HEAD_DIM)
            grown = jnp.exp(r.cums[span(k), h : h + 1] + befores[k][h])
            r.out[span(k), lanes] = r.out[span(k), lanes] + grown * dot(c_rows, r.entering[h], NT)
            r.states[k, h] = r.states[k, h] + jnp.exp(befores[k][h]) * r.entering[h]
    for h in range(heads):
        r.states[chunks, h] = r.states[chunks, h] + whole[h] * r.entering[h]

    def drain():
        @pl.when(ctx < SHARDS - 1)
        def _():
            halo.wait_send()

        for copy in factor_copies:
            copy.wait_send()
        forward.drain()

    return SimpleNamespace(
        total=total, both=both, width=width, heads=heads, chunks=chunks, span=span, lane=lane, bias=bias, rate=rate,
        valid=valid, kernel=kernel, ends=ends, factors=factors, drain=drain, rows_at=rows_at, cols_at=cols_at,
    )


def token_sums(r, f):
    gain = r.gain[...]
    ones = jnp.ones((8, f.width), F32)
    for k in range(f.chunks):
        gate = r.gate[f.span(k), :].astype(F32)
        gated = r.out[f.span(k), :] * (gate * jax.nn.sigmoid(gate))
        squares = dot(ones, gated * gated, NT)
        crosses = dot(ones, gain * r.local[f.span(k), :] * gated, NT)
        r.tot_out[0, 0:1, f.span(k)] = squares[0:1, :]
        r.tot_out[0, 1:2, f.span(k)] = crosses[0:1, :]
    yh, z, core = place()
    copies = []

    def swap(phase, partners, base):
        mine = []
        for j, partner in enumerate(partners):
            slot = base + j
            copy = remote(
                "tp", partner, r.tot_out.at[phase], r.tot_in.at[slot], r.tot_send.at[slot], r.tot_recv.at[slot]
            )
            copy.start()
            mine.append(copy)
        sums = r.tot_out[phase]
        for j, copy in enumerate(mine):
            copy.wait_recv()
            sums = sums + r.tot_in[base + j]
        copies.extend(mine)
        return sums

    near = [tp_id(yh, z, 1 - core), tp_id(1 - yh, z, core), tp_id(1 - yh, z, 1 - core)]
    r.tot_out[1] = swap(0, near, 0)
    sums = swap(1, [tp_id(yh, z + j, core) for j in range(1, Z)], len(near))
    return sums, copies


def mixer_backward(r, f, sums):
    ctx = lax.axis_index("ctx")
    span, chunks, heads, width, total = f.span, f.chunks, f.heads, f.width, f.total
    channels = width * GROUP
    gain = r.gain[...]
    anti = (f.rows_at <= f.cols_at).astype(F32)
    ends = f.ends
    for k in range(chunks):
        held = jnp.concatenate([sums[:, span(k)], jnp.zeros((CHUNK - 2, CHUNK), F32)], axis=0).T
        inverse = lax.rsqrt(held[:, 0:1] / channels + EPSILON)
        pull = inverse * inverse * inverse * (held[:, 1:2] / channels)
        gate = r.gate[span(k), :].astype(F32)
        sigmoid = jax.nn.sigmoid(gate)
        opened = gate * sigmoid
        value = r.out[span(k), :]
        d_gated = inverse * (gain * r.local[span(k), :]) - value * opened * pull
        r.d_gate[span(k), :] = (d_gated * value * sigmoid * (1.0 + gate * (1.0 - sigmoid))).astype(BF16)
        r.dy[span(k), :] = d_gated * opened

    for k in range(chunks - 1, -1, -1):
        c_rows = r.act[span(k), width + STATE :]
        for h in range(heads):
            lanes = slice(h * HEAD_DIM, (h + 1) * HEAD_DIM)
            own = dot(r.dy[span(k), lanes] * jnp.exp(r.cums[span(k), h : h + 1]), c_rows, TN)
            if k < chunks - 1:
                own += jnp.exp(ends[k][h]) * r.d_states[k + 1, h]
            r.d_states[k, h] = own
    for h in range(heads):
        r.bwd_out[h * HEAD_DIM : (h + 1) * HEAD_DIM, :] = r.d_states[0, h]
    backward = Exchange(
        r.bwd_out, r.bwd_in, r.cross_out.at[1], r.cross_in.at[1], r.bwd_send, r.bwd_recv, r.factors_in, heads, False
    )
    backward.cross_sum = r.cross_sum
    backward.start()

    def local(k):
        b_rows, c_rows = r.act[span(k), width : width + STATE], r.act[span(k), width + STATE :]
        d_cb = jnp.zeros((CHUNK, CHUNK), F32)
        d_crows = jnp.zeros((CHUNK, STATE), F32)
        for h in range(heads):
            lanes = slice(h * HEAD_DIM, (h + 1) * HEAD_DIM)
            grad = r.dy[span(k), lanes]
            d_cb += r.decays[k, h] * dot(grad, r.xd[span(k), lanes], NT)
            r.u_loc[span(k), lanes] = dot(r.decays[k, h] * r.cb[k], grad, TN)
            d_crows += jnp.exp(r.cums[span(k), h : h + 1]) * dot(grad, r.states[k, h], NN)
        r.d_b[span(k), :] = dot(d_cb, c_rows, TN)
        r.d_c[span(k), :] = d_crows + dot(d_cb, b_rows, NN)

    for k in range(chunks // 2):
        local(k)
    backward.give(r.d_leaving, r.d_states.at[0], f.factors)
    for k in range(chunks // 2, chunks):
        local(k)
    backward.take(r.d_leaving)
    after = [jnp.zeros((1, 1), F32) for _ in range(heads)]
    for h in range(heads):
        r.d_states[chunks, h] = r.d_leaving[h]
    for k in range(chunks - 1, 0, -1):
        after = [after[h] + ends[k][h] for h in range(heads)]
        for h in range(heads):
            r.d_states[k, h] = r.d_states[k, h] + jnp.exp(after[h]) * r.d_leaving[h]

    halo = remote("ctx", lax.rem(ctx + SHARDS - 1, SHARDS), r.d_pre.at[:HALO, :], r.d_pre.at[total:, :], r.halo_sem.at[2], r.halo_sem.at[3])
    for k in range(chunks):
        b_rows = r.act[span(k), width : width + STATE]
        d_brows = r.d_b[span(k), :]
        d_acts = []
        pulls = jnp.zeros((CHUNK, CHUNK), F32)
        feeds = jnp.zeros((CHUNK, CHUNK), F32)
        edge = jnp.zeros((1, CHUNK), F32)
        for h in range(heads):
            lanes = slice(h * HEAD_DIM, (h + 1) * HEAD_DIM)
            step = r.steps[span(k), h : h + 1]
            left = jnp.exp(ends[k][h] - r.cums[span(k), h : h + 1])
            d_next = r.d_states[k + 1, h]
            grad = r.u_loc[span(k), lanes] + left * dot(b_rows, d_next, NT)
            d_brows += dot(r.xd[span(k), lanes] * left, d_next, NN)
            d_acts.append(grad * step)
            fed = jnp.sum(grad * r.act[span(k), lanes], axis=1, keepdims=True)
            met = jnp.sum(r.dy[span(k), lanes] * r.out[span(k), lanes], axis=1, keepdims=True)
            pulls = jnp.where(f.lane == h, met - step * fed, pulls)
            feeds = jnp.where(f.lane == h, fed, feeds)
            edge = jnp.where(f.lane == h, jnp.sum(d_next * r.states[k + 1, h]), edge)
        d_decay = dot(anti, pulls, NN, EXACT) + edge
        raw = jnp.where(f.valid, r.stepraw[span(k), :], 0.0) + f.bias
        d_raw = (feeds - f.rate * d_decay) * jax.nn.sigmoid(raw)
        r.d_step[span(k), :] = d_raw[:, :heads].astype(BF16)
        d_act = jnp.concatenate(d_acts + [d_brows, r.d_c[span(k), :]], axis=1)
        value = r.pre[span(k), :]
        sigmoid = jax.nn.sigmoid(value)
        r.d_pre[span(k), :] = d_act * sigmoid * (1.0 + value * (1.0 - sigmoid))
        if k == 0:

            @pl.when(ctx > 0)
            def _():
                halo.start()

    @pl.when(ctx == SHARDS - 1)
    def _():
        r.d_pre[total:, :] = jnp.zeros((HALO, f.both), F32)

    @pl.when(ctx < SHARDS - 1)
    def _():
        halo.wait_recv()

    for k in range(chunks):
        blended = jnp.zeros((CHUNK, f.both), F32)
        for tap in range(CONV):
            start = k * CHUNK + CONV - 1 - tap
            blended += f.kernel[tap] * r.d_pre[start : start + CHUNK, :]
        r.d_inner[span(k), :] = blended[:, :width].astype(BF16)
        r.d_state[span(k), :] = blended[:, width:].astype(BF16)

    def drain():
        @pl.when(ctx > 0)
        def _():
            halo.wait_send()

        backward.drain()

    return drain


def whole_kernel(names, *refs):
    r = SimpleNamespace(**dict(zip(names, refs, strict=True)))
    loads = [
        pltpu.make_async_copy(src, dst, r.weight_sem.at[i])
        for i, (src, dst) in enumerate(
            ((r.inner_hbm, r.inner_w), (r.state_hbm, r.state_w), (r.step_hbm, r.step_w))
        )
    ]
    for load in loads:
        load.start()
    turned = Turned(r)
    turned.begin()
    yh, z, core = place()
    ctx = lax.axis_index("ctx")
    barrier = pltpu.get_barrier_semaphore()
    tp_partners = [tp_id(yh, z, 1 - core), tp_id(1 - yh, z, core), tp_id(1 - yh, z, 1 - core)]
    tp_partners += [tp_id(yh, z + j, core) for j in range(1, Z)]
    row = ctx // ROW * ROW
    ctx_partners = [row + lax.rem(ctx - row + j, ROW) for j in range(1, ROW)]
    ctx_partners += [lax.rem(ctx + j, SHARDS) for j in (ROW, 1, SHARDS - 1)]
    for axis, partners in (("tp", tp_partners), ("ctx", ctx_partners)):
        for partner in partners:
            pl.semaphore_signal(barrier, inc=1, device_id={axis: partner}, device_id_type=MESH)
    pl.semaphore_wait(barrier, len(tp_partners) + len(ctx_partners))

    first = Gather(r.rows, r.rows_all, r.swaps.at[0], r.send_r, r.recv_r)
    second = Gather(r.grads, r.grads_all, r.swaps.at[1], r.send_g, r.recv_g)
    first.first_swap()
    second.first_swap()
    first.begin()
    early, late = first.steps()[:-3], first.steps()[-3:]
    turned.some(6)
    for load in loads:
        load.wait()
    for step in early:
        step()
        turned.some(4)
    second.begin()
    pending = second.steps()
    for step in late:
        step()
        pending.pop(0)()
    turned.finish()
    first.finish()

    def tick():
        if pending:
            pending.pop(0)()

    total, tile = r.rows_all.shape[0], 128

    def project(dst, column, weight, source, contract):
        def tiles(low, high):
            def turn(i, carry):
                at = pl.ds(pl.multiple_of(i * tile, tile), tile)
                value = dot16(source[at, :], weight[...], contract)
                if dst.dtype == F32 and source is r.rows_all:
                    value = value.astype(BF16)
                dst[at, pl.ds(column, value.shape[1])] = value.astype(dst.dtype)
                return carry

            lax.fori_loop(low, high, turn, 0)

        tiles(0, total // tile // 2)
        tick()
        tiles(total // tile // 2, total // tile)
        tick()

    width = r.inner_w.shape[2]
    project(r.conv, 0, r.inner_w.at[1], r.rows_all, NN)
    project(r.conv, width, r.state_w, r.rows_all, NN)
    project(r.stepraw, 0, r.step_w, r.rows_all, NT)

    def while_sent():
        project(r.gate, 0, r.inner_w.at[0], r.rows_all, NN)
        first.drain()
        weights.extend(turned.back())

    def while_crossing():
        while pending:
            tick()
        second.finish()
        project(r.local, 0, r.out_t, r.grads_all, NN)

    weights = []
    f = mixer_forward(r, tick, while_sent, while_crossing)
    sums, total_copies = token_sums(r, f)
    drain = mixer_backward(r, f, sums)
    for load in weights:
        load.wait()
    rows, depth = r.result.shape
    Scatter(r, rows, depth).run(r.result)
    f.drain()
    drain()
    for copy in total_copies:
        copy.wait_send()
    second.drain()


def body(
    normed_rows,
    out_grad,
    inner_weight,
    state_weight,
    step_weight,
    conv_inner,
    conv_state,
    step_bias,
    decay_log,
    norm_gain,
    out_weight,
):
    count, depth = normed_rows.shape
    total = count * GROUP
    width, state_width = inner_weight.shape[2], state_weight.shape[1]
    both = width + state_width
    heads = width // HEAD_DIM
    chunks = total // CHUNK
    pair, half = 2 * count, depth // 2
    quarter = half // 2
    vmem = pl.BlockSpec(memory_space=pltpu.VMEM)
    smem = pl.BlockSpec(memory_space=pltpu.SMEM)
    anywhere = pl.BlockSpec(memory_space=pl.ANY)
    inputs = {
        "step_bias": (step_bias, smem),
        "decay_log": (decay_log, smem),
        "rows": (normed_rows, vmem),
        "grads": (out_grad, vmem),
        "conv_inner": (conv_inner, vmem),
        "conv_state": (conv_state, vmem),
        "gain": (norm_gain.reshape(1, -1), vmem),
        "inner_hbm": (inner_weight, anywhere),
        "state_hbm": (state_weight, anywhere),
        "out_hbm": (out_weight, anywhere),
        "step_hbm": (step_weight.T, anywhere),
    }
    state = (heads, HEAD_DIM, STATE)
    message = (heads * HEAD_DIM, STATE)
    scratch = {
        "rows_all": ((total, depth), BF16),
        "grads_all": ((total, depth), BF16),
        "swaps": ((2, count, half), BF16),
        "inner_w": (inner_weight.shape, BF16),
        "state_w": (state_weight.shape, BF16),
        "out_t": (out_weight.shape[::-1], BF16),
        "stage": ((6, width, width), BF16),
        "step_w": (step_weight.shape[::-1], BF16),
        "gate": ((total, width), BF16),
        "conv": ((total, both), BF16),
        "stepraw": ((total, CHUNK), F32),
        "local": ((total, width), F32),
        "ext": ((HALO + total, both), F32),
        "pre": ((total, both), F32),
        "act": ((total, both), F32),
        "xd": ((total, width), F32),
        "steps": ((total, CHUNK), F32),
        "cums": ((total, CHUNK), F32),
        "cb": ((chunks, CHUNK, CHUNK), F32),
        "decays": ((chunks, heads, CHUNK, CHUNK), F32),
        "out": ((total, width), F32),
        "dy": ((total, width), F32),
        "states": ((chunks + 1,) + state, F32),
        "d_states": ((chunks + 1,) + state, F32),
        "entering": (state, F32),
        "d_leaving": (state, F32),
        "fwd_out": (message, F32),
        "fwd_in": ((ROW - 1,) + message, F32),
        "bwd_out": (message, F32),
        "bwd_in": ((ROW - 1,) + message, F32),
        "cross_out": ((2,) + message, F32),
        "cross_in": ((2,) + message, F32),
        "cross_sum": (state, F32),
        "factors_out": ((8, CHUNK), F32),
        "factors_in": ((ROW - 1, 8, CHUNK), F32),
        "tot_out": ((2, 2, total), F32),
        "tot_in": ((3 + Z - 1, 2, total), F32),
        "d_pre": ((total + HALO, both), F32),
        "d_b": ((total, STATE), F32),
        "d_c": ((total, STATE), F32),
        "u_loc": ((total, width), F32),
        "d_gate": ((total, width), BF16),
        "d_inner": ((total, width), BF16),
        "d_state": ((total, state_width), BF16),
        "d_step": ((total, heads), BF16),
        "mine": ((Z, 2, pair, half), F32),
        "sib_out": ((Z, 2, pair, half), BF16),
        "sib_in": ((Z, 2, pair, half), BF16),
        "ring_out": ((30, pair, quarter), BF16),
        "ring_in": ((30, pair, quarter), BF16),
        "last_out": ((2, count, quarter), BF16),
        "last_in": ((2, count, quarter), BF16),
    }
    semaphores = {
        "weight_sem": 3,
        "stage_sem": 6,
        "back_sem": 3,
        "send_r": 63,
        "recv_r": 63,
        "send_g": 63,
        "recv_g": 63,
        "halo_sem": 4,
        "factor_send": ROW - 1,
        "factor_recv": ROW - 1,
        "fwd_send": ROW,
        "fwd_recv": ROW,
        "bwd_send": ROW,
        "bwd_recv": ROW,
        "tot_send": 3 + Z - 1,
        "tot_recv": 3 + Z - 1,
        "sib_send": Z,
        "sib_recv": Z,
        "ring_send": 30,
        "ring_recv": 30,
        "last_send": 2,
        "last_recv": 2,
    }
    names = list(inputs) + ["result", "turned_hbm"] + list(scratch) + list(semaphores)
    return pl.pallas_call(
        functools.partial(whole_kernel, names),
        out_shape=(
            jax.ShapeDtypeStruct((count, depth), BF16),
            jax.ShapeDtypeStruct((3, width, depth), BF16),
        ),
        in_specs=[spec for _, spec in inputs.values()],
        out_specs=(vmem, anywhere),
        scratch_shapes=[pltpu.VMEM(shape, dtype) for shape, dtype in scratch.values()]
        + [pltpu.SemaphoreType.DMA((n,)) for n in semaphores.values()],
        compiler_params=pltpu.CompilerParams(collective_id=0, has_side_effects=True, vmem_limit_bytes=VMEM_LIMIT),
        name="mixer_grad",
    )(*[value for value, _ in inputs.values()])[0]


def solution(mesh):
    placed = (
        P(("ctx", "tp"), None),
        P(("ctx", "tp"), None),
        P(None, None, "tp"),
        P(),
        P(None, "tp"),
        P(None, "tp"),
        P(),
        P("tp"),
        P("tp"),
        P("tp"),
        P("tp", None),
    )
    return jax.shard_map(
        body, mesh=mesh, in_specs=placed, out_specs=P(("ctx", "tp"), None), check_vma=False
    )
```

```python
import functools
from types import SimpleNamespace

import jax
import jax.numpy as jnp
from jax import lax
from jax.experimental import pallas as pl
from jax.experimental.pallas import tpu as pltpu
from jax.sharding import PartitionSpec as P

HEAD_DIM = 128
STATE = 128
CONV = 4
EPSILON = 1e-05
EXACT = lax.Precision.HIGHEST
NEAR = lax.Precision.HIGH
MESH = pl.DeviceIdType.MESH
F32 = jnp.float32
BF16 = jnp.bfloat16
VMEM_LIMIT = 62 * 1024 * 1024

Z = 8
GROUP = 4 * Z
ROW = 4
SHARDS = 2 * ROW
CHUNK = 128
HALO = 8
NN, NT, TN = ((1,), (0,)), ((1,), (1,)), ((0,), (0,))


def place():
    tp = lax.axis_index("tp")
    return tp // (2 * Z), lax.rem(tp // 2, Z), lax.rem(tp, 2)


def tp_id(yh, z, core):
    return (yh * Z + lax.rem(z + Z, Z)) * 2 + core


def remote(axis, partner, src, dst, send_sem, recv_sem):
    return pltpu.make_async_remote_copy(
        src_ref=src,
        dst_ref=dst,
        send_sem=send_sem,
        recv_sem=recv_sem,
        device_id={axis: partner},
        device_id_type=MESH,
    )


def dot(a, b, contract, precision=NEAR):
    return lax.dot_general(a, b, (contract, ((), ())), precision=precision, preferred_element_type=F32)


def dot16(a, b, contract):
    return lax.dot_general(a, b, (contract, ((), ())), preferred_element_type=F32)


class Gather:
    def __init__(self, own_ref, buf, swap, send_sem, recv_sem):
        self.own_ref, self.buf, self.swap = own_ref, buf, swap
        self.send_sem, self.recv_sem = send_sem, recv_sem
        self.yh, self.z, self.core = place()
        self.pair = 2 * own_ref.shape[0]
        self.half = own_ref.shape[1] // 2
        self.sibling = tp_id(self.yh, self.z, 1 - self.core)
        self.started = []

    def block(self, h, dz, sub, core=None):
        yh = self.yh if h == 0 else 1 - self.yh
        chip = yh * Z + lax.rem(self.z + (dz + Z), Z)
        rows = pl.ds(pl.multiple_of(chip * self.pair, 16), self.pair)
        quarter = self.half // 2
        at = (self.core if core is None else core) * self.half + sub * quarter
        return self.buf.at[rows, pl.ds(pl.multiple_of(at, quarter), quarter)]

    def copy(self, slot, src, dst, partner):
        return remote("tp", partner, src, dst, self.send_sem.at[slot], self.recv_sem.at[slot])

    def send(self, slot, src, dst, partner):
        copy = self.copy(slot, src, dst, partner)
        copy.start()
        self.started.append(copy)

    def got(self, slot, block):
        self.copy(slot, block, block, self.sibling).wait_recv()

    def across(self, sub, d):
        here = self.block(0, (1 - 2 * sub) * d, sub)
        self.send(sub * 31 + d, here, here, tp_id(1 - self.yh, self.z, self.core))

    def along(self, kind, sub, d):
        way = 1 - 2 * sub
        if kind == "long":
            here = self.block(0, way * (d - 1), sub)
            self.send(sub * 31 + 4 + d, here, here, tp_id(self.yh, self.z - way, self.core))
        elif kind == "short":
            here = self.block(0, -way * (d - 1), sub)
            self.send(sub * 31 + 9 + d, here, here, tp_id(self.yh, self.z + way, self.core))
        else:
            here = self.block(1, -way * (d - 1), sub)
            self.send(sub * 31 + 11 + d, here, here, tp_id(self.yh, self.z + way, self.core))

    def sibling_slot(self, h, dz, sub):
        return sub * 31 + 15 + h * 8 + dz % 8

    def to_sibling(self, h, dz, sub):
        here = self.block(h, dz, sub)
        self.send(self.sibling_slot(h, dz, sub), here, here, self.sibling)

    def first_swap(self):
        columns = pl.ds(pl.multiple_of((1 - self.core) * self.half, self.half), self.half)
        self.send(62, self.own_ref.at[:, columns], self.swap, self.sibling)

    def begin(self):
        self.got(62, self.swap)
        columns = pl.ds(pl.multiple_of(self.core * self.half, self.half), self.half)
        mine = self.own_ref[:, columns].astype(F32)
        other = self.swap[...].astype(F32)
        first = self.core == 0
        both = jnp.concatenate([jnp.where(first, mine, other), jnp.where(first, other, mine)], axis=0)
        quarter = self.half // 2
        for sub in (0, 1):
            self.block(0, 0, sub)[...] = both[:, sub * quarter : (sub + 1) * quarter].astype(BF16)
        for sub in (0, 1):
            self.along("long", sub, 1)
            self.across(sub, 0)
            self.along("short", sub, 1)
            self.to_sibling(0, 0, sub)

    def long(self, d):
        for sub in (0, 1):
            dz = (1 - 2 * sub) * d
            self.got(sub * 31 + 4 + d, self.block(0, dz, sub))
            if d < 5:
                self.along("long", sub, d + 1)
                self.across(sub, d)
            self.to_sibling(0, dz, sub)

    def short(self, d):
        for sub in (0, 1):
            dz = -(1 - 2 * sub) * d
            self.got(sub * 31 + 9 + d, self.block(0, dz, sub))
            if d < 2:
                self.along("short", sub, d + 1)
            self.to_sibling(0, dz, sub)

    def met(self, d):
        for sub in (0, 1):
            dz = (1 - 2 * sub) * d
            self.got(sub * 31 + d, self.block(1, dz, sub))
            if d == 0:
                self.along("other", sub, 1)
            self.to_sibling(1, dz, sub)

    def other(self, d):
        for sub in (0, 1):
            dz = -(1 - 2 * sub) * d
            self.got(sub * 31 + 11 + d, self.block(1, dz, sub))
            if d < 3:
                self.along("other", sub, d + 1)
            self.to_sibling(1, dz, sub)

    def steps(self):
        order = [
            (self.long, 1), (self.short, 1), (self.met, 0), (self.long, 2), (self.short, 2), (self.met, 1),
            (self.other, 1), (self.long, 3), (self.met, 2), (self.other, 2), (self.long, 4), (self.met, 3),
            (self.other, 3), (self.long, 5), (self.met, 4),
        ]
        return [functools.partial(step, d) for step, d in order]

    def finish(self):
        for sub in (0, 1):
            for h in (0, 1):
                for dz in range(8):
                    self.got(self.sibling_slot(h, dz, sub), self.block(h, dz, sub, 1 - self.core))

    def drain(self):
        for copy in self.started:
            copy.wait_send()


class Scatter:
    order = (-3, 3, -4, 2, -2, 1, -1, 0)

    def __init__(self, r, rows, depth):
        self.r = r
        self.yh, self.z, self.core = place()
        self.sibling = tp_id(self.yh, self.z, 1 - self.core)
        self.rows, self.pair, self.half = rows, 2 * rows, depth // 2
        self.quarter = self.half // 2
        self.tile = 512
        self.started = []

    def at(self, dz):
        return self.order.index(dz if dz < 4 and dz > -4 else -4 if abs(dz) == 4 else dz - 8 if dz > 0 else dz + 8)

    def start(self, copy):
        copy.start()
        self.started.append(copy)

    def product(self, dz):
        r, at, half, tile = self.r, self.at(dz), self.half, self.tile
        zt = lax.rem(self.z + (dz + Z), Z)
        spots = []
        for h in (0, 1):
            yt = self.yh if h == 0 else 1 - self.yh
            spots.append(pl.ds(pl.multiple_of((yt * Z + zt) * self.pair, 16), self.pair))

        parts = []
        for ref in (r.d_gate, r.d_inner, r.d_state, r.d_step):
            parts.append(jnp.concatenate([ref[spots[0], :], ref[spots[1], :]], axis=0))

        def side(which, keep):
            def turn(j, carry):
                here = pl.ds(pl.multiple_of(j * tile, tile), tile)
                cols = pl.ds(pl.multiple_of(which * half + j * tile, tile), tile)
                value = dot16(parts[3], r.step_w[:, cols], NN)
                for i in range(3):
                    width = parts[i].shape[1]
                    value += dot16(parts[i], r.rows_all[i * width : (i + 1) * width, cols], NN)
                for h in (0, 1):
                    keep[at, h, :, here] = value[h * self.pair : (h + 1) * self.pair].astype(keep.dtype)
                return carry

            lax.fori_loop(0, half // tile, turn, 0)

        side(1 - self.core, r.sib_out)
        self.start(
            remote("tp", self.sibling, r.sib_out.at[at], r.sib_in.at[at], r.sib_send.at[at], r.sib_recv.at[at])
        )
        side(self.core, r.mine)

    def sib_got(self, dz):
        at, r = self.at(dz), self.r
        there = r.sib_in.at[at]
        remote("tp", self.sibling, there, there, r.sib_send.at[at], r.sib_recv.at[at]).wait_recv()

    def got(self, slot):
        there = self.r.ring_in.at[slot]
        remote("tp", self.sibling, there, there, self.r.ring_send.at[slot], self.r.ring_recv.at[slot]).wait_recv()

    def slot(self, kind, sub, d):
        return sub * 15 + {"y": 0, "long": 4, "short": 9, "other": 11}[kind] + d

    def value(self, h, dz, sub, slots, columns):
        at, r = self.at(dz), self.r
        here = pl.ds(pl.multiple_of(sub * self.quarter + columns, self.tile), self.tile)
        there = pl.ds(pl.multiple_of(columns, self.tile), self.tile)
        total = r.mine[at, h, :, here] + r.sib_in[at, h, :, here].astype(F32)
        for slot in slots:
            total += r.ring_in[slot, :, there].astype(F32)
        return total

    def message(self, kind, sub, d):
        way = 1 - 2 * sub
        earlier = []
        if kind == "y":
            h, dz, partner = 1, way * d, tp_id(1 - self.yh, self.z, self.core)
            if d == 0:
                earlier.append(self.slot("other", sub, 1))
        elif kind == "long":
            h, dz, partner = 0, way * d, tp_id(self.yh, self.z + way, self.core)
            if d < 5:
                earlier += [self.slot("long", sub, d + 1), self.slot("y", sub, d)]
        elif kind == "short":
            h, dz, partner = 0, -way * d, tp_id(self.yh, self.z - way, self.core)
            if d < 2:
                earlier.append(self.slot("short", sub, d + 1))
        else:
            h, dz, partner = 1, -way * d, tp_id(self.yh, self.z - way, self.core)
            if d < 3:
                earlier.append(self.slot("other", sub, d + 1))
        for slot in earlier:
            self.got(slot)
        slot, r = self.slot(kind, sub, d), self.r

        def turn(j, carry):
            columns = j * self.tile
            there = pl.ds(pl.multiple_of(columns, self.tile), self.tile)
            r.ring_out[slot, :, there] = self.value(h, dz, sub, earlier, columns).astype(BF16)
            return carry

        lax.fori_loop(0, self.quarter // self.tile, turn, 0)
        self.start(
            remote("tp", partner, r.ring_out.at[slot], r.ring_in.at[slot], r.ring_send.at[slot], r.ring_recv.at[slot])
        )

    def run(self, out_ref):
        r, core, half = self.r, self.core, self.half

        def both(kind, d):
            for sub in (0, 1):
                self.message(kind, sub, d)

        self.product(-4)
        self.product(-3)
        self.sib_got(-4)
        both("y", 4)
        self.sib_got(-3)
        self.message("long", 0, 5)
        self.message("other", 0, 3)
        self.product(3)
        self.sib_got(3)
        self.message("long", 1, 5)
        self.message("other", 1, 3)
        both("y", 3)
        self.product(2)
        both("long", 4)
        self.product(-2)
        self.sib_got(2)
        self.message("short", 1, 2)
        self.message("y", 0, 2)
        self.sib_got(-2)
        self.message("short", 0, 2)
        self.message("y", 1, 2)
        both("other", 2)
        self.product(1)
        both("long", 3)
        self.product(-1)
        self.sib_got(1)
        self.sib_got(-1)
        both("y", 1)
        both("other", 1)
        self.product(0)
        both("long", 2)
        self.sib_got(0)
        both("y", 0)
        both("short", 1)
        both("long", 1)
        first = core == 0
        for sub in (0, 1):
            earlier = [self.slot(*key) for key in (("short", sub, 1), ("y", sub, 0), ("long", sub, 1))]
            for slot in earlier:
                self.got(slot)

            def final(j, carry, sub=sub, earlier=earlier):
                columns = j * self.tile
                value = self.value(0, 0, sub, earlier, columns)
                low, high = value[: self.rows], value[self.rows :]
                at = sub * self.quarter + columns
                here = pl.ds(pl.multiple_of(core * half + at, self.tile), self.tile)
                out_ref[:, here] = jnp.where(first, low, high).astype(BF16)
                there = pl.ds(pl.multiple_of(columns, self.tile), self.tile)
                r.last_out[sub, :, there] = jnp.where(first, high, low).astype(BF16)
                return carry

            lax.fori_loop(0, self.quarter // self.tile, final, 0)
            self.start(
                remote(
                    "tp", self.sibling, r.last_out.at[sub], r.last_in.at[sub], r.last_send.at[sub], r.last_recv.at[sub]
                )
            )
        for sub in (0, 1):
            there = r.last_in.at[sub]
            remote("tp", self.sibling, there, there, r.last_send.at[sub], r.last_recv.at[sub]).wait_recv()
            at = (1 - core) * half + sub * self.quarter
            out_ref[:, pl.ds(pl.multiple_of(at, self.quarter), self.quarter)] = r.last_in[sub]
        for copy in self.started:
            copy.wait_send()


class Turned:
    def __init__(self, r):
        self.r = r
        self.size = r.stage.shape[1]
        self.blocks = r.step_w.shape[1] // self.size
        self.todo = [functools.partial(self.out_block, j) for j in range(self.blocks)]
        self.copies = []
        for i, ref in enumerate((r.inner_w.at[0], r.inner_w.at[1], r.state_w)):
            self.todo += [functools.partial(self.block, i, ref, j) for j in range(self.blocks)]

    def span(self, j):
        return slice(j * self.size, (j + 1) * self.size)

    def out_load(self, j):
        r = self.r
        return pltpu.make_async_copy(r.out_hbm.at[:, self.span(j)], r.stage.at[j % 2], r.stage_sem.at[j % 2])

    def begin(self):
        for j in (0, 1):
            self.out_load(j).start()

    def out_block(self, j):
        self.out_load(j).wait()
        self.r.out_t[self.span(j), :] = self.r.stage[j % 2].T
        if j + 2 < self.blocks:
            self.out_load(j + 2).start()

    def block(self, i, ref, j):
        slot = len(self.copies) % 4
        if len(self.copies) >= 4:
            self.copies[-4].wait()
        self.r.stage[2 + slot] = ref[self.span(j), :].T
        copy = pltpu.make_async_copy(
            self.r.stage.at[2 + slot], self.r.turned_hbm.at[i, :, self.span(j)], self.r.stage_sem.at[2 + slot]
        )
        copy.start()
        self.copies.append(copy)

    def some(self, count):
        for _ in range(count):
            if self.todo:
                self.todo.pop(0)()

    def finish(self):
        self.some(len(self.todo))
        for copy in self.copies[-4:]:
            copy.wait()

    def back(self):
        width = self.r.inner_w.shape[2]
        loads = [
            pltpu.make_async_copy(
                self.r.turned_hbm.at[i], self.r.rows_all.at[i * width : (i + 1) * width, :], self.r.back_sem.at[i]
            )
            for i in range(3)
        ]
        for load in loads:
            load.start()
        return loads


class Exchange:
    def __init__(self, out, into, cross_out, cross_in, send_sem, recv_sem, factors_in, heads, forward):
        self.ctx = lax.axis_index("ctx")
        self.x, self.y = lax.rem(self.ctx, ROW), self.ctx // ROW
        self.out, self.into, self.heads, self.forward = out, into, heads, forward
        self.factors_in, self.cross_out, self.cross_in = factors_in, cross_out, cross_in
        self.gives = self.y == (0 if forward else 1)
        self.copies = [
            remote("ctx", self.peer(j), out, into.at[j - 1], send_sem.at[j - 1], recv_sem.at[j - 1])
            for j in range(1, ROW)
        ]
        self.cross = remote(
            "ctx", lax.rem(self.ctx + ROW, SHARDS), cross_out, cross_in, send_sem.at[ROW - 1], recv_sem.at[ROW - 1]
        )

    def peer(self, j):
        return self.y * ROW + lax.rem(self.x + j, ROW)

    def start(self):
        for copy in self.copies:
            copy.start()

    def step(self, value, slot):
        parts = []
        for h in range(self.heads):
            state = self.into[slot, h * HEAD_DIM : (h + 1) * HEAD_DIM, :].astype(F32)
            parts.append(value[h] * self.factors_in[slot, h : h + 1, :] + state)
        return parts

    def chain(self, total):
        for j in range(ROW - 1, 0, -1):
            there = self.x >= j if self.forward else self.x + j < ROW
            slot = j - 1 if self.forward else ROW - 1 - j

            @pl.when(there)
            def _(slot=slot):
                for h, part in enumerate(self.step([total[h] for h in range(self.heads)], slot)):
                    total[h] = part

    def give(self, total, own, factors):
        for copy in self.copies:
            copy.wait_recv()

        @pl.when(self.gives)
        def _():
            total[...] = jnp.zeros_like(total)
            self.chain(total)
            for h in range(self.heads):
                self.cross_sum[h] = total[h] * factors[h : h + 1, :] + own[h]
            for j in range(1, ROW):
                there = self.x + j < ROW if self.forward else self.x >= j
                slot = ROW - 1 - j if self.forward else j - 1

                @pl.when(there)
                def _(slot=slot):
                    for h, part in enumerate(self.step([self.cross_sum[h] for h in range(self.heads)], slot)):
                        self.cross_sum[h] = part

            for h in range(self.heads):
                self.cross_out[h * HEAD_DIM : (h + 1) * HEAD_DIM, :] = self.cross_sum[h]
            self.cross.start()

    def take(self, total):
        @pl.when(jnp.logical_not(self.gives))
        def _():
            self.cross.wait_recv()
            for h in range(self.heads):
                total[h] = self.cross_in[h * HEAD_DIM : (h + 1) * HEAD_DIM, :].astype(F32)
            self.chain(total)

    def drain(self):
        for copy in self.copies:
            copy.wait_send()

        @pl.when(self.gives)
        def _():
            self.cross.wait_send()


def mixer_forward(r, tick, while_sent, while_crossing):
    ctx = lax.axis_index("ctx")
    total, both = r.conv.shape
    width = both - 2 * STATE
    heads = width // HEAD_DIM
    chunks = total // CHUNK
    span = lambda k: slice(k * CHUNK, (k + 1) * CHUNK)
    r.ext[HALO:, :] = r.conv[...].astype(F32)
    halo = remote("ctx", lax.rem(ctx + 1, SHARDS), r.ext.at[total:, :], r.ext.at[:HALO, :], r.halo_sem.at[0], r.halo_sem.at[1])

    @pl.when(ctx < SHARDS - 1)
    def _():
        halo.start()

    lane = lax.broadcasted_iota(jnp.int32, (1, CHUNK), 1)
    rows_at = lax.broadcasted_iota(jnp.int32, (CHUNK, CHUNK), 0)
    cols_at = lax.broadcasted_iota(jnp.int32, (CHUNK, CHUNK), 1)
    causal = (rows_at >= cols_at).astype(F32)

    def per_lane(values):
        row = jnp.zeros_like(values[0])
        for h, value in enumerate(values):
            row = jnp.where(lane == h, value, row)
        return row

    bias = per_lane([jnp.full((1, CHUNK), r.step_bias[h], F32) for h in range(heads)])
    rate = per_lane([jnp.exp(jnp.full((1, CHUNK), r.decay_log[h], F32)) for h in range(heads)])
    valid = lane < heads
    kernel = [
        jnp.concatenate([r.conv_inner[k : k + 1, :], r.conv_state[k : k + 1, :]], axis=1) for k in range(CONV)
    ]
    ends = []
    for k in range(chunks):
        raw = jnp.where(valid, r.stepraw[span(k), :], 0.0) + bias
        step = jnp.maximum(raw, 0.0) + jnp.log1p(jnp.exp(-jnp.abs(raw)))
        step = jnp.where(valid, step, 0.0)
        r.steps[span(k), :] = step
        cum = dot(causal, -step * rate, NN, EXACT)
        r.cums[span(k), :] = cum
        turned = cum.T
        ends.append([cum[CHUNK - 1 :, h : h + 1] for h in range(heads)])
        for h in range(heads):
            spread = cum[:, h : h + 1] - turned[h : h + 1, :]
            r.decays[k, h] = jnp.exp(jnp.minimum(spread, 0.0)) * causal
    tick()

    @pl.when(ctx == 0)
    def _():
        r.ext[:HALO, :] = jnp.zeros((HALO, both), F32)

    @pl.when(ctx > 0)
    def _():
        halo.wait_recv()

    for k in range(chunks):
        blended = jnp.zeros((CHUNK, both), F32)
        for tap in range(CONV):
            start = k * CHUNK + HALO - (CONV - 1) + tap
            blended += kernel[tap] * r.ext[start : start + CHUNK, :]
        r.pre[span(k), :] = blended
        active = blended * jax.nn.sigmoid(blended)
        r.act[span(k), :] = active
        b_rows, c_rows = active[:, width : width + STATE], active[:, width + STATE :]
        r.cb[k] = dot(c_rows, b_rows, NT)
        for h in range(heads):
            lanes = slice(h * HEAD_DIM, (h + 1) * HEAD_DIM)
            fed = active[:, lanes] * r.steps[span(k), h : h + 1]
            r.xd[span(k), lanes] = fed
            left = jnp.exp(ends[k][h] - r.cums[span(k), h : h + 1])
            own = dot(fed * left, b_rows, TN)
            if k == 0:
                r.states[0, h] = jnp.zeros_like(own)
                r.states[1, h] = own
            else:
                r.states[k + 1, h] = jnp.exp(ends[k][h]) * r.states[k, h] + own
        if k % 3 == 2:
            tick()

    befores = [[jnp.zeros((1, 1), F32) for _ in range(heads)]]
    for k in range(chunks):
        befores.append([befores[k][h] + ends[k][h] for h in range(heads)])
    whole = [jnp.exp(befores[chunks][h]) for h in range(heads)]
    row8 = lax.broadcasted_iota(jnp.int32, (8, CHUNK), 0)
    factors = jnp.zeros((8, CHUNK), F32)
    for h in range(heads):
        r.fwd_out[h * HEAD_DIM : (h + 1) * HEAD_DIM, :] = r.states[chunks, h]
        factors = jnp.where(row8 == h, whole[h], factors)
    r.factors_out[...] = factors
    forward = Exchange(
        r.fwd_out, r.fwd_in, r.cross_out.at[0], r.cross_in.at[0], r.fwd_send, r.fwd_recv, r.factors_in, heads, True
    )
    forward.cross_sum = r.cross_sum
    factor_copies = [
        remote(
            "ctx", forward.peer(j), r.factors_out, r.factors_in.at[j - 1], r.factor_send.at[j - 1], r.factor_recv.at[j - 1]
        )
        for j in range(1, ROW)
    ]
    for copy in factor_copies:
        copy.start()
    forward.start()
    tick()

    for k in range(chunks):
        c_rows = r.act[span(k), width + STATE :]
        for h in range(heads):
            lanes = slice(h * HEAD_DIM, (h + 1) * HEAD_DIM)
            value = dot(r.decays[k, h] * r.cb[k], r.xd[span(k), lanes], NN)
            if k > 0:
                value += jnp.exp(r.cums[span(k), h : h + 1]) * dot(c_rows, r.states[k, h], NT)
            r.out[span(k), lanes] = value
        if k % 3 == 2:
            tick()

    while_sent()
    for copy in factor_copies:
        copy.wait_recv()
    forward.give(r.entering, r.states.at[chunks], factors)
    while_crossing()
    forward.take(r.entering)
    for k in range(chunks):
        c_rows = r.act[span(k), width + STATE :]
        for h in range(heads):
            lanes = slice(h * HEAD_DIM, (h + 1) * HEAD_DIM)
            grown = jnp.exp(r.cums[span(k), h : h + 1] + befores[k][h])
            r.out[span(k), lanes] = r.out[span(k), lanes] + grown * dot(c_rows, r.entering[h], NT)
            r.states[k, h] = r.states[k, h] + jnp.exp(befores[k][h]) * r.entering[h]
    for h in range(heads):
        r.states[chunks, h] = r.states[chunks, h] + whole[h] * r.entering[h]

    def drain():
        @pl.when(ctx < SHARDS - 1)
        def _():
            halo.wait_send()

        for copy in factor_copies:
            copy.wait_send()
        forward.drain()

    return SimpleNamespace(
        total=total, both=both, width=width, heads=heads, chunks=chunks, span=span, lane=lane, bias=bias, rate=rate,
        valid=valid, kernel=kernel, ends=ends, factors=factors, drain=drain, rows_at=rows_at, cols_at=cols_at,
    )


def token_sums(r, f):
    gain = r.gain[...]
    ones = jnp.ones((8, f.width), F32)
    for k in range(f.chunks):
        gate = r.gate[f.span(k), :].astype(F32)
        gated = r.out[f.span(k), :] * (gate * jax.nn.sigmoid(gate))
        squares = dot(ones, gated * gated, NT)
        crosses = dot(ones, gain * r.local[f.span(k), :] * gated, NT)
        r.tot_out[0, 0:1, f.span(k)] = squares[0:1, :]
        r.tot_out[0, 1:2, f.span(k)] = crosses[0:1, :]
    yh, z, core = place()
    copies = []

    def swap(phase, partners, base):
        mine = []
        for j, partner in enumerate(partners):
            slot = base + j
            copy = remote(
                "tp", partner, r.tot_out.at[phase], r.tot_in.at[slot], r.tot_send.at[slot], r.tot_recv.at[slot]
            )
            copy.start()
            mine.append(copy)
        sums = r.tot_out[phase]
        for j, copy in enumerate(mine):
            copy.wait_recv()
            sums = sums + r.tot_in[base + j]
        copies.extend(mine)
        return sums

    near = [tp_id(yh, z, 1 - core), tp_id(1 - yh, z, core), tp_id(1 - yh, z, 1 - core)]
    r.tot_out[1] = swap(0, near, 0)
    sums = swap(1, [tp_id(yh, z + j, core) for j in range(1, Z)], len(near))
    return sums, copies


def mixer_backward(r, f, sums):
    ctx = lax.axis_index("ctx")
    span, chunks, heads, width, total = f.span, f.chunks, f.heads, f.width, f.total
    channels = width * GROUP
    gain = r.gain[...]
    anti = (f.rows_at <= f.cols_at).astype(F32)
    ends = f.ends
    for k in range(chunks):
        held = jnp.concatenate([sums[:, span(k)], jnp.zeros((CHUNK - 2, CHUNK), F32)], axis=0).T
        inverse = lax.rsqrt(held[:, 0:1] / channels + EPSILON)
        pull = inverse * inverse * inverse * (held[:, 1:2] / channels)
        gate = r.gate[span(k), :].astype(F32)
        sigmoid = jax.nn.sigmoid(gate)
        opened = gate * sigmoid
        value = r.out[span(k), :]
        d_gated = inverse * (gain * r.local[span(k), :]) - value * opened * pull
        r.d_gate[span(k), :] = (d_gated * value * sigmoid * (1.0 + gate * (1.0 - sigmoid))).astype(BF16)
        r.dy[span(k), :] = d_gated * opened

    for k in range(chunks - 1, -1, -1):
        c_rows = r.act[span(k), width + STATE :]
        for h in range(heads):
            lanes = slice(h * HEAD_DIM, (h + 1) * HEAD_DIM)
            own = dot(r.dy[span(k), lanes] * jnp.exp(r.cums[span(k), h : h + 1]), c_rows, TN)
            if k < chunks - 1:
                own += jnp.exp(ends[k][h]) * r.d_states[k + 1, h]
            r.d_states[k, h] = own
    for h in range(heads):
        r.bwd_out[h * HEAD_DIM : (h + 1) * HEAD_DIM, :] = r.d_states[0, h]
    backward = Exchange(
        r.bwd_out, r.bwd_in, r.cross_out.at[1], r.cross_in.at[1], r.bwd_send, r.bwd_recv, r.factors_in, heads, False
    )
    backward.cross_sum = r.cross_sum
    backward.start()

    def local(k):
        b_rows, c_rows = r.act[span(k), width : width + STATE], r.act[span(k), width + STATE :]
        d_cb = jnp.zeros((CHUNK, CHUNK), F32)
        d_crows = jnp.zeros((CHUNK, STATE), F32)
        for h in range(heads):
            lanes = slice(h * HEAD_DIM, (h + 1) * HEAD_DIM)
            grad = r.dy[span(k), lanes]
            d_cb += r.decays[k, h] * dot(grad, r.xd[span(k), lanes], NT)
            r.u_loc[span(k), lanes] = dot(r.decays[k, h] * r.cb[k], grad, TN)
            d_crows += jnp.exp(r.cums[span(k), h : h + 1]) * dot(grad, r.states[k, h], NN)
        r.d_b[span(k), :] = dot(d_cb, c_rows, TN)
        r.d_c[span(k), :] = d_crows + dot(d_cb, b_rows, NN)

    for k in range(chunks // 2):
        local(k)
    backward.give(r.d_leaving, r.d_states.at[0], f.factors)
    for k in range(chunks // 2, chunks):
        local(k)
    backward.take(r.d_leaving)
    after = [jnp.zeros((1, 1), F32) for _ in range(heads)]
    for h in range(heads):
        r.d_states[chunks, h] = r.d_leaving[h]
    for k in range(chunks - 1, 0, -1):
        after = [after[h] + ends[k][h] for h in range(heads)]
        for h in range(heads):
            r.d_states[k, h] = r.d_states[k, h] + jnp.exp(after[h]) * r.d_leaving[h]

    halo = remote("ctx", lax.rem(ctx + SHARDS - 1, SHARDS), r.d_pre.at[:HALO, :], r.d_pre.at[total:, :], r.halo_sem.at[2], r.halo_sem.at[3])
    for k in range(chunks):
        b_rows = r.act[span(k), width : width + STATE]
        d_brows = r.d_b[span(k), :]
        d_acts = []
        pulls = jnp.zeros((CHUNK, CHUNK), F32)
        feeds = jnp.zeros((CHUNK, CHUNK), F32)
        edge = jnp.zeros((1, CHUNK), F32)
        for h in range(heads):
            lanes = slice(h * HEAD_DIM, (h + 1) * HEAD_DIM)
            step = r.steps[span(k), h : h + 1]
            left = jnp.exp(ends[k][h] - r.cums[span(k), h : h + 1])
            d_next = r.d_states[k + 1, h]
            grad = r.u_loc[span(k), lanes] + left * dot(b_rows, d_next, NT)
            d_brows += dot(r.xd[span(k), lanes] * left, d_next, NN)
            d_acts.append(grad * step)
            fed = jnp.sum(grad * r.act[span(k), lanes], axis=1, keepdims=True)
            met = jnp.sum(r.dy[span(k), lanes] * r.out[span(k), lanes], axis=1, keepdims=True)
            pulls = jnp.where(f.lane == h, met - step * fed, pulls)
            feeds = jnp.where(f.lane == h, fed, feeds)
            edge = jnp.where(f.lane == h, jnp.sum(d_next * r.states[k + 1, h]), edge)
        d_decay = dot(anti, pulls, NN, EXACT) + edge
        raw = jnp.where(f.valid, r.stepraw[span(k), :], 0.0) + f.bias
        d_raw = (feeds - f.rate * d_decay) * jax.nn.sigmoid(raw)
        r.d_step[span(k), :] = d_raw[:, :heads].astype(BF16)
        d_act = jnp.concatenate(d_acts + [d_brows, r.d_c[span(k), :]], axis=1)
        value = r.pre[span(k), :]
        sigmoid = jax.nn.sigmoid(value)
        r.d_pre[span(k), :] = d_act * sigmoid * (1.0 + value * (1.0 - sigmoid))
        if k == 0:

            @pl.when(ctx > 0)
            def _():
                halo.start()

    @pl.when(ctx == SHARDS - 1)
    def _():
        r.d_pre[total:, :] = jnp.zeros((HALO, f.both), F32)

    @pl.when(ctx < SHARDS - 1)
    def _():
        halo.wait_recv()

    for k in range(chunks):
        blended = jnp.zeros((CHUNK, f.both), F32)
        for tap in range(CONV):
            start = k * CHUNK + CONV - 1 - tap
            blended += f.kernel[tap] * r.d_pre[start : start + CHUNK, :]
        r.d_inner[span(k), :] = blended[:, :width].astype(BF16)
        r.d_state[span(k), :] = blended[:, width:].astype(BF16)

    def drain():
        @pl.when(ctx > 0)
        def _():
            halo.wait_send()

        backward.drain()

    return drain


def whole_kernel(names, *refs):
    r = SimpleNamespace(**dict(zip(names, refs, strict=True)))
    loads = [
        pltpu.make_async_copy(src, dst, r.weight_sem.at[i])
        for i, (src, dst) in enumerate(
            ((r.inner_hbm, r.inner_w), (r.state_hbm, r.state_w), (r.step_hbm, r.step_w))
        )
    ]
    for load in loads:
        load.start()
    turned = Turned(r)
    turned.begin()
    yh, z, core = place()
    ctx = lax.axis_index("ctx")
    barrier = pltpu.get_barrier_semaphore()
    tp_partners = [tp_id(yh, z, 1 - core), tp_id(1 - yh, z, core), tp_id(1 - yh, z, 1 - core)]
    tp_partners += [tp_id(yh, z + j, core) for j in range(1, Z)]
    row = ctx // ROW * ROW
    ctx_partners = [row + lax.rem(ctx - row + j, ROW) for j in range(1, ROW)]
    ctx_partners += [lax.rem(ctx + j, SHARDS) for j in (ROW, 1, SHARDS - 1)]
    for axis, partners in (("tp", tp_partners), ("ctx", ctx_partners)):
        for partner in partners:
            pl.semaphore_signal(barrier, inc=1, device_id={axis: partner}, device_id_type=MESH)
    pl.semaphore_wait(barrier, len(tp_partners) + len(ctx_partners))

    first = Gather(r.rows, r.rows_all, r.swaps.at[0], r.send_r, r.recv_r)
    second = Gather(r.grads, r.grads_all, r.swaps.at[1], r.send_g, r.recv_g)
    first.first_swap()
    second.first_swap()
    first.begin()
    early, late = first.steps()[:-1], first.steps()[-1:]
    turned.some(6)
    for load in loads:
        load.wait()
    for step in early:
        step()
        turned.some(4)
    second.begin()
    pending = second.steps()
    for step in late:
        step()
        pending.pop(0)()
    turned.finish()
    first.finish()

    def tick():
        if pending:
            pending.pop(0)()

    total, tile = r.rows_all.shape[0], 128

    def project(dst, column, weight, source, contract):
        def tiles(low, high):
            def turn(i, carry):
                at = pl.ds(pl.multiple_of(i * tile, tile), tile)
                value = dot16(source[at, :], weight[...], contract)
                if dst.dtype == F32 and source is r.rows_all:
                    value = value.astype(BF16)
                dst[at, pl.ds(column, value.shape[1])] = value.astype(dst.dtype)
                return carry

            lax.fori_loop(low, high, turn, 0)

        tiles(0, total // tile // 2)
        tick()
        tiles(total // tile // 2, total // tile)
        tick()

    width = r.inner_w.shape[2]
    project(r.conv, 0, r.inner_w.at[1], r.rows_all, NN)
    project(r.conv, width, r.state_w, r.rows_all, NN)
    project(r.stepraw, 0, r.step_w, r.rows_all, NT)

    def while_sent():
        project(r.gate, 0, r.inner_w.at[0], r.rows_all, NN)
        first.drain()
        weights.extend(turned.back())

    def while_crossing():
        while pending:
            tick()
        second.finish()
        project(r.local, 0, r.out_t, r.grads_all, NN)

    weights = []
    f = mixer_forward(r, tick, while_sent, while_crossing)
    sums, total_copies = token_sums(r, f)
    drain = mixer_backward(r, f, sums)
    for load in weights:
        load.wait()
    rows, depth = r.result.shape
    Scatter(r, rows, depth).run(r.result)
    f.drain()
    drain()
    for copy in total_copies:
        copy.wait_send()
    second.drain()


def body(
    normed_rows,
    out_grad,
    inner_weight,
    state_weight,
    step_weight,
    conv_inner,
    conv_state,
    step_bias,
    decay_log,
    norm_gain,
    out_weight,
):
    count, depth = normed_rows.shape
    total = count * GROUP
    width, state_width = inner_weight.shape[2], state_weight.shape[1]
    both = width + state_width
    heads = width // HEAD_DIM
    chunks = total // CHUNK
    pair, half = 2 * count, depth // 2
    quarter = half // 2
    vmem = pl.BlockSpec(memory_space=pltpu.VMEM)
    smem = pl.BlockSpec(memory_space=pltpu.SMEM)
    anywhere = pl.BlockSpec(memory_space=pl.ANY)
    inputs = {
        "step_bias": (step_bias, smem),
        "decay_log": (decay_log, smem),
        "rows": (normed_rows, vmem),
        "grads": (out_grad, vmem),
        "conv_inner": (conv_inner, vmem),
        "conv_state": (conv_state, vmem),
        "gain": (norm_gain.reshape(1, -1), vmem),
        "inner_hbm": (inner_weight, anywhere),
        "state_hbm": (state_weight, anywhere),
        "out_hbm": (out_weight, anywhere),
        "step_hbm": (step_weight.T, anywhere),
    }
    state = (heads, HEAD_DIM, STATE)
    message = (heads * HEAD_DIM, STATE)
    scratch = {
        "rows_all": ((total, depth), BF16),
        "grads_all": ((total, depth), BF16),
        "swaps": ((2, count, half), BF16),
        "inner_w": (inner_weight.shape, BF16),
        "state_w": (state_weight.shape, BF16),
        "out_t": (out_weight.shape[::-1], BF16),
        "stage": ((6, width, width), BF16),
        "step_w": (step_weight.shape[::-1], BF16),
        "gate": ((total, width), BF16),
        "conv": ((total, both), BF16),
        "stepraw": ((total, CHUNK), F32),
        "local": ((total, width), F32),
        "ext": ((HALO + total, both), F32),
        "pre": ((total, both), F32),
        "act": ((total, both), F32),
        "xd": ((total, width), F32),
        "steps": ((total, CHUNK), F32),
        "cums": ((total, CHUNK), F32),
        "cb": ((chunks, CHUNK, CHUNK), F32),
        "decays": ((chunks, heads, CHUNK, CHUNK), F32),
        "out": ((total, width), F32),
        "dy": ((total, width), F32),
        "states": ((chunks + 1,) + state, F32),
        "d_states": ((chunks + 1,) + state, F32),
        "entering": (state, F32),
        "d_leaving": (state, F32),
        "fwd_out": (message, F32),
        "fwd_in": ((ROW - 1,) + message, F32),
        "bwd_out": (message, F32),
        "bwd_in": ((ROW - 1,) + message, F32),
        "cross_out": ((2,) + message, F32),
        "cross_in": ((2,) + message, F32),
        "cross_sum": (state, F32),
        "factors_out": ((8, CHUNK), F32),
        "factors_in": ((ROW - 1, 8, CHUNK), F32),
        "tot_out": ((2, 2, total), F32),
        "tot_in": ((3 + Z - 1, 2, total), F32),
        "d_pre": ((total + HALO, both), F32),
        "d_b": ((total, STATE), F32),
        "d_c": ((total, STATE), F32),
        "u_loc": ((total, width), F32),
        "d_gate": ((total, width), BF16),
        "d_inner": ((total, width), BF16),
        "d_state": ((total, state_width), BF16),
        "d_step": ((total, heads), BF16),
        "mine": ((Z, 2, pair, half), F32),
        "sib_out": ((Z, 2, pair, half), BF16),
        "sib_in": ((Z, 2, pair, half), BF16),
        "ring_out": ((30, pair, quarter), BF16),
        "ring_in": ((30, pair, quarter), BF16),
        "last_out": ((2, count, quarter), BF16),
        "last_in": ((2, count, quarter), BF16),
    }
    semaphores = {
        "weight_sem": 3,
        "stage_sem": 6,
        "back_sem": 3,
        "send_r": 63,
        "recv_r": 63,
        "send_g": 63,
        "recv_g": 63,
        "halo_sem": 4,
        "factor_send": ROW - 1,
        "factor_recv": ROW - 1,
        "fwd_send": ROW,
        "fwd_recv": ROW,
        "bwd_send": ROW,
        "bwd_recv": ROW,
        "tot_send": 3 + Z - 1,
        "tot_recv": 3 + Z - 1,
        "sib_send": Z,
        "sib_recv": Z,
        "ring_send": 30,
        "ring_recv": 30,
        "last_send": 2,
        "last_recv": 2,
    }
    names = list(inputs) + ["result", "turned_hbm"] + list(scratch) + list(semaphores)
    return pl.pallas_call(
        functools.partial(whole_kernel, names),
        out_shape=(
            jax.ShapeDtypeStruct((count, depth), BF16),
            jax.ShapeDtypeStruct((3, width, depth), BF16),
        ),
        in_specs=[spec for _, spec in inputs.values()],
        out_specs=(vmem, anywhere),
        scratch_shapes=[pltpu.VMEM(shape, dtype) for shape, dtype in scratch.values()]
        + [pltpu.SemaphoreType.DMA((n,)) for n in semaphores.values()],
        compiler_params=pltpu.CompilerParams(collective_id=0, has_side_effects=True, vmem_limit_bytes=VMEM_LIMIT),
        name="mixer_grad",
    )(*[value for value, _ in inputs.values()])[0]


def solution(mesh):
    placed = (
        P(("ctx", "tp"), None),
        P(("ctx", "tp"), None),
        P(None, None, "tp"),
        P(),
        P(None, "tp"),
        P(None, "tp"),
        P(),
        P("tp"),
        P("tp"),
        P("tp"),
        P("tp", None),
    )
    return jax.shard_map(
        body, mesh=mesh, in_specs=placed, out_specs=P(("ctx", "tp"), None), check_vma=False
    )
```
